256 devices in a mesh: seq: 16 (over x, z_hi), mp: 16 (over y, z_lo, core).
Axes of the slice: x: 4, y: 4, z: 8 (z_hi: 4, z_lo: 2; z = z_hi * 2 + z_lo), core: 2. Of those that a mesh axis runs over, the one named last changes fastest.
Arguments:
- hidden: bfloat16 [4096, 4096], P('seq', 'mp'), may hold values from -6 to 6
- cotangent: bfloat16 [4096, 4096], P('seq', 'mp'), may hold values from -6 to 6
- neighbour_ids: int32 [64, 2, 128], P('seq'), may hold values from 0 to 63999
- neighbour_lengths: int32 [64, 2], replicated, may hold values from 1 to 128
- embed_table: bfloat16 [64000, 896], P('mp'), may hold values from -6 to 6
- enc_up: bfloat16 [3584, 896], P('mp'), may hold values from -0.1875 to 0.1875
- enc_down: bfloat16 [3584, 896], P('mp'), may hold values from -0.09375 to 0.09375
- w_query: bfloat16 [4096, 32, 128], P('seq', 'mp'), may hold values from -0.125 to 0.125
- w_keyval: bfloat16 [896, 32, 2, 128], P('seq', 'mp'), may hold values from -0.1875 to 0.1875
- w_out: bfloat16 [4096, 32, 128], P('seq', 'mp'), may hold values from -0.75 to 0.75
Outputs:
- cca_out: bfloat16 [4096, 4096], P('seq', 'mp')
- hidden_grad: bfloat16 [4096, 4096], P('seq', 'mp')
The draws below stay inside these ranges and needn't reach their ends.
All inputs are finite; a program needn't handle non-finite values.
Results may differ from the reference program's by a relative error of at most 0.012.
Values may be sent and summed in bfloat16 or wider, within the bound.
A program may use at most 128 MiB of HBM per device.

```python
import math
import jax
import jax.numpy as jnp
import numpy as np
from jax import lax

D = 4096
HEADS = 32
HD = 128
ENC = 896
ENC_FF = 3584
VOCAB = 64000
SPAN = 64
NEIGH = 2
NLEN = 128
SPANS = 64
SEQ_LEN = 4096


def place_ends(drawn, rng, least, top_value):
    spot = [jax.random.randint(jax.random.fold_in(rng, axis), (), 0, length) for axis, length in enumerate(drawn.shape)]
    widest = drawn.shape.index(max(drawn.shape))
    next_to = spot[:widest] + [(spot[widest] + 1) % drawn.shape[widest]] + spot[widest + 1:]
    return drawn.at[tuple(spot)].set(least).at[tuple(next_to)].set(top_value)


def spiked(entries, own_key, source, target, blocks, factor):
    owner, partner = [(jnp.arange(entries.shape[dim]) // (entries.shape[dim] // blocks)).reshape([-1 if axis == dim else 1 for axis in range(entries.ndim)]) for dim in (source, target)]
    chosen = jax.random.permutation(own_key, blocks)[partner]
    strong = (owner == chosen) | (owner == (partner + blocks // 2) % blocks)
    return jnp.where(strong, factor * entries, entries)


def block_scale(stream_key, extent, pieces, smallest, top_value):
    def one(position, shards_of):
        heights = jax.random.uniform(jax.random.fold_in(jax.random.fold_in(stream_key, 6), position), (shards_of,), jnp.float32, smallest / len(pieces), top_value / len(pieces))
        return jnp.repeat(jnp.exp(heights), extent[position] // shards_of).reshape((-1,) + (1,) * (len(extent) - position - 1))

    gain = one(*pieces[0])
    for cut in pieces[1:]:
        gain = gain * one(*cut)
    return gain


def cumulative_ranks(number_of, skew):
    portions = [(1 << 20) // math.isqrt(rank ** skew) + 1 for rank in range(1, number_of + 1)]
    deviation = 1 + sum(portions) // (1 << 30)
    return np.cumsum(np.array([max(1, weight // deviation) for weight in portions]))


def skewed_ids(own_key, shape, count, lean):
    table = cumulative_ranks(count, lean)
    pick = jax.random.randint(jax.random.fold_in(own_key, 1), shape, 0, int(table[count - 1]))
    grade = jnp.searchsorted(jnp.asarray(table, jnp.int32), pick, side="right")
    return jax.random.permutation(jax.random.fold_in(own_key, 2), count)[grade].astype(jnp.int32)


def normal_values(own_key, dims, spread, reach, pieces=(), kind=jnp.bfloat16):
    level = block_scale(own_key, dims, pieces, -0.22, 0.18) if pieces else 1.0
    result = jax.random.normal(own_key, dims, jnp.float32) * spread * level
    return jnp.minimum(jnp.maximum(result, -reach), reach).astype(kind)


def bell_draw_with(key, dims, scale, bound, shards, heavy, kind=jnp.bfloat16):
    entries = scale * jax.random.normal(key, dims, jnp.float32)
    if shards:
        entries = entries * block_scale(key, dims, shards, -0.22, 0.18)
    return jnp.clip(spiked(entries, jax.random.fold_in(key, 3), *heavy), -bound, bound).astype(kind)


def setup_inputs(seed: int = 0) -> dict:
    splits = jax.random.split(jax.random.key(seed), 11)
    return {
        "hidden": normal_values(splits[0], (SEQ_LEN, D), 1.0, 6.0, ((0, 16), (1, 16))),
        "cotangent": normal_values(splits[1], (SEQ_LEN, D), 1.0, 6.0, ((0, 16), (1, 16))),
        "neighbour_ids": place_ends(skewed_ids(splits[2], (SPANS, NEIGH, NLEN), VOCAB, 2), jax.random.fold_in(splits[2], 3), 0, VOCAB - 1).astype(jnp.int32),
        "neighbour_lengths": place_ends(jax.random.randint(splits[3], (SPANS, NEIGH), 1, NLEN + 1), jax.random.fold_in(splits[3], 1), 1, NLEN).astype(jnp.int32),
        "embed_table": normal_values(splits[4], (VOCAB, ENC), 1.0, 6.0, ((0, 16),)),
        "enc_up": normal_values(splits[5], (ENC_FF, ENC), ENC ** -0.5, 0.1875, ((0, 16),)),
        "enc_down": normal_values(splits[6], (ENC_FF, ENC), ENC_FF ** -0.5, 0.09375, ((0, 16),)),
        "w_query": bell_draw_with(splits[7], (D, HEADS, HD), D ** -0.5, 0.125, ((0, 16), (1, 16)), (1, 0, 16, 2.0)),
        "w_keyval": normal_values(splits[8], (ENC, HEADS, 2, HD), ENC ** -0.5, 0.1875, ((0, 16), (1, 16))),
        "w_out": bell_draw_with(splits[9], (D, HEADS, HD), HD ** -0.5, 0.75, ((0, 16), (1, 16)), (1, 0, 16, 2.0)),
    }


def rms_rows(values):
    return values * lax.rsqrt(lax.optimization_barrier(jnp.mean(values * values, axis=-1, keepdims=True)) + 1e-06)

def shift_rows(flat):
    width = flat.shape[1]
    front = jnp.zeros((1, width), flat.dtype)
    back = jnp.zeros((SPAN - 1, width), flat.dtype)
    return jnp.concatenate([front, flat, back], axis=0)

def reference(hidden, cotangent, neighbour_ids, neighbour_lengths, embed_table, enc_up, enc_down, w_query, w_keyval, w_out):
    groups = SPANS + 1
    keys_per = NEIGH * NLEN
    inner = HEADS * HD
    scale = HD ** (-0.5)
    emb = jnp.take(embed_table, neighbour_ids.reshape(SPANS * keys_per), axis=0)
    emb_wide = emb.astype(jnp.float32)
    normed = rms_rows(emb_wide).astype(jnp.bfloat16)
    act = jax.nn.gelu(jnp.dot(normed, enc_up.T, preferred_element_type=jnp.float32)).astype(jnp.bfloat16)
    ffn = jnp.dot(act, enc_down, preferred_element_type=jnp.float32)
    encoded = rms_rows(emb_wide + ffn).astype(jnp.bfloat16)
    keyval = jnp.dot(encoded, w_keyval.reshape(ENC, 2 * inner), preferred_element_type=jnp.float32).astype(jnp.bfloat16)
    keyval = keyval.reshape(SPANS, keys_per, HEADS, 2, HD)
    empty = jnp.zeros((1, keys_per, HEADS, 2, HD), jnp.bfloat16)
    keyval = jnp.concatenate([empty, keyval], axis=0)
    keys = keyval[:, :, :, 0].astype(jnp.float32)
    values = keyval[:, :, :, 1].astype(jnp.float32)
    lens = jnp.concatenate([jnp.ones((1, NEIGH), jnp.int32), neighbour_lengths], axis=0)
    key_mask = (jnp.arange(NLEN, dtype=jnp.int32)[None, None, :] < lens[:, :, None]).reshape(groups, keys_per)
    valid = (jnp.arange(groups) > 0).astype(jnp.float32)
    wq_flat = w_query.reshape(D, inner)
    wo_flat = w_out.reshape(D, inner)
    query = jnp.dot(hidden, wq_flat, preferred_element_type=jnp.float32).astype(jnp.bfloat16)
    query_g = shift_rows(query).reshape(groups, SPAN, HEADS, HD).astype(jnp.float32)
    scores = jnp.einsum('gqhd,gkhd->ghqk', query_g, keys) * scale
    expo = jnp.where(key_mask[:, None, None, :], jnp.exp(scores), 0.0)
    prob = expo / lax.optimization_barrier(jnp.sum(expo, axis=-1, keepdims=True)) * valid[:, None, None, None]
    prob_low = prob.astype(jnp.bfloat16).astype(jnp.float32)
    attn = jnp.einsum('ghqk,gkhd->gqhd', prob_low, values).astype(jnp.bfloat16)
    attn_flat = attn.reshape(groups * SPAN, inner)[1:SEQ_LEN + 1]
    cca_out = jnp.dot(attn_flat, wo_flat.T, preferred_element_type=jnp.float32).astype(jnp.bfloat16)
    d_attn = jnp.dot(cotangent, wo_flat, preferred_element_type=jnp.float32).astype(jnp.bfloat16)
    d_group = shift_rows(d_attn).reshape(groups, SPAN, HEADS, HD).astype(jnp.float32)
    d_prob = jnp.einsum('gqhd,gkhd->ghqk', d_group, values)
    delta = lax.optimization_barrier(jnp.sum(prob * d_prob, axis=-1, keepdims=True))
    d_score = (prob * (d_prob - delta) * scale).astype(jnp.bfloat16).astype(jnp.float32)
    d_query = jnp.einsum('ghqk,gkhd->gqhd', d_score, keys).astype(jnp.bfloat16)
    d_flat = d_query.reshape(groups * SPAN, inner)[1:SEQ_LEN + 1]
    hidden_grad = jnp.dot(d_flat, wq_flat.T, preferred_element_type=jnp.float32).astype(jnp.bfloat16)
    return (cca_out, hidden_grad)
```

```python
import functools

import jax
import jax.numpy as jnp
from jax import lax
from jax.experimental import pallas as pl
from jax.experimental.pallas import tpu as pltpu
from jax.sharding import PartitionSpec as P

MESH = pl.DeviceIdType.MESH
F32 = jnp.float32
BF16 = jnp.bfloat16


class Place:
    def __init__(self):
        s = lax.axis_index("seq")
        m = lax.axis_index("mp")
        self.s, self.m = s, m
        self.x, self.zh = s // 4, s % 4
        self.y, self.zl, self.c = m // 4, (m // 2) % 2, m % 2
        self.sib = (s, self.mp(0, self.zl, 1 - self.c))
        self.zn = (s, self.mp(0, 1 - self.zl, self.c))
        self.yp = (s, self.mp(1, self.zl, self.c))
        self.ym = (s, self.mp(3, self.zl, self.c))
        self.zp = (self.seq(0, 1), m)
        self.zm = (self.seq(0, 3), m)
        self.xp = (self.seq(1, 0), m)
        self.xm = (self.seq(3, 0), m)
        self.nxt = ((s + 1) % 16, m)
        self.prv = ((s + 15) % 16, m)

    def mp(self, dy, zl, c):
        return (((self.y + dy) % 4) * 2 + zl) * 2 + c

    def pair(self, dy, zl):
        return ((self.y + dy) % 4) * 2 + zl

    def seq(self, dx, dz):
        return ((self.x + dx) % 4) * 4 + (self.zh + dz) % 4


class Wire:
    def __init__(self, send_sem, recv_sem):
        self.send_sem, self.recv_sem = send_sem, recv_sem
        self.count = 0
        self.open = []

    def send(self, src, dst, to):
        k = self.count
        self.count += 1
        copy = pltpu.make_async_remote_copy(
            src_ref=src,
            dst_ref=dst,
            send_sem=self.send_sem.at[k],
            recv_sem=self.recv_sem.at[k],
            device_id=to,
            device_id_type=MESH,
        )
        copy.start()
        self.open.append(copy)
        return k

    def wait(self, k, landing, frm):
        pltpu.make_async_remote_copy(
            src_ref=landing,
            dst_ref=landing,
            send_sem=self.send_sem.at[k],
            recv_sem=self.recv_sem.at[k],
            device_id=frm,
            device_id_type=MESH,
        ).wait_recv()

    def finish(self):
        for copy in self.open:
            copy.wait_send()


def greet(peers):
    barrier = pltpu.get_barrier_semaphore()
    for peer in peers:
        pl.semaphore_signal(barrier, inc=1, device_id=peer, device_id_type=MESH)
    pl.semaphore_wait(barrier, len(peers))


def gather_mp(w, p, shard, out):
    mine = p.mp(0, p.zl, p.c)
    o = 1 - p.zl
    oc = 1 - p.c
    at = lambda dy, zl, c: out.at[p.mp(dy, zl, c)]
    own = out.at[mine]
    k_y1 = w.send(shard, own, p.yp)
    k_y2 = w.send(shard, own, p.ym)
    k_z = w.send(shard, own, p.zn)
    k_s = w.send(shard, own, p.sib)
    out[mine] = shard[...]
    yield
    w.wait(k_z, at(0, o, p.c), p.zn)
    zb = at(0, o, p.c)
    k_z1 = w.send(zb, zb, p.yp)
    k_z2 = w.send(zb, zb, p.ym)
    k_zs = w.send(zb, zb, p.sib)
    yield
    b = at(3, p.zl, p.c)
    w.wait(k_y1, b, p.ym)
    k_f1 = w.send(b, b, p.yp)
    k_s1 = w.send(b, b, p.sib)
    b = at(1, p.zl, p.c)
    w.wait(k_y2, b, p.yp)
    k_s2 = w.send(b, b, p.sib)
    yield
    b = at(1, o, p.c)
    w.wait(k_z2, b, p.yp)
    k_f2 = w.send(b, b, p.ym)
    k_s3 = w.send(b, b, p.sib)
    b = at(3, o, p.c)
    w.wait(k_z1, b, p.ym)
    k_s4 = w.send(b, b, p.sib)
    yield
    b = at(2, p.zl, p.c)
    w.wait(k_f1, b, p.ym)
    k_s5 = w.send(b, b, p.sib)
    b = at(2, o, p.c)
    w.wait(k_f2, b, p.yp)
    k_s6 = w.send(b, b, p.sib)
    yield
    w.wait(k_s, at(0, p.zl, oc), p.sib)
    w.wait(k_zs, at(0, o, oc), p.sib)
    w.wait(k_s1, at(3, p.zl, oc), p.sib)
    w.wait(k_s2, at(1, p.zl, oc), p.sib)
    w.wait(k_s3, at(1, o, oc), p.sib)
    w.wait(k_s4, at(3, o, oc), p.sib)
    w.wait(k_s5, at(2, p.zl, oc), p.sib)
    w.wait(k_s6, at(2, o, oc), p.sib)


def gather_seq(w, p, shard, out, up):
    mine = p.seq(0, 0)
    at = lambda dx, dz: out.at[p.seq(dx, dz)]
    own = out.at[mine]
    k_zp = w.send(shard, own, p.zp)
    k_zm = w.send(shard, own, p.zm)
    kx = {}
    kx[0] = (w.send(shard, own, p.xp), w.send(shard, own, p.xm))
    out[mine] = shard[...]

    def spread(dz):
        b = at(0, dz)
        kx[dz] = (w.send(b, b, p.xp), w.send(b, b, p.xm))

    kf = {}

    def relay(dz, upward):
        k1, k2 = kx[dz]
        if upward:
            b = at(3, dz)
            w.wait(k1, b, p.xm)
            kf[dz] = (w.send(b, b, p.xp), upward)
            w.wait(k2, at(1, dz), p.xp)
        else:
            b = at(1, dz)
            w.wait(k2, b, p.xp)
            kf[dz] = (w.send(b, b, p.xm), upward)
            w.wait(k1, at(3, dz), p.xm)

    yield
    if up:
        b = at(0, 3)
        w.wait(k_zp, b, p.zm)
        k_zf = w.send(b, b, p.zp)
        spread(3)
        w.wait(k_zm, at(0, 1), p.zp)
        spread(1)
    else:
        b = at(0, 1)
        w.wait(k_zm, b, p.zp)
        k_zf = w.send(b, b, p.zm)
        spread(1)
        w.wait(k_zp, at(0, 3), p.zm)
        spread(3)
    yield
    relay(0, up)
    yield
    w.wait(k_zf, at(0, 2), p.zm if up else p.zp)
    spread(2)
    yield
    relay(3 if up else 1, up)
    yield
    relay(1 if up else 3, not up)
    yield
    relay(2, not up)
    yield
    for dz, (k, upward) in kf.items():
        w.wait(k, at(2, dz), p.xm if upward else p.xp)


def scatter_mp(w, p, part, sibl, acc, land, result):
    o = 1 - p.zl
    ks = {}
    for dy in (2, 1, 3, 0):
        row = ((p.y + dy) % 4) * 2
        ks[dy] = w.send(
            part.at[pl.ds(row, 2), 1 - p.c], sibl.at[pl.ds(row, 2)], p.sib
        )
    yield

    def combine(dy):
        row = ((p.y + dy) % 4) * 2
        w.wait(ks[dy], sibl.at[pl.ds(row, 2)], p.sib)
        for zl in (0, 1):
            acc[row + zl] = (
                part[row + zl, p.c].astype(F32) + sibl[row + zl].astype(F32)
            ).astype(BF16)

    combine(2)
    k0 = w.send(acc.at[p.pair(2, p.zl)], land.at[0], p.yp)
    k1 = w.send(acc.at[p.pair(2, o)], land.at[1], p.ym)
    combine(1)
    k2b = w.send(acc.at[p.pair(1, o)], land.at[2], p.yp)
    combine(3)
    k3a = w.send(acc.at[p.pair(3, p.zl)], land.at[3], p.ym)
    combine(0)
    yield
    w.wait(k0, land.at[0], p.ym)
    i = p.pair(1, p.zl)
    acc[i] = (acc[i].astype(F32) + land[0].astype(F32)).astype(BF16)
    k2a = w.send(acc.at[i], land.at[4], p.yp)
    w.wait(k1, land.at[1], p.yp)
    i = p.pair(3, o)
    acc[i] = (acc[i].astype(F32) + land[1].astype(F32)).astype(BF16)
    k3b = w.send(acc.at[i], land.at[5], p.ym)
    yield
    w.wait(k2b, land.at[2], p.ym)
    w.wait(k3b, land.at[5], p.yp)
    i = p.pair(0, o)
    acc[i] = (acc[i].astype(F32) + land[2].astype(F32) + land[5].astype(F32)).astype(BF16)
    kz = w.send(acc.at[i], land.at[6], p.zn)
    yield
    w.wait(k3a, land.at[3], p.yp)
    w.wait(k2a, land.at[4], p.ym)
    w.wait(kz, land.at[6], p.zn)
    result(
        acc[p.pair(0, p.zl)].astype(F32)
        + land[3].astype(F32)
        + land[4].astype(F32)
        + land[6].astype(F32)
    )


def drain(gens):
    gens = list(gens)
    while gens:
        gens = [g for g in gens if next(g, True) is None]


def k1_body(
    hid, cot, wq, wo, wkv, part,
    q_o, d_o, wq_o, wo_o, wkv_o, emb_o,
    hid_s, cot_s, sibl, acc, land, emb_own, q_land, send_sem, recv_sem,
):
    p = Place()
    w = Wire(send_sem, recv_sem)
    greet((p.sib, p.zn, p.yp, p.ym, p.zp, p.zm, p.xp, p.xm, p.nxt, p.prv))

    def keep(total):
        emb_own[...] = total.astype(BF16)

    ers = scatter_mp(w, p, part, sibl, acc, land, keep)
    gq = gather_seq(w, p, wq, wq_o, True)
    go = gather_seq(w, p, wo, wo_o, False)
    gk = gather_seq(w, p, wkv, wkv_o, True)
    gh = gather_mp(w, p, hid, hid_s)
    gc = gather_mp(w, p, cot, cot_s)
    next(ers)
    next(gq), next(go), next(gk)
    next(ers)
    next(gh), next(gc)
    next(ers)
    next(gq), next(go), next(gk)
    next(ers)
    next(gh), next(gc)
    next(ers, None)
    ea = gather_mp(w, p, emb_own, emb_o)
    next(ea)
    drain([ea, gh, gc, gq, go, gk])

    def project(src, weights, dst):
        def step(b, total):
            return total + jnp.dot(src[b], weights[b], preferred_element_type=F32)

        total = lax.fori_loop(0, 16, step, jnp.zeros((256, 256), F32))
        dst[...] = total.astype(BF16)

    project(hid_s, wq_o, q_o)
    kq = w.send(q_o.at[pl.ds(192, 64)], q_land.at[0], p.prv)
    project(cot_s, wo_o, d_o)
    kd = w.send(d_o.at[pl.ds(192, 64)], q_land.at[1], p.prv)
    w.wait(kq, q_land.at[0], p.nxt)
    w.wait(kd, q_land.at[1], p.nxt)
    w.finish()
    first = lax.broadcasted_iota(jnp.int32, (64, 256), 0) == 0
    for dst, i in ((q_o, 0), (d_o, 1)):
        tail = dst[pl.ds(192, 64), :].astype(F32)
        dst[pl.ds(192, 64), :] = jnp.where(first, tail, q_land[i].astype(F32)).astype(BF16)


def k2_body(part, emb_mine, enc_o, sibl, acc, land, enc_own, send_sem, recv_sem):
    p = Place()
    w = Wire(send_sem, recv_sem)
    greet((p.sib, p.zn, p.yp, p.ym))

    def keep(total):
        v = emb_mine[...].astype(F32) + total
        v = v * lax.rsqrt(jnp.mean(v * v, axis=-1, keepdims=True) + 1e-06)
        enc_own[...] = v.astype(BF16)

    drain([scatter_mp(w, p, part, sibl, acc, land, keep)])
    drain([gather_mp(w, p, enc_own, enc_o)])
    w.finish()


def k3_body(
    attn, dq, wo, wq, out_o, grad_o,
    a_s, a_land, part_o, part_g, sibl_o, sibl_g, acc_o, acc_g, land_o, land_g,
    send_sem, recv_sem,
):
    p = Place()
    w = Wire(send_sem, recv_sem)
    greet((p.sib, p.zn, p.yp, p.ym, p.nxt, p.prv))
    ka = w.send(attn.at[pl.ds(192, 64)], a_land.at[0], p.nxt)
    kd = w.send(dq.at[pl.ds(192, 64)], a_land.at[1], p.nxt)
    first = lax.broadcasted_iota(jnp.int32, (64, 256), 0) == 0
    has_prev = p.s > 0
    for i, (src, k) in enumerate(((attn, ka), (dq, kd))):
        a_s[i, pl.ds(0, 192), :] = src[pl.ds(0, 192), :]
        w.wait(k, a_land.at[i], p.prv)
        got = jnp.where(has_prev, a_land[i].astype(F32), 0.0)
        tail = src[pl.ds(192, 64), :].astype(F32)
        a_s[i, pl.ds(192, 64), :] = jnp.where(first, tail, got).astype(BF16)

    def fill(i, weights, part):
        @pl.loop(0, 8)
        def _(b):
            for c in (0, 1):
                part[b, c] = lax.dot_general(
                    a_s[i], weights[b * 2 + c], (((1,), (1,)), ((), ())),
                    preferred_element_type=F32,
                ).astype(BF16)

    def keep_out(total):
        out_o[...] = total.astype(BF16)

    def keep_grad(total):
        grad_o[...] = total.astype(BF16)

    fill(0, wo, part_o)
    ro = scatter_mp(w, p, part_o, sibl_o, acc_o, land_o, keep_out)
    next(ro)
    fill(1, wq, part_g)
    rg = scatter_mp(w, p, part_g, sibl_g, acc_g, land_g, keep_grad)
    next(rg)
    drain([ro, rg])
    w.finish()


def vmem(n):
    return [pl.BlockSpec(memory_space=pltpu.VMEM)] * n


def call(body, outs, n_in, scratch, messages, cid, name):
    return pl.pallas_call(
        body,
        out_shape=[jax.ShapeDtypeStruct(s, BF16) for s in outs],
        in_specs=vmem(n_in),
        out_specs=vmem(len(outs)),
        scratch_shapes=[pltpu.VMEM(s, BF16) for s in scratch]
        + [pltpu.SemaphoreType.DMA((messages,)), pltpu.SemaphoreType.DMA((messages,))],
        compiler_params=pltpu.CompilerParams(
            collective_id=cid, has_side_effects=True, vmem_limit_bytes=56 * 1024 * 1024
        ),
        name=name,
    )


def rms_rows(values):
    return values * lax.rsqrt(jnp.mean(values * values, axis=-1, keepdims=True) + 1e-06)


def per_device(
    hidden, cotangent, neighbour_ids, neighbour_lengths, embed_table,
    enc_up, enc_down, w_query, w_keyval, w_out,
):
    scale = 128 ** (-0.5)
    vocab_here = embed_table.shape[0]
    local_ids = neighbour_ids.reshape(1024) - lax.axis_index("mp") * vocab_here
    inside = jnp.logical_and(local_ids >= 0, local_ids < vocab_here)
    picked = jnp.take(embed_table, jnp.clip(local_ids, 0, vocab_here - 1), axis=0)
    masked = jnp.where(inside[:, None], picked, jnp.zeros((), picked.dtype))

    hid_r = jnp.roll(hidden, -63, axis=0)
    cot_r = jnp.roll(cotangent, -63, axis=0)
    enc_blk = (64, 896)
    out_blk = (256, 256)
    q, d, wq, wo, wkv, emb = call(
        k1_body,
        [out_blk, out_blk, (16,) + out_blk, (16,) + out_blk, (16, 56, 512), (16,) + enc_blk],
        6,
        [(16,) + out_blk, (16,) + out_blk, (8,) + enc_blk, (8,) + enc_blk, (7,) + enc_blk,
         enc_blk, (2, 64, 256)],
        110, 1, "gathers",
    )(
        hid_r, cot_r, w_query.reshape(256, 256), w_out.reshape(256, 256),
        w_keyval.reshape(56, 512), masked.reshape((8, 2) + enc_blk),
    )
    emb_flat = emb.reshape(1024, 896)
    emb_wide = emb_flat.astype(F32)
    normed = rms_rows(emb_wide).astype(BF16)
    act = jax.nn.gelu(
        lax.dot_general(normed, enc_up, (((1,), (1,)), ((), ())), preferred_element_type=F32)
    ).astype(BF16)
    ffn = jnp.dot(act, enc_down, preferred_element_type=F32).astype(BF16)
    emb_mine = lax.dynamic_index_in_dim(emb, lax.axis_index("mp"), 0, keepdims=False)
    (enc,) = call(
        k2_body,
        [(16,) + enc_blk],
        2,
        [(8,) + enc_blk, (8,) + enc_blk, (7,) + enc_blk, enc_blk],
        30, 2, "ffn_sums",
    )(ffn.reshape((8, 2) + enc_blk), emb_mine)

    keyval = jnp.dot(
        enc.reshape(1024, 896), wkv.reshape(896, 512), preferred_element_type=F32
    ).astype(BF16).reshape(4, 256, 2, 2, 128)
    keys, values = keyval[:, :, :, 0], keyval[:, :, :, 1]
    lens = lax.dynamic_slice_in_dim(neighbour_lengths, lax.axis_index("seq") * 4, 4, 0)
    key_mask = (
        jnp.arange(128, dtype=jnp.int32)[None, None, :] < lens[:, :, None]
    ).reshape(4, 256)
    qg = q.reshape(4, 64, 2, 128)
    dg = d.reshape(4, 64, 2, 128)
    scores = jnp.einsum("gqhd,gkhd->ghqk", qg, keys, preferred_element_type=F32) * scale
    expo = jnp.where(key_mask[:, None, None, :], jnp.exp(scores), 0.0)
    prob = expo / jnp.sum(expo, axis=-1, keepdims=True)
    attn = jnp.einsum(
        "ghqk,gkhd->gqhd", prob.astype(BF16), values, preferred_element_type=F32
    ).astype(BF16)
    d_prob = jnp.einsum("gqhd,gkhd->ghqk", dg, values, preferred_element_type=F32)
    delta = jnp.sum(prob * d_prob, axis=-1, keepdims=True)
    d_score = (prob * (d_prob - delta) * scale).astype(BF16)
    dq = jnp.einsum("ghqk,gkhd->gqhd", d_score, keys, preferred_element_type=F32).astype(BF16)

    big = (8, 2) + out_blk
    out, grad = call(
        k3_body,
        [out_blk, out_blk],
        4,
        [(2,) + out_blk, (2, 64, 256), big, big, (8,) + out_blk, (8,) + out_blk,
         (8,) + out_blk, (8,) + out_blk, (7,) + out_blk, (7,) + out_blk],
        30, 3, "out_sums",
    )(attn.reshape(256, 256), dq.reshape(256, 256), wo, wq)
    return jnp.roll(out, 63, axis=0), jnp.roll(grad, 63, axis=0)


def solution(mesh):
    return jax.shard_map(
        per_device,
        mesh=mesh,
        in_specs=(
            P("seq", "mp"),
            P("seq", "mp"),
            P("seq", None, None),
            P(),
            P("mp", None),
            P("mp", None),
            P("mp", None),
            P("seq", "mp", None),
            P("seq", "mp", None, None),
            P("seq", "mp", None),
        ),
        out_specs=(P("seq", "mp"), P("seq", "mp")),
        check_vma=False,
    )
```

```python
import functools

import jax
import jax.numpy as jnp
from jax import lax
from jax.experimental import pallas as pl
from jax.experimental.pallas import tpu as pltpu
from jax.sharding import PartitionSpec as P

MESH = pl.DeviceIdType.MESH
F32 = jnp.float32
BF16 = jnp.bfloat16


class Place:
    def __init__(self):
        s = lax.axis_index("seq")
        m = lax.axis_index("mp")
        self.s, self.m = s, m
        self.x, self.zh = s // 4, s % 4
        self.y, self.zl, self.c = m // 4, (m // 2) % 2, m % 2
        self.sib = (s, self.mp(0, self.zl, 1 - self.c))
        self.zn = (s, self.mp(0, 1 - self.zl, self.c))
        self.yp = (s, self.mp(1, self.zl, self.c))
        self.ym = (s, self.mp(3, self.zl, self.c))
        self.zp = (self.seq(0, 1), m)
        self.zm = (self.seq(0, 3), m)
        self.xp = (self.seq(1, 0), m)
        self.xm = (self.seq(3, 0), m)
        self.nxt = ((s + 1) % 16, m)
        self.prv = ((s + 15) % 16, m)

    def mp(self, dy, zl, c):
        return (((self.y + dy) % 4) * 2 + zl) * 2 + c

    def pair(self, dy, zl):
        return ((self.y + dy) % 4) * 2 + zl

    def seq(self, dx, dz):
        return ((self.x + dx) % 4) * 4 + (self.zh + dz) % 4


class Wire:
    def __init__(self, send_sem, recv_sem):
        self.send_sem, self.recv_sem = send_sem, recv_sem
        self.count = 0
        self.open = []

    def send(self, src, dst, to):
        k = self.count
        self.count += 1
        copy = pltpu.make_async_remote_copy(
            src_ref=src,
            dst_ref=dst,
            send_sem=self.send_sem.at[k],
            recv_sem=self.recv_sem.at[k],
            device_id=to,
            device_id_type=MESH,
        )
        copy.start()
        self.open.append(copy)
        return k

    def wait(self, k, landing, frm):
        pltpu.make_async_remote_copy(
            src_ref=landing,
            dst_ref=landing,
            send_sem=self.send_sem.at[k],
            recv_sem=self.recv_sem.at[k],
            device_id=frm,
            device_id_type=MESH,
        ).wait_recv()

    def finish(self):
        for copy in self.open:
            copy.wait_send()


def greet(peers):
    barrier = pltpu.get_barrier_semaphore()
    for peer in peers:
        pl.semaphore_signal(barrier, inc=1, device_id=peer, device_id_type=MESH)
    pl.semaphore_wait(barrier, len(peers))


def gather_mp(w, p, shard, out):
    mine = p.mp(0, p.zl, p.c)
    o = 1 - p.zl
    oc = 1 - p.c
    at = lambda dy, zl, c: out.at[p.mp(dy, zl, c)]
    own = out.at[mine]
    k_y1 = w.send(shard, own, p.yp)
    k_y2 = w.send(shard, own, p.ym)
    k_z = w.send(shard, own, p.zn)
    k_s = w.send(shard, own, p.sib)
    out[mine] = shard[...]
    yield
    w.wait(k_z, at(0, o, p.c), p.zn)
    zb = at(0, o, p.c)
    k_z1 = w.send(zb, zb, p.yp)
    k_z2 = w.send(zb, zb, p.ym)
    k_zs = w.send(zb, zb, p.sib)
    yield
    b = at(3, p.zl, p.c)
    w.wait(k_y1, b, p.ym)
    k_f1 = w.send(b, b, p.yp)
    k_s1 = w.send(b, b, p.sib)
    b = at(1, p.zl, p.c)
    w.wait(k_y2, b, p.yp)
    k_s2 = w.send(b, b, p.sib)
    yield
    b = at(1, o, p.c)
    w.wait(k_z2, b, p.yp)
    k_f2 = w.send(b, b, p.ym)
    k_s3 = w.send(b, b, p.sib)
    b = at(3, o, p.c)
    w.wait(k_z1, b, p.ym)
    k_s4 = w.send(b, b, p.sib)
    yield
    b = at(2, p.zl, p.c)
    w.wait(k_f1, b, p.ym)
    k_s5 = w.send(b, b, p.sib)
    b = at(2, o, p.c)
    w.wait(k_f2, b, p.yp)
    k_s6 = w.send(b, b, p.sib)
    yield
    w.wait(k_s, at(0, p.zl, oc), p.sib)
    w.wait(k_zs, at(0, o, oc), p.sib)
    w.wait(k_s1, at(3, p.zl, oc), p.sib)
    w.wait(k_s2, at(1, p.zl, oc), p.sib)
    w.wait(k_s3, at(1, o, oc), p.sib)
    w.wait(k_s4, at(3, o, oc), p.sib)
    w.wait(k_s5, at(2, p.zl, oc), p.sib)
    w.wait(k_s6, at(2, o, oc), p.sib)


def gather_seq(w, p, shard, out, up):
    mine = p.seq(0, 0)
    at = lambda dx, dz: out.at[p.seq(dx, dz)]
    own = out.at[mine]
    k_zp = w.send(shard, own, p.zp)
    k_zm = w.send(shard, own, p.zm)
    kx = {}
    kx[0] = (w.send(shard, own, p.xp), w.send(shard, own, p.xm))
    out[mine] = shard[...]

    def spread(dz):
        b = at(0, dz)
        kx[dz] = (w.send(b, b, p.xp), w.send(b, b, p.xm))

    kf = {}

    def relay(dz, upward):
        k1, k2 = kx[dz]
        if upward:
            b = at(3, dz)
            w.wait(k1, b, p.xm)
            kf[dz] = (w.send(b, b, p.xp), upward)
            w.wait(k2, at(1, dz), p.xp)
        else:
            b = at(1, dz)
            w.wait(k2, b, p.xp)
            kf[dz] = (w.send(b, b, p.xm), upward)
            w.wait(k1, at(3, dz), p.xm)

    yield
    if up:
        b = at(0, 3)
        w.wait(k_zp, b, p.zm)
        k_zf = w.send(b, b, p.zp)
        spread(3)
        w.wait(k_zm, at(0, 1), p.zp)
        spread(1)
    else:
        b = at(0, 1)
        w.wait(k_zm, b, p.zp)
        k_zf = w.send(b, b, p.zm)
        spread(1)
        w.wait(k_zp, at(0, 3), p.zm)
        spread(3)
    yield
    relay(0, up)
    yield
    w.wait(k_zf, at(0, 2), p.zm if up else p.zp)
    spread(2)
    yield
    relay(3 if up else 1, up)
    yield
    relay(1 if up else 3, not up)
    yield
    relay(2, not up)
    yield
    for dz, (k, upward) in kf.items():
        w.wait(k, at(2, dz), p.xm if upward else p.xp)


def scatter_mp(w, p, part, sibl, acc, land, result):
    o = 1 - p.zl
    ks = {}
    for dy in (2, 1, 3, 0):
        row = ((p.y + dy) % 4) * 2
        ks[dy] = w.send(
            part.at[pl.ds(row, 2), 1 - p.c], sibl.at[pl.ds(row, 2)], p.sib
        )
    yield

    def combine(dy):
        row = ((p.y + dy) % 4) * 2
        w.wait(ks[dy], sibl.at[pl.ds(row, 2)], p.sib)
        for zl in (0, 1):
            acc[row + zl] = (
                part[row + zl, p.c].astype(F32) + sibl[row + zl].astype(F32)
            ).astype(BF16)

    combine(2)
    k0 = w.send(acc.at[p.pair(2, p.zl)], land.at[0], p.yp)
    k1 = w.send(acc.at[p.pair(2, o)], land.at[1], p.ym)
    combine(1)
    k2b = w.send(acc.at[p.pair(1, o)], land.at[2], p.yp)
    combine(3)
    k3a = w.send(acc.at[p.pair(3, p.zl)], land.at[3], p.ym)
    combine(0)
    yield
    w.wait(k0, land.at[0], p.ym)
    i = p.pair(1, p.zl)
    acc[i] = (acc[i].astype(F32) + land[0].astype(F32)).astype(BF16)
    k2a = w.send(acc.at[i], land.at[4], p.yp)
    w.wait(k1, land.at[1], p.yp)
    i = p.pair(3, o)
    acc[i] = (acc[i].astype(F32) + land[1].astype(F32)).astype(BF16)
    k3b = w.send(acc.at[i], land.at[5], p.ym)
    yield
    w.wait(k2b, land.at[2], p.ym)
    w.wait(k3b, land.at[5], p.yp)
    i = p.pair(0, o)
    acc[i] = (acc[i].astype(F32) + land[2].astype(F32) + land[5].astype(F32)).astype(BF16)
    kz = w.send(acc.at[i], land.at[6], p.zn)
    yield
    w.wait(k3a, land.at[3], p.yp)
    w.wait(k2a, land.at[4], p.ym)
    w.wait(kz, land.at[6], p.zn)
    result(
        acc[p.pair(0, p.zl)].astype(F32)
        + land[3].astype(F32)
        + land[4].astype(F32)
        + land[6].astype(F32)
    )


def drain(gens):
    gens = list(gens)
    while gens:
        gens = [g for g in gens if next(g, True) is None]


def gather_pair(w, p, shard, out):
    o, oc = 1 - p.zl, 1 - p.c
    mine = p.zl * 2 + p.c
    k_z = w.send(shard, out.at[mine], p.zn)
    k_s = w.send(shard, out.at[mine], p.sib)
    out[mine] = shard[...]
    yield
    b = out.at[o * 2 + p.c]
    w.wait(k_z, b, p.zn)
    k_zs = w.send(b, b, p.sib)
    yield
    w.wait(k_s, out.at[p.zl * 2 + oc], p.sib)
    w.wait(k_zs, out.at[o * 2 + oc], p.sib)


def gather_y(w, p, shard, out):
    rows = shard.shape[0] // 2
    lo, hi = pl.ds(0, rows), pl.ds(rows, rows)
    at = lambda dy: (p.y + dy) % 4
    own = out.at[at(0)]
    k1 = w.send(shard, own, p.yp)
    k2 = w.send(shard, own, p.ym)
    out[at(0)] = shard[...]
    yield
    w.wait(k1, out.at[at(3)], p.ym)
    b = out.at[at(3), lo]
    f1 = w.send(b, b, p.yp)
    w.wait(k2, out.at[at(1)], p.yp)
    b = out.at[at(1), hi]
    f2 = w.send(b, b, p.ym)
    yield
    w.wait(f1, out.at[at(2), lo], p.ym)
    w.wait(f2, out.at[at(2), hi], p.yp)


def scatter_y(w, p, blk, index, ready, land, result):
    rows = blk.shape[1] // 2
    lo, hi = pl.ds(0, rows), pl.ds(rows, rows)
    i0, i1, i2, i3 = index(0), index(1), index(2), index(3)
    ready(2)
    k0 = w.send(blk.at[i2, lo], land.at[0], p.yp)
    k1 = w.send(blk.at[i2, hi], land.at[1], p.ym)
    yield
    ready(1)
    k2b = w.send(blk.at[i1, hi], land.at[2], p.yp)
    ready(3)
    k3a = w.send(blk.at[i3, lo], land.at[3], p.ym)
    yield
    w.wait(k0, land.at[0], p.ym)
    blk[i1, lo, :] = (blk[i1, lo, :].astype(F32) + land[0].astype(F32)).astype(BF16)
    k2a = w.send(blk.at[i1, lo], land.at[4], p.yp)
    w.wait(k1, land.at[1], p.yp)
    blk[i3, hi, :] = (blk[i3, hi, :].astype(F32) + land[1].astype(F32)).astype(BF16)
    k3b = w.send(blk.at[i3, hi], land.at[5], p.ym)
    yield
    ready(0)
    w.wait(k2b, land.at[2], p.ym)
    w.wait(k3a, land.at[3], p.yp)
    w.wait(k2a, land.at[4], p.ym)
    w.wait(k3b, land.at[5], p.yp)
    f = lambda v: v.astype(F32)
    result(lo, f(blk[i0, lo, :]) + f(land[4]) + f(land[3]))
    result(hi, f(blk[i0, hi, :]) + f(land[2]) + f(land[5]))


def scatter_zy(w, p, part, sibl, acc, zland, land, result):
    o = 1 - p.zl
    ks, kz = {}, {}
    for dy in (2, 1, 3, 0):
        row = ((p.y + dy) % 4) * 2
        ks[dy] = w.send(
            part.at[pl.ds(row, 2), 1 - p.c], sibl.at[pl.ds(row, 2)], p.sib
        )
    yield
    for dy in (2, 1, 3, 0):
        row = ((p.y + dy) % 4) * 2
        w.wait(ks[dy], sibl.at[pl.ds(row, 2)], p.sib)
        for zl in (o, p.zl):
            acc[row + zl] = (
                part[row + zl, p.c].astype(F32) + sibl[row + zl].astype(F32)
            ).astype(BF16)
        kz[dy] = w.send(acc.at[row + o], zland.at[dy], p.zn)
    yield

    def ready(dy):
        w.wait(kz[dy], zland.at[dy], p.zn)
        i = p.pair(dy, p.zl)
        acc[i] = (acc[i].astype(F32) + zland[dy].astype(F32)).astype(BF16)

    yield from scatter_y(w, p, acc, lambda dy: p.pair(dy, p.zl), ready, land, result)


NT = (((1,), (1,)), ((), ()))


def body(
    hid, cot, wq, wo, wkv, table, ids, lens, up, down,
    out_o, grad_o,
    tab, idsb, onehot, epart, esib, eacc, eland, emb_own, emb4, normed,
    up4, down4, fpart, fblk, fland, enc_own, enc,
    hid_s, cot_s, wq_s, wo_s, wkv_s, wkv_w, wkv_f, kv_s,
    q_s, d_s, q_land, a_s, a_land,
    part_o, part_g, sib_o, sib_g, acc_o, acc_g, land_o, zland_g, land_g, sum_o,
    tab_sem, send_sem, recv_sem,
):
    p = Place()
    w = Wire(send_sem, recv_sem)
    fetch = pltpu.make_async_copy(table, tab.at[pl.ds(0, 4000)], tab_sem)
    fetch.start()
    greet((p.sib, p.zn, p.yp, p.ym, p.zp, p.zm, p.xp, p.xm, p.nxt, p.prv))

    gh = gather_mp(w, p, hid, hid_s)
    gc = gather_mp(w, p, cot, cot_s)
    gu = gather_pair(w, p, up, up4)
    gd = gather_pair(w, p, down, down4)
    gq = gather_seq(w, p, wq, wq_s, True)
    go = gather_seq(w, p, wo, wo_s, False)
    gk = gather_seq(w, p, wkv, wkv_s, True)
    next(gh), next(gc), next(gu), next(gq), next(gd), next(go), next(gk)

    tab[pl.ds(4000, 96), :] = jnp.zeros((96, 896), BF16)
    cols = jnp.transpose(ids[...] - p.m * 4000)
    for r in range(8):
        idsb[r] = jnp.broadcast_to(cols[:, r : r + 1], (128, 128))
    lane = lax.broadcasted_iota(jnp.int32, (64, 128), 1)

    def lookup(c):
        def hot(r, _):
            mine = idsb[r, pl.ds(pl.multiple_of(c * 64, 64), 64), :] - lane
            rows = pl.ds(pl.multiple_of(r * 64, 64), 64)
            for k in range(32):
                onehot[rows, k * 128 : (k + 1) * 128] = jnp.where(
                    mine == k * 128, 1.0, 0.0
                ).astype(BF16)
            return 0

        lax.fori_loop(0, 8, hot, 0)

        def pick(cols_at, width):
            got = jnp.dot(onehot[...], tab[:, cols_at], preferred_element_type=F32)
            for r in range(8):
                epart[r, c, :, cols_at] = got[r * 64 : (r + 1) * 64].astype(BF16)

        def wide(n, _):
            pick(pl.ds(pl.multiple_of(n * 256, 256), 256), 256)
            return 0

        lax.fori_loop(0, 3, wide, 0)
        pick(pl.ds(768, 128), 128)

    def keep_emb(total):
        emb_own[...] = total.astype(BF16)

    fetch.wait()
    lookup(1 - p.c)
    ers = scatter_mp(w, p, epart, esib, eacc, eland, keep_emb)
    next(ers)
    next(gh), next(gc)
    lookup(p.c)
    next(ers)
    next(gh), next(gc)
    next(ers)
    next(gq)
    next(ers)
    next(gh), next(gc)
    next(ers, None)
    ey = gather_y(w, p, emb_own, emb4)
    next(ey)
    next(gu), next(gq)
    next(ey)
    next(gh), next(gc)
    next(ey, None)
    e = emb4[...].reshape(256, 896).astype(F32)
    normed[...] = (
        e * lax.rsqrt(jnp.mean(e * e, axis=-1, keepdims=True) + 1e-06)
    ).astype(BF16)
    next(gd), next(gu, None), next(gd, None)

    def units(j, first):
        act = jax.nn.gelu(
            lax.dot_general(normed[...], up4[j], NT, preferred_element_type=F32)
        ).astype(BF16)
        got = jnp.dot(act, down4[j], preferred_element_type=F32)
        if first:
            fpart[...] = got
        else:
            fpart[...] += got

    units(0, True)

    def more(j, _):
        units(j, False)
        return 0

    lax.fori_loop(1, 4, more, 0)
    for y in range(4):
        fblk[y] = fpart[y * 64 : (y + 1) * 64, :].astype(BF16)

    def keep_enc(rows, total):
        v = emb_own[rows, :].astype(F32) + total
        v = v * lax.rsqrt(jnp.mean(v * v, axis=-1, keepdims=True) + 1e-06)
        enc_own[rows, :] = v.astype(BF16)

    fy = scatter_y(
        w, p, fblk, lambda dy: (p.y + dy) % 4, lambda dy: None, fland, keep_enc
    )
    next(fy)
    next(fy)
    next(go)
    next(fy)
    next(gk)
    next(fy, None)
    ga = gather_mp(w, p, enc_own, enc)
    next(ga)
    next(gh, None), next(gc, None)
    next(gq), next(go), next(gk)
    next(ga)
    next(gq), next(go), next(gk)
    next(ga)
    next(gq), next(go), next(gk)
    next(ga)
    drain([gq])

    def project(src, weights, dst):
        def step(b, total):
            return total + jnp.dot(src[b], weights[b], preferred_element_type=F32)

        total = lax.fori_loop(0, 16, step, jnp.zeros((256, 256), F32))
        dst[...] = pltpu.roll(total, 193, 0).astype(BF16)

    project(hid_s, wq_s, q_s)
    kq = w.send(q_s.at[pl.ds(192, 64)], q_land.at[0], p.prv)
    next(go), next(gk)
    next(ga)
    drain([go, gk])
    project(cot_s, wo_s, d_s)
    kd = w.send(d_s.at[pl.ds(192, 64)], q_land.at[1], p.prv)
    for i in range(16):
        wkv_f[pl.ds(56 * i, 56), :] = wkv_s[i].astype(F32)
    wkv_w[...] = wkv_f[...].astype(BF16)
    next(ga, None)

    def keyval(g, _):
        rows = enc[pl.ds(g * 4, 4)].reshape(256, 896)
        kv_s[g] = jnp.dot(rows, wkv_w[...], preferred_element_type=F32).astype(BF16)
        return 0

    lax.fori_loop(0, 4, keyval, 0)
    w.wait(kq, q_land.at[0], p.nxt)
    w.wait(kd, q_land.at[1], p.nxt)
    for copy in w.open:
        copy.wait_send()
    w.open = []
    first = lax.broadcasted_iota(jnp.int32, (64, 256), 0) == 0
    tail = pl.ds(192, 64)
    for dst, i in ((q_s, 0), (d_s, 1)):
        dst[tail, :] = jnp.where(
            first, dst[tail, :].astype(F32), q_land[i].astype(F32)
        ).astype(BF16)

    key = lax.broadcasted_iota(jnp.int32, (64, 256), 1)
    scale = 128 ** (-0.5)

    def attend(g):
        rows = pl.ds(pl.multiple_of(g * 64, 64), 64)
        span = p.s * 4 + g
        live = key < jnp.where(key < 128, lens[span, 0], lens[span, 1] + 128)
        for h in range(2):
            head = slice(h * 128, (h + 1) * 128)
            k = kv_s[g, :, h * 256 : h * 256 + 128]
            v = kv_s[g, :, h * 256 + 128 : (h + 1) * 256]
            score = lax.dot_general(q_s[rows, head], k, NT, preferred_element_type=F32)
            expo = jnp.where(live, jnp.exp(score * scale), 0.0)
            prob = expo / jnp.sum(expo, axis=-1, keepdims=True)
            a_s[0, rows, head] = jnp.dot(
                prob.astype(BF16), v, preferred_element_type=F32
            ).astype(BF16)
            d_prob = lax.dot_general(d_s[rows, head], v, NT, preferred_element_type=F32)
            delta = jnp.sum(prob * d_prob, axis=-1, keepdims=True)
            d_score = (prob * (d_prob - delta) * scale).astype(BF16)
            a_s[1, rows, head] = jnp.dot(
                d_score, k, preferred_element_type=F32
            ).astype(BF16)

    attend(3)
    ka = w.send(a_s.at[:, tail], a_land, p.nxt)

    def others(g, _):
        attend(g)
        return 0

    lax.fori_loop(0, 3, others, 0)
    w.wait(ka, a_land, p.prv)
    for copy in w.open:
        copy.wait_send()
    w.open = []
    for i in range(2):
        got = jnp.where(p.s > 0, a_land[i].astype(F32), 0.0)
        a_s[i, tail, :] = jnp.where(first, a_s[i, tail, :].astype(F32), got).astype(BF16)

    def fill(i, weights, part, c):
        @pl.loop(0, 8)
        def _(b):
            part[b, c] = lax.dot_general(
                a_s[i], weights[b * 2 + c], NT, preferred_element_type=F32
            ).astype(BF16)

    def keep_out(total):
        out_o[...] = pltpu.roll(total, 63, 0).astype(BF16)

    def keep_grad(rows, total):
        sum_o[rows, :] = total

    ro = scatter_mp(w, p, part_o, sib_o, acc_o, land_o, keep_out)
    rg = scatter_zy(w, p, part_g, sib_g, acc_g, zland_g, land_g, keep_grad)
    fill(1, wq_s, part_g, 1 - p.c)
    next(rg)
    fill(0, wo_s, part_o, 1 - p.c)
    next(ro)
    fill(1, wq_s, part_g, p.c)
    next(rg)
    fill(0, wo_s, part_o, p.c)
    next(ro)
    next(rg)
    next(ro)
    next(rg)
    next(ro)
    next(rg)
    next(ro, None)
    next(rg, None)
    grad_o[...] = pltpu.roll(sum_o[...], 63, 0).astype(BF16)
    w.finish()


def per_device(
    hidden, cotangent, neighbour_ids, neighbour_lengths, embed_table,
    enc_up, enc_down, w_query, w_keyval, w_out,
):
    blk = (256, 256)
    row = (64, 896)
    bf = lambda *s: pltpu.VMEM(s, BF16)
    vm = pl.BlockSpec(memory_space=pltpu.VMEM)
    messages = 190
    out, grad = pl.pallas_call(
        body,
        out_shape=[jax.ShapeDtypeStruct(blk, BF16)] * 2,
        in_specs=[vm] * 5
        + [pl.BlockSpec(memory_space=pl.ANY), vm, pl.BlockSpec(memory_space=pltpu.SMEM), vm, vm],
        out_specs=[vm, vm],
        scratch_shapes=[
            bf(4096, 896), pltpu.VMEM((8, 128, 128), jnp.int32), bf(512, 4096),
            bf(8, 2, *row), bf(8, *row), bf(8, *row), bf(7, *row), bf(*row), bf(4, *row),
            bf(256, 896),
            bf(4, 224, 896), bf(4, 224, 896), pltpu.VMEM((256, 896), F32), bf(4, *row),
            bf(6, 32, 896), bf(*row), bf(16, *row),
            bf(16, *blk), bf(16, *blk), bf(16, *blk), bf(16, *blk), bf(16, 56, 512),
            bf(896, 512), pltpu.VMEM((896, 512), F32), bf(4, 256, 512),
            bf(*blk), bf(*blk), bf(2, 64, 256), bf(2, *blk), bf(2, 64, 256),
            bf(8, 2, *blk), bf(8, 2, *blk), bf(8, *blk), bf(8, *blk), bf(8, *blk), bf(8, *blk),
            bf(7, *blk), bf(4, *blk), bf(6, 128, 256), pltpu.VMEM(blk, F32),
            pltpu.SemaphoreType.DMA,
            pltpu.SemaphoreType.DMA((messages,)), pltpu.SemaphoreType.DMA((messages,)),
        ],
        compiler_params=pltpu.CompilerParams(
            collective_id=1, has_side_effects=True, vmem_limit_bytes=62 * 1024 * 1024
        ),
        name="block",
    )(
        hidden, cotangent, w_query.reshape(blk), w_out.reshape(blk),
        w_keyval.reshape(56, 512), embed_table, neighbour_ids.reshape(8, 128),
        neighbour_lengths, enc_up, enc_down,
    )
    return out, grad


def solution(mesh):
    return jax.shard_map(
        per_device,
        mesh=mesh,
        in_specs=(
            P("seq", "mp"),
            P("seq", "mp"),
            P("seq", None, None),
            P(),
            P("mp", None),
            P("mp", None),
            P("mp", None),
            P("seq", "mp", None),
            P("seq", "mp", None, None),
            P("seq", "mp", None),
        ),
        out_specs=(P("seq", "mp"), P("seq", "mp")),
        check_vma=False,
    )
```

```python
import functools

import jax
import jax.numpy as jnp
from jax import lax
from jax.experimental import pallas as pl
from jax.experimental.pallas import tpu as pltpu
from jax.sharding import PartitionSpec as P

MESH = pl.DeviceIdType.MESH
F32 = jnp.float32
BF16 = jnp.bfloat16


class Place:
    def __init__(self):
        s = lax.axis_index("seq")
        m = lax.axis_index("mp")
        self.s, self.m = s, m
        self.x, self.zh = s // 4, s % 4
        self.y, self.zl, self.c = m // 4, (m // 2) % 2, m % 2
        self.sib = (s, self.mp(0, self.zl, 1 - self.c))
        self.zn = (s, self.mp(0, 1 - self.zl, self.c))
        self.zo = (self.seq(0, 2 * self.zl + 3), self.mp(0, 1 - self.zl, self.c))
        self.yp = (s, self.mp(1, self.zl, self.c))
        self.ym = (s, self.mp(3, self.zl, self.c))
        self.zp = (self.seq(0, 1), m)
        self.zm = (self.seq(0, 3), m)
        self.xp = (self.seq(1, 0), m)
        self.xm = (self.seq(3, 0), m)
        self.nxt = ((s + 1) % 16, m)
        self.prv = ((s + 15) % 16, m)

    def mp(self, dy, zl, c):
        return (((self.y + dy) % 4) * 2 + zl) * 2 + c

    def pair(self, dy, zl):
        return ((self.y + dy) % 4) * 2 + zl

    def seq(self, dx, dz):
        return ((self.x + dx) % 4) * 4 + (self.zh + dz) % 4


class Wire:
    def __init__(self, send_sem, recv_sem):
        self.send_sem, self.recv_sem = send_sem, recv_sem
        self.count = 0
        self.open = []

    def send(self, src, dst, to):
        k = self.count
        self.count += 1
        copy = pltpu.make_async_remote_copy(
            src_ref=src,
            dst_ref=dst,
            send_sem=self.send_sem.at[k],
            recv_sem=self.recv_sem.at[k],
            device_id=to,
            device_id_type=MESH,
        )
        copy.start()
        self.open.append(copy)
        return k

    def wait(self, k, landing, frm):
        pltpu.make_async_remote_copy(
            src_ref=landing,
            dst_ref=landing,
            send_sem=self.send_sem.at[k],
            recv_sem=self.recv_sem.at[k],
            device_id=frm,
            device_id_type=MESH,
        ).wait_recv()

    def finish(self):
        for copy in self.open:
            copy.wait_send()


def greet(peers):
    barrier = pltpu.get_barrier_semaphore()
    for peer in peers:
        pl.semaphore_signal(barrier, inc=1, device_id=peer, device_id_type=MESH)
    pl.semaphore_wait(barrier, len(peers))


def gather_mp(w, p, shard, out):
    mine = p.mp(0, p.zl, p.c)
    o = 1 - p.zl
    oc = 1 - p.c
    at = lambda dy, zl, c: out.at[p.mp(dy, zl, c)]
    own = out.at[mine]
    k_y1 = w.send(shard, own, p.yp)
    k_y2 = w.send(shard, own, p.ym)
    k_z = w.send(shard, own, p.zn)
    k_s = w.send(shard, own, p.sib)
    out[mine] = shard[...]
    yield
    w.wait(k_z, at(0, o, p.c), p.zn)
    zb = at(0, o, p.c)
    k_z1 = w.send(zb, zb, p.yp)
    k_z2 = w.send(zb, zb, p.ym)
    k_zs = w.send(zb, zb, p.sib)
    yield
    b = at(3, p.zl, p.c)
    w.wait(k_y1, b, p.ym)
    k_f1 = w.send(b, b, p.yp)
    k_s1 = w.send(b, b, p.sib)
    b = at(1, p.zl, p.c)
    w.wait(k_y2, b, p.yp)
    k_s2 = w.send(b, b, p.sib)
    yield
    b = at(1, o, p.c)
    w.wait(k_z2, b, p.yp)
    k_f2 = w.send(b, b, p.ym)
    k_s3 = w.send(b, b, p.sib)
    b = at(3, o, p.c)
    w.wait(k_z1, b, p.ym)
    k_s4 = w.send(b, b, p.sib)
    yield
    b = at(2, p.zl, p.c)
    w.wait(k_f1, b, p.ym)
    k_s5 = w.send(b, b, p.sib)
    b = at(2, o, p.c)
    w.wait(k_f2, b, p.yp)
    k_s6 = w.send(b, b, p.sib)
    yield
    w.wait(k_s, at(0, p.zl, oc), p.sib)
    w.wait(k_zs, at(0, o, oc), p.sib)
    w.wait(k_s1, at(3, p.zl, oc), p.sib)
    w.wait(k_s2, at(1, p.zl, oc), p.sib)
    w.wait(k_s3, at(1, o, oc), p.sib)
    w.wait(k_s4, at(3, o, oc), p.sib)
    w.wait(k_s5, at(2, p.zl, oc), p.sib)
    w.wait(k_s6, at(2, o, oc), p.sib)


def scatter_mp(w, p, part, sibl, acc, land, result):
    o = 1 - p.zl
    ks = {}
    for dy in (2, 1, 3, 0):
        row = ((p.y + dy) % 4) * 2
        ks[dy] = w.send(
            part.at[pl.ds(row, 2), 1 - p.c], sibl.at[pl.ds(row, 2)], p.sib
        )
    yield

    def combine(dy):
        row = ((p.y + dy) % 4) * 2
        w.wait(ks[dy], sibl.at[pl.ds(row, 2)], p.sib)
        for zl in (0, 1):
            acc[row + zl] = (
                part[row + zl, p.c].astype(F32) + sibl[row + zl].astype(F32)
            ).astype(BF16)

    combine(2)
    k0 = w.send(acc.at[p.pair(2, p.zl)], land.at[0], p.yp)
    k1 = w.send(acc.at[p.pair(2, o)], land.at[1], p.ym)
    combine(1)
    k2b = w.send(acc.at[p.pair(1, o)], land.at[2], p.yp)
    combine(3)
    k3a = w.send(acc.at[p.pair(3, p.zl)], land.at[3], p.ym)
    combine(0)
    yield
    w.wait(k0, land.at[0], p.ym)
    i = p.pair(1, p.zl)
    acc[i] = (acc[i].astype(F32) + land[0].astype(F32)).astype(BF16)
    k2a = w.send(acc.at[i], land.at[4], p.yp)
    w.wait(k1, land.at[1], p.yp)
    i = p.pair(3, o)
    acc[i] = (acc[i].astype(F32) + land[1].astype(F32)).astype(BF16)
    k3b = w.send(acc.at[i], land.at[5], p.ym)
    yield
    w.wait(k2b, land.at[2], p.ym)
    w.wait(k3b, land.at[5], p.yp)
    i = p.pair(0, o)
    acc[i] = (acc[i].astype(F32) + land[2].astype(F32) + land[5].astype(F32)).astype(BF16)
    kz = w.send(acc.at[i], land.at[6], p.zn)
    yield
    w.wait(k3a, land.at[3], p.yp)
    w.wait(k2a, land.at[4], p.ym)
    w.wait(kz, land.at[6], p.zn)
    result(
        acc[p.pair(0, p.zl)].astype(F32)
        + land[3].astype(F32)
        + land[4].astype(F32)
        + land[6].astype(F32)
    )


def drain(gens):
    gens = list(gens)
    while gens:
        gens = [g for g in gens if next(g, True) is None]


def gather_seq(w, p, shard, out, up, late):
    mine = p.seq(0, 0)
    at = lambda dx, dz: out.at[p.seq(dx, dz)]
    own = out.at[mine]
    kx = {0: (w.send(shard, own, p.xp), w.send(shard, own, p.xm))}
    out[mine] = shard[...]

    def spread(dz):
        b = at(0, dz)
        kx[dz] = (w.send(b, b, p.xp), w.send(b, b, p.xm))

    kf = {}

    def relay(dz, upward):
        k1, k2 = kx[dz]
        if upward:
            b = at(3, dz)
            w.wait(k1, b, p.xm)
            kf[dz] = (w.send(b, b, p.xp), upward)
            w.wait(k2, at(1, dz), p.xp)
        else:
            b = at(1, dz)
            w.wait(k2, b, p.xp)
            kf[dz] = (w.send(b, b, p.xm), upward)
            w.wait(k1, at(3, dz), p.xm)

    yield
    if late:
        relay(0, up)
        yield
    k_zp = w.send(shard, own, p.zp)
    k_zm = w.send(shard, own, p.zm)
    yield
    if not late:
        relay(0, up)
        yield
    if up:
        b = at(0, 3)
        w.wait(k_zp, b, p.zm)
        k_zf = w.send(b, b, p.zp)
        spread(3)
        w.wait(k_zm, at(0, 1), p.zp)
        spread(1)
    else:
        b = at(0, 1)
        w.wait(k_zm, b, p.zp)
        k_zf = w.send(b, b, p.zm)
        spread(1)
        w.wait(k_zp, at(0, 3), p.zm)
        spread(3)
    yield
    w.wait(k_zf, at(0, 2), p.zm if up else p.zp)
    spread(2)
    yield
    relay(3 if up else 1, up)
    yield
    relay(1 if up else 3, not up)
    yield
    relay(2, not up)
    yield
    for dz, (k, upward) in kf.items():
        w.wait(k, at(2, dz), p.xm if upward else p.xp)


def gather_pair(w, p, shard, out):
    o, oc = 1 - p.zl, 1 - p.c
    mine = p.zl * 2 + p.c
    k_z = w.send(shard, out.at[mine], p.zo)
    k_s = w.send(shard, out.at[mine], p.sib)
    out[mine] = shard[...]
    yield
    b = out.at[o * 2 + p.c]
    w.wait(k_z, b, p.zo)
    k_zs = w.send(b, b, p.sib)
    yield
    w.wait(k_s, out.at[p.zl * 2 + oc], p.sib)
    w.wait(k_zs, out.at[o * 2 + oc], p.sib)


def gather_y(w, p, shard, out):
    rows = shard.shape[0] // 2
    lo, hi = pl.ds(0, rows), pl.ds(rows, rows)
    at = lambda dy: (p.y + dy) % 4
    own = out.at[at(0)]
    k1 = w.send(shard, own, p.yp)
    k2 = w.send(shard, own, p.ym)
    out[at(0)] = shard[...]
    yield
    w.wait(k1, out.at[at(3)], p.ym)
    b = out.at[at(3), lo]
    f1 = w.send(b, b, p.yp)
    w.wait(k2, out.at[at(1)], p.yp)
    b = out.at[at(1), hi]
    f2 = w.send(b, b, p.ym)
    yield
    w.wait(f1, out.at[at(2), lo], p.ym)
    w.wait(f2, out.at[at(2), hi], p.yp)


def scatter_y(w, p, blk, index, ready, land, result):
    rows = blk.shape[1] // 2
    lo, hi = pl.ds(0, rows), pl.ds(rows, rows)
    i0, i1, i2, i3 = index(0), index(1), index(2), index(3)
    ready(2)
    k0 = w.send(blk.at[i2, lo], land.at[0], p.yp)
    k1 = w.send(blk.at[i2, hi], land.at[1], p.ym)
    yield
    ready(1)
    k2b = w.send(blk.at[i1, hi], land.at[2], p.yp)
    ready(3)
    k3a = w.send(blk.at[i3, lo], land.at[3], p.ym)
    yield
    w.wait(k0, land.at[0], p.ym)
    blk[i1, lo, :] = (blk[i1, lo, :].astype(F32) + land[0].astype(F32)).astype(BF16)
    k2a = w.send(blk.at[i1, lo], land.at[4], p.yp)
    w.wait(k1, land.at[1], p.yp)
    blk[i3, hi, :] = (blk[i3, hi, :].astype(F32) + land[1].astype(F32)).astype(BF16)
    k3b = w.send(blk.at[i3, hi], land.at[5], p.ym)
    yield
    ready(0)
    w.wait(k2b, land.at[2], p.ym)
    w.wait(k3a, land.at[3], p.yp)
    w.wait(k2a, land.at[4], p.ym)
    w.wait(k3b, land.at[5], p.yp)
    f = lambda v: v.astype(F32)
    result(lo, f(blk[i0, lo, :]) + f(land[4]) + f(land[3]))
    result(hi, f(blk[i0, hi, :]) + f(land[2]) + f(land[5]))


def scatter_zy(w, p, part, sibl, acc, zland, land, result):
    o = 1 - p.zl
    ks, kz = {}, {}
    for dy in (2, 1, 3, 0):
        row = ((p.y + dy) % 4) * 2
        ks[dy] = w.send(
            part.at[pl.ds(row, 2), 1 - p.c], sibl.at[pl.ds(row, 2)], p.sib
        )
    yield
    for dy in (2, 1, 3, 0):
        row = ((p.y + dy) % 4) * 2
        w.wait(ks[dy], sibl.at[pl.ds(row, 2)], p.sib)
        for zl in (o, p.zl):
            acc[row + zl] = (
                part[row + zl, p.c].astype(F32) + sibl[row + zl].astype(F32)
            ).astype(BF16)
        kz[dy] = w.send(acc.at[row + o], zland.at[dy], p.zn)
    yield

    def ready(dy):
        w.wait(kz[dy], zland.at[dy], p.zn)
        i = p.pair(dy, p.zl)
        acc[i] = (acc[i].astype(F32) + zland[dy].astype(F32)).astype(BF16)

    yield from scatter_y(w, p, acc, lambda dy: p.pair(dy, p.zl), ready, land, result)


NT = (((1,), (1,)), ((), ()))


def body(
    hid, cot, wq, wo, wkv, table, ids, lens, up, down,
    res,
    tab, idsb, onehot, epart, esib, eacc, eland, emb_own, emb4, normed,
    up4, down4, acts, fblk, fland, enc_own, enc,
    hid_s, cot_s, wq_s, wo_s, wkv_s, wkv_w, wkv_f, kv_s,
    q_s, d_s, q_land, last, a_s, a_land,
    part_o, part_g, sib_o, sib_g, acc_o, acc_g, land_o, zland_g, land_g, sum_o,
    tab_sem, send_sem, recv_sem,
):
    p = Place()
    w = Wire(send_sem, recv_sem)
    fetch = pltpu.make_async_copy(table, tab.at[pl.ds(0, 4000)], tab_sem)
    fetch.start()
    greet((p.sib, p.zn, p.zo, p.yp, p.ym, p.zp, p.zm, p.xp, p.xm, p.nxt, p.prv))

    gh = gather_mp(w, p, hid, hid_s)
    gc = gather_mp(w, p, cot, cot_s)
    gu = gather_pair(w, p, up, up4)
    gd = gather_pair(w, p, down, down4)
    gq = gather_seq(w, p, wq, wq_s, True, False)
    go = gather_seq(w, p, wo, wo_s, False, True)
    gk = gather_seq(w, p, wkv, wkv_s, True, True)
    next(gh), next(gc), next(gu)
    next(gq), next(gk), next(go)

    tab[pl.ds(4000, 96), :] = jnp.zeros((96, 896), BF16)
    cols = jnp.transpose(ids[...] - p.m * 4000)
    for r in range(8):
        idsb[r] = jnp.broadcast_to(cols[:, r : r + 1], (128, 128))
    lane = lax.broadcasted_iota(jnp.int32, (64, 128), 1)

    def lookup(c):
        def hot(r, _):
            mine = idsb[r, pl.ds(pl.multiple_of(c * 64, 64), 64), :] - lane
            rows = pl.ds(pl.multiple_of(r * 64, 64), 64)
            for k in range(32):
                onehot[rows, k * 128 : (k + 1) * 128] = jnp.where(
                    mine == k * 128, 1.0, 0.0
                ).astype(BF16)
            return 0

        lax.fori_loop(0, 8, hot, 0)

        def pick(cols_at, width):
            got = jnp.dot(onehot[...], tab[:, cols_at], preferred_element_type=F32)
            for r in range(8):
                epart[r, c, :, cols_at] = got[r * 64 : (r + 1) * 64].astype(BF16)

        def wide(n, _):
            pick(pl.ds(pl.multiple_of(n * 256, 256), 256), 256)
            return 0

        lax.fori_loop(0, 3, wide, 0)
        pick(pl.ds(768, 128), 128)

    def keep_emb(total):
        emb_own[...] = total.astype(BF16)

    fetch.wait()
    lookup(1 - p.c)
    ers = scatter_mp(w, p, epart, esib, eacc, eland, keep_emb)
    next(ers)
    next(gh), next(gc)
    next(gq)
    lookup(p.c)
    next(ers)
    next(gd)
    next(gq), next(gk), next(go)
    next(ers)
    next(gh), next(gc)
    next(gq)
    next(ers)
    next(gk), next(go)
    next(gh), next(gc)
    next(ers, None)
    ey = gather_y(w, p, emb_own, emb4)
    next(ey)
    next(gu)
    next(ey)
    next(gd)
    next(ey, None)
    next(gu, None), next(gd, None)

    e = emb4[...].reshape(256, 896).astype(F32)
    normed[...] = (
        e * lax.rsqrt(jnp.mean(e * e, axis=-1, keepdims=True) + 1e-06)
    ).astype(BF16)
    for j in range(4):
        acts[j] = jax.nn.gelu(
            lax.dot_general(normed[...], up4[j], NT, preferred_element_type=F32)
        ).astype(BF16)
    next(gh), next(gc)
    total = jnp.dot(acts[0], down4[0], preferred_element_type=F32)
    for j in range(1, 4):
        total = total + jnp.dot(acts[j], down4[j], preferred_element_type=F32)
    for y in range(4):
        fblk[y] = total[y * 64 : (y + 1) * 64, :].astype(BF16)

    def keep_enc(rows, total):
        v = emb_own[rows, :].astype(F32) + total
        v = v * lax.rsqrt(jnp.mean(v * v, axis=-1, keepdims=True) + 1e-06)
        enc_own[rows, :] = v.astype(BF16)

    fy = scatter_y(
        w, p, fblk, lambda dy: (p.y + dy) % 4, lambda dy: None, fland, keep_enc
    )
    next(fy)
    next(fy)
    next(gq)
    next(fy)
    next(gh, None), next(gc, None)
    next(gk)
    next(fy, None)
    ga = gather_mp(w, p, enc_own, enc)
    next(ga)
    next(gq), next(go)
    next(ga)
    next(gq)
    next(ga)
    next(gk), next(gq)
    next(ga)
    next(go), next(gk)
    next(ga)
    next(gk), next(go), next(gk)
    drain([gq])

    def project(src, weights, sums, columns, start):
        total = None if start else sums[...]
        for dx in columns:
            for dz in range(4):
                b = p.seq(dx, dz)
                got = jnp.dot(src[b], weights[b], preferred_element_type=F32)
                total = got if total is None else total + got
        sums[...] = total

    project(hid_s, wq_s, sum_o, (0, 1, 2, 3), True)
    q_s[...] = pltpu.roll(sum_o[...], 193, 0).astype(BF16)
    kq = w.send(q_s.at[pl.ds(192, 64)], q_land.at[0], p.prv)
    next(go)
    next(go)
    project(cot_s, wo_s, sum_o, (0,), True)
    drain([gk])
    for i in range(16):
        wkv_f[pl.ds(56 * i, 56), :] = wkv_s[i].astype(F32)
    wkv_w[...] = wkv_f[...].astype(BF16)
    drain([go])
    project(cot_s, wo_s, sum_o, (1, 3, 2), False)
    d_s[...] = pltpu.roll(sum_o[...], 193, 0).astype(BF16)
    kd = w.send(d_s.at[pl.ds(192, 64)], q_land.at[1], p.prv)
    next(ga, None)

    def keyval(g, _):
        rows = enc[pl.ds(g * 4, 4)].reshape(256, 896)
        kv_s[g] = jnp.dot(rows, wkv_w[...], preferred_element_type=F32).astype(BF16)
        return 0

    lax.fori_loop(0, 4, keyval, 0)
    w.wait(kq, q_land.at[0], p.nxt)
    w.wait(kd, q_land.at[1], p.nxt)
    first = lax.broadcasted_iota(jnp.int32, (64, 256), 0) == 0
    tail = pl.ds(192, 64)
    for i, src in ((0, q_s), (1, d_s)):
        last[i] = jnp.where(
            first, src[tail, :].astype(F32), q_land[i].astype(F32)
        ).astype(BF16)

    key = lax.broadcasted_iota(jnp.int32, (64, 256), 1)
    scale = 128 ** (-0.5)

    def attend(g):
        rows = slice(g * 64, (g + 1) * 64)
        span = p.s * 4 + g
        live = key < jnp.where(key < 128, lens[0, span], lens[1, span] + 128)
        for h in range(2):
            head = slice(h * 128, (h + 1) * 128)
            k = kv_s[g, :, h * 256 : h * 256 + 128]
            v = kv_s[g, :, h * 256 + 128 : (h + 1) * 256]
            q = last[0, :, head] if g == 3 else q_s[rows, head]
            d = last[1, :, head] if g == 3 else d_s[rows, head]
            score = lax.dot_general(q, k, NT, preferred_element_type=F32)
            expo = jnp.where(live, jnp.exp(score * scale), 0.0)
            prob = expo / jnp.sum(expo, axis=-1, keepdims=True)
            a_s[0, rows, head] = jnp.dot(
                prob.astype(BF16), v, preferred_element_type=F32
            ).astype(BF16)
            d_prob = lax.dot_general(d, v, NT, preferred_element_type=F32)
            delta = jnp.sum(prob * d_prob, axis=-1, keepdims=True)
            d_score = (prob * (d_prob - delta) * scale).astype(BF16)
            a_s[1, rows, head] = jnp.dot(
                d_score, k, preferred_element_type=F32
            ).astype(BF16)

    attend(3)
    ka = w.send(a_s.at[:, tail], a_land, p.nxt)

    for g in range(3):
        attend(g)
    w.wait(ka, a_land, p.prv)
    w.open.pop().wait_send()
    for i in range(2):
        got = jnp.where(p.s > 0, a_land[i].astype(F32), 0.0)
        a_s[i, tail, :] = jnp.where(first, a_s[i, tail, :].astype(F32), got).astype(BF16)

    def fill(i, weights, part, c):
        for b in range(8):
            part[b, c] = lax.dot_general(
                a_s[i], weights[b * 2 + c], NT, preferred_element_type=F32
            ).astype(BF16)

    def keep_out(total):
        res[0] = pltpu.roll(total, 63, 0).astype(BF16)

    def keep_grad(rows, total):
        sum_o[rows, :] = total

    ro = scatter_mp(w, p, part_o, sib_o, acc_o, land_o, keep_out)
    rg = scatter_zy(w, p, part_g, sib_g, acc_g, zland_g, land_g, keep_grad)
    fill(1, wq_s, part_g, 1 - p.c)
    next(rg)
    fill(0, wo_s, part_o, 1 - p.c)
    next(ro)
    fill(1, wq_s, part_g, p.c)
    next(rg)
    fill(0, wo_s, part_o, p.c)
    next(ro)
    next(rg)
    next(ro)
    next(rg)
    next(ro)
    next(rg)
    next(ro, None)
    next(rg, None)
    res[1] = pltpu.roll(sum_o[...], 63, 0).astype(BF16)
    w.finish()


def per_device(
    hidden, cotangent, neighbour_ids, neighbour_lengths, embed_table,
    enc_up, enc_down, w_query, w_keyval, w_out,
):
    blk = (256, 256)
    row = (64, 896)
    bf = lambda *s: pltpu.VMEM(s, BF16)
    vm = pl.BlockSpec(memory_space=pltpu.VMEM)
    messages = 145
    res = pl.pallas_call(
        body,
        out_shape=jax.ShapeDtypeStruct((2,) + blk, BF16),
        in_specs=[vm] * 5
        + [pl.BlockSpec(memory_space=pl.ANY), vm, pl.BlockSpec(memory_space=pltpu.SMEM), vm, vm],
        out_specs=vm,
        scratch_shapes=[
            bf(4096, 896), pltpu.VMEM((8, 128, 128), jnp.int32), bf(512, 4096),
            bf(8, 2, *row), bf(8, *row), bf(8, *row), bf(7, *row), bf(*row), bf(4, *row),
            bf(256, 896),
            bf(4, 224, 896), bf(4, 224, 896), bf(4, 256, 224), bf(4, *row),
            bf(6, 32, 896), bf(*row), bf(16, *row),
            bf(16, *blk), bf(16, *blk), bf(16, *blk), bf(16, *blk), bf(16, 56, 512),
            bf(896, 512), pltpu.VMEM((896, 512), F32), bf(4, 256, 512),
            bf(*blk), bf(*blk), bf(2, 64, 256), bf(2, 64, 256), bf(2, *blk), bf(2, 64, 256),
            bf(8, 2, *blk), bf(8, 2, *blk), bf(8, *blk), bf(8, *blk), bf(8, *blk), bf(8, *blk),
            bf(7, *blk), bf(4, *blk), bf(6, 128, 256), pltpu.VMEM(blk, F32),
            pltpu.SemaphoreType.DMA,
            pltpu.SemaphoreType.DMA((messages,)), pltpu.SemaphoreType.DMA((messages,)),
        ],
        compiler_params=pltpu.CompilerParams(
            collective_id=1, has_side_effects=True, vmem_limit_bytes=62 * 1024 * 1024
        ),
        name="block",
    )(
        hidden, cotangent, w_query.reshape(blk), w_out.reshape(blk),
        w_keyval.reshape(56, 512), embed_table, neighbour_ids.reshape(8, 128),
        neighbour_lengths.T, enc_up, enc_down,
    )
    return res[0], res[1]


def solution(mesh):
    return jax.shard_map(
        per_device,
        mesh=mesh,
        in_specs=(
            P("seq", "mp"),
            P("seq", "mp"),
            P("seq", None, None),
            P(),
            P("mp", None),
            P("mp", None),
            P("mp", None),
            P("seq", "mp", None),
            P("seq", "mp", None, None),
            P("seq", "mp", None),
        ),
        out_specs=(P("seq", "mp"), P("seq", "mp")),
        check_vma=False,
    )
```

```python
import functools

import jax
import jax.numpy as jnp
from jax import lax
from jax.experimental import pallas as pl
from jax.experimental.pallas import tpu as pltpu
from jax.sharding import PartitionSpec as P

MESH = pl.DeviceIdType.MESH
F32 = jnp.float32
BF16 = jnp.bfloat16


class Place:
    def __init__(self):
        s = lax.axis_index("seq")
        m = lax.axis_index("mp")
        self.s, self.m = s, m
        self.x, self.zh = s // 4, s % 4
        self.y, self.zl, self.c = m // 4, (m // 2) % 2, m % 2
        self.sib = (s, self.mp(0, self.zl, 1 - self.c))
        self.zn = (s, self.mp(0, 1 - self.zl, self.c))
        self.zo = (self.seq(0, 2 * self.zl + 3), self.mp(0, 1 - self.zl, self.c))
        self.yp = (s, self.mp(1, self.zl, self.c))
        self.ym = (s, self.mp(3, self.zl, self.c))
        self.zp = (self.seq(0, 1), m)
        self.zm = (self.seq(0, 3), m)
        self.xp = (self.seq(1, 0), m)
        self.xm = (self.seq(3, 0), m)
        self.nxt = ((s + 1) % 16, m)
        self.prv = ((s + 15) % 16, m)

    def mp(self, dy, zl, c):
        return (((self.y + dy) % 4) * 2 + zl) * 2 + c

    def pair(self, dy, zl):
        return ((self.y + dy) % 4) * 2 + zl

    def seq(self, dx, dz):
        return ((self.x + dx) % 4) * 4 + (self.zh + dz) % 4


class Wire:
    def __init__(self, send_sem, recv_sem):
        self.send_sem, self.recv_sem = send_sem, recv_sem
        self.count = 0
        self.groups = []
        self.open = []

    def slot(self):
        self.count += 1
        return self.count - 1

    def wait(self, k, landing, frm):
        pltpu.make_async_remote_copy(
            src_ref=landing,
            dst_ref=landing,
            send_sem=self.send_sem.at[0],
            recv_sem=self.recv_sem.at[k],
            device_id=frm,
            device_id_type=MESH,
        ).wait_recv()

    def group(self, total):
        return Group(self, total)

    def finish(self):
        for group in list(self.open):
            group.flush()


class Group:
    def __init__(self, wire, total):
        self.wire, self.total = wire, total
        self.sem = wire.send_sem.at[len(wire.groups)]
        wire.groups.append(self)
        wire.open.append(self)

    def send(self, src, dst, to, k=None):
        k = self.wire.slot() if k is None else k
        self.to = to
        pltpu.make_async_remote_copy(
            src_ref=src,
            dst_ref=dst,
            send_sem=self.sem,
            recv_sem=self.wire.recv_sem.at[k],
            device_id=to,
            device_id_type=MESH,
        ).start()
        return k

    def flush(self):
        self.wire.open.remove(self)
        pltpu.make_async_remote_copy(
            src_ref=self.total,
            dst_ref=self.total,
            send_sem=self.sem,
            recv_sem=self.wire.recv_sem.at[0],
            device_id=self.to,
            device_id_type=MESH,
        ).wait_send()


def greet(peers):
    barrier = pltpu.get_barrier_semaphore()
    for peer in peers:
        pl.semaphore_signal(barrier, inc=1, device_id=peer, device_id_type=MESH)
    pl.semaphore_wait(barrier, len(peers))


def gather_mp(w, p, shard, out, flip=False):
    n = w.group(out.at[pl.ds(0, 15)])
    ks = w.slot()
    mine = p.mp(0, p.zl, p.c)
    o = 1 - p.zl
    fore, back, f, b3 = (p.ym, p.yp, 3, 1) if flip else (p.yp, p.ym, 1, 3)
    at = lambda dy, zl, c: out.at[p.mp(dy, zl, c)]
    own = out.at[mine]
    k_y1 = n.send(shard, own, fore)
    k_y2 = n.send(shard, own, back)
    k_z = n.send(shard, own, p.zn)
    n.send(shard, own, p.sib, ks)
    out[mine] = shard[...]
    yield
    w.wait(k_z, at(0, o, p.c), p.zn)
    zb = at(0, o, p.c)
    k_z1 = n.send(zb, zb, fore)
    k_z2 = n.send(zb, zb, back)
    n.send(zb, zb, p.sib, ks)
    yield
    b = at(b3, p.zl, p.c)
    w.wait(k_y1, b, back)
    k_f1 = n.send(b, b, fore)
    n.send(b, b, p.sib, ks)
    b = at(f, p.zl, p.c)
    w.wait(k_y2, b, fore)
    n.send(b, b, p.sib, ks)
    yield
    b = at(f, o, p.c)
    w.wait(k_z2, b, fore)
    k_f2 = n.send(b, b, back)
    n.send(b, b, p.sib, ks)
    b = at(b3, o, p.c)
    w.wait(k_z1, b, back)
    n.send(b, b, p.sib, ks)
    yield
    b = at(2, p.zl, p.c)
    w.wait(k_f1, b, back)
    n.send(b, b, p.sib, ks)
    b = at(2, o, p.c)
    w.wait(k_f2, b, fore)
    n.send(b, b, p.sib, ks)
    yield
    w.wait(ks, out.at[pl.ds(0, 8)], p.sib)


def scatter_mp(w, p, n, part, sibl, acc, land, result, late):
    o = 1 - p.zl
    ks = {}

    def share(dy):
        row = ((p.y + dy) % 4) * 2
        ks[dy] = n.send(
            part.at[pl.ds(row, 2), 1 - p.c], sibl.at[pl.ds(row, 2)], p.sib
        )

    def combine(dy):
        row = ((p.y + dy) % 4) * 2
        w.wait(ks[dy], sibl.at[pl.ds(row, 2)], p.sib)
        for zl in (0, 1):
            acc[row + zl] = (
                part[row + zl, p.c].astype(F32) + sibl[row + zl].astype(F32)
            ).astype(BF16)

    for dy in (2, 1, 3) if late else (2, 1, 3, 0):
        share(dy)
    yield
    combine(2)
    k0 = n.send(acc.at[p.pair(2, p.zl)], land.at[0], p.yp)
    k1 = n.send(acc.at[p.pair(2, o)], land.at[1], p.ym)
    combine(1)
    k2b = n.send(acc.at[p.pair(1, o)], land.at[2], p.yp)
    combine(3)
    k3a = n.send(acc.at[p.pair(3, p.zl)], land.at[3], p.ym)
    yield
    if late:
        share(0)
        yield
    w.wait(k0, land.at[0], p.ym)
    i = p.pair(1, p.zl)
    acc[i] = (acc[i].astype(F32) + land[0].astype(F32)).astype(BF16)
    k2a = n.send(acc.at[i], land.at[4], p.yp)
    w.wait(k1, land.at[1], p.yp)
    i = p.pair(3, o)
    acc[i] = (acc[i].astype(F32) + land[1].astype(F32)).astype(BF16)
    k3b = n.send(acc.at[i], land.at[5], p.ym)
    combine(0)
    yield
    w.wait(k2b, land.at[2], p.ym)
    w.wait(k3b, land.at[5], p.yp)
    i = p.pair(0, o)
    acc[i] = (acc[i].astype(F32) + land[2].astype(F32) + land[5].astype(F32)).astype(BF16)
    kz = n.send(acc.at[i], land.at[6], p.zn)
    yield
    w.wait(k3a, land.at[3], p.yp)
    w.wait(k2a, land.at[4], p.ym)
    w.wait(kz, land.at[6], p.zn)
    result(
        acc[p.pair(0, p.zl)].astype(F32)
        + land[3].astype(F32)
        + land[4].astype(F32)
        + land[6].astype(F32)
    )


def drain(gens):
    gens = list(gens)
    while gens:
        gens = [g for g in gens if next(g, True) is None]


def gather_seq(w, p, shard, out, up, late):
    n = w.group(out.at[pl.ds(0, 15)])
    k_last = w.slot()
    mine = p.seq(0, 0)
    at = lambda dx, dz: out.at[p.seq(dx, dz)]
    own = out.at[mine]
    kx = {0: (n.send(shard, own, p.xp), n.send(shard, own, p.xm))}
    out[mine] = shard[...]

    def spread(dz):
        b = at(0, dz)
        kx[dz] = (n.send(b, b, p.xp), n.send(b, b, p.xm))

    def relay(dz, upward):
        k1, k2 = kx[dz]
        if upward:
            b = at(3, dz)
            w.wait(k1, b, p.xm)
            n.send(b, b, p.xp, k_last)
            w.wait(k2, at(1, dz), p.xp)
        else:
            b = at(1, dz)
            w.wait(k2, b, p.xp)
            n.send(b, b, p.xm, k_last)
            w.wait(k1, at(3, dz), p.xm)

    yield
    if late:
        relay(0, up)
        yield
    k_zp = n.send(shard, own, p.zp)
    k_zm = n.send(shard, own, p.zm)
    yield
    if not late:
        relay(0, up)
        yield
    if up:
        b = at(0, 3)
        w.wait(k_zp, b, p.zm)
        k_zf = n.send(b, b, p.zp)
        spread(3)
        w.wait(k_zm, at(0, 1), p.zp)
        spread(1)
    else:
        b = at(0, 1)
        w.wait(k_zm, b, p.zp)
        k_zf = n.send(b, b, p.zm)
        spread(1)
        w.wait(k_zp, at(0, 3), p.zm)
        spread(3)
    yield
    w.wait(k_zf, at(0, 2), p.zm if up else p.zp)
    spread(2)
    yield
    relay(3 if up else 1, up)
    yield
    relay(1 if up else 3, not up)
    yield
    relay(2, not up)
    yield
    w.wait(k_last, out.at[pl.ds(0, 4)], p.xm)


def gather_pair(w, p, shard, out, other):
    n = w.group(out.at[pl.ds(0, 3)])
    o, oc = 1 - p.zl, 1 - p.c
    mine = p.zl * 2 + p.c
    k_z = n.send(shard, out.at[mine], other)
    k_s = n.send(shard, out.at[mine], p.sib)
    out[mine] = shard[...]
    yield
    b = out.at[o * 2 + p.c]
    w.wait(k_z, b, other)
    k_zs = n.send(b, b, p.sib)
    yield
    w.wait(k_s, out.at[p.zl * 2 + oc], p.sib)
    w.wait(k_zs, out.at[o * 2 + oc], p.sib)


def gather_y(w, p, shard, out):
    n = w.group(out.at[pl.ds(0, 3)])
    rows = shard.shape[0] // 2
    lo, hi = pl.ds(0, rows), pl.ds(rows, rows)
    at = lambda dy: (p.y + dy) % 4
    own = out.at[at(0)]
    k1 = n.send(shard, own, p.yp)
    k2 = n.send(shard, own, p.ym)
    out[at(0)] = shard[...]
    yield
    w.wait(k1, out.at[at(3)], p.ym)
    b = out.at[at(3), lo]
    f1 = n.send(b, b, p.yp)
    w.wait(k2, out.at[at(1)], p.yp)
    b = out.at[at(1), hi]
    f2 = n.send(b, b, p.ym)
    yield
    w.wait(f1, out.at[at(2), lo], p.ym)
    w.wait(f2, out.at[at(2), hi], p.yp)


def scatter_y(w, p, n, blk, index, ready, land, result):
    rows = blk.shape[1] // 2
    lo, hi = pl.ds(0, rows), pl.ds(rows, rows)
    i0, i1, i2, i3 = index(0), index(1), index(2), index(3)
    ready(2)
    k0 = n.send(blk.at[i2, lo], land.at[0], p.yp)
    k1 = n.send(blk.at[i2, hi], land.at[1], p.ym)
    yield
    ready(1)
    k2b = n.send(blk.at[i1, hi], land.at[2], p.yp)
    ready(3)
    k3a = n.send(blk.at[i3, lo], land.at[3], p.ym)
    yield
    w.wait(k0, land.at[0], p.ym)
    blk[i1, lo, :] = (blk[i1, lo, :].astype(F32) + land[0].astype(F32)).astype(BF16)
    k2a = n.send(blk.at[i1, lo], land.at[4], p.yp)
    w.wait(k1, land.at[1], p.yp)
    blk[i3, hi, :] = (blk[i3, hi, :].astype(F32) + land[1].astype(F32)).astype(BF16)
    k3b = n.send(blk.at[i3, hi], land.at[5], p.ym)
    yield
    ready(0)
    w.wait(k2b, land.at[2], p.ym)
    w.wait(k3a, land.at[3], p.yp)
    w.wait(k2a, land.at[4], p.ym)
    w.wait(k3b, land.at[5], p.yp)
    f = lambda v: v.astype(F32)
    result(lo, f(blk[i0, lo, :]) + f(land[4]) + f(land[3]))
    result(hi, f(blk[i0, hi, :]) + f(land[2]) + f(land[5]))


def scatter_zy(w, p, n, part, sibl, acc, zland, land, result):
    o = 1 - p.zl
    ks, kz = {}, {}
    for dy in (2, 1, 3, 0):
        row = ((p.y + dy) % 4) * 2
        ks[dy] = n.send(
            part.at[pl.ds(row, 2), 1 - p.c], sibl.at[pl.ds(row, 2)], p.sib
        )
    yield
    for dy in (2, 1, 3, 0):
        row = ((p.y + dy) % 4) * 2
        w.wait(ks[dy], sibl.at[pl.ds(row, 2)], p.sib)
        for zl in (o, p.zl):
            acc[row + zl] = (
                part[row + zl, p.c].astype(F32) + sibl[row + zl].astype(F32)
            ).astype(BF16)
        kz[dy] = n.send(acc.at[row + o], zland.at[dy], p.zn)
    yield

    def ready(dy):
        w.wait(kz[dy], zland.at[dy], p.zn)
        i = p.pair(dy, p.zl)
        acc[i] = (acc[i].astype(F32) + zland[dy].astype(F32)).astype(BF16)

    yield from scatter_y(w, p, n, acc, lambda dy: p.pair(dy, p.zl), ready, land, result)


NT = (((1,), (1,)), ((), ()))


def body(
    hid, cot, wq, wo, wkv, table, ids, lens, up, down,
    res,
    tab, idsb, onehot, epart, esib, eacc, eland, emb_own, emb4, normed,
    up4, down4, acts, fblk, fland, enc_own, enc,
    hid_s, cot_s, wq_s, wo_s, wkv_s, wkv_w, wkv_f, kv_s,
    q_s, d_s, q_land, last, a_s, a_land,
    part_o, part_g, sib_o, sib_g, acc_o, acc_g, land_o, zland_g, land_g, sum_o, prob_s,
    tab_sem, send_sem, recv_sem,
):
    p = Place()
    w = Wire(send_sem, recv_sem)
    fetch = pltpu.make_async_copy(table, tab.at[pl.ds(0, 4000)], tab_sem)
    fetch.start()
    greet((p.sib, p.zn, p.zo, p.yp, p.ym, p.zp, p.zm, p.xp, p.xm, p.nxt, p.prv))

    gh = gather_mp(w, p, hid, hid_s)
    gc = gather_mp(w, p, cot, cot_s, True)
    gu = gather_pair(w, p, up, up4, p.zo)
    lo, hi = pl.ds(0, 112), pl.ds(112, 112)
    gd = gather_pair(w, p, down.at[lo], down4.at[:, lo], p.zo)
    ge = gather_pair(w, p, down.at[hi], down4.at[:, hi], p.zn)
    gq = gather_seq(w, p, wq, wq_s, True, False)
    gk = gather_seq(w, p, wkv, wkv_s, True, False)
    go = gather_seq(w, p, wo, wo_s, False, True)
    next(gh), next(gc), next(gu)
    next(gq), next(gq)
    next(gk), next(gk)
    next(gd), next(ge), next(go)

    tab[pl.ds(4000, 96), :] = jnp.zeros((96, 896), BF16)
    cols = jnp.transpose(ids[...] - p.m * 4000)
    for r in range(8):
        idsb[r] = jnp.broadcast_to(cols[:, r : r + 1], (128, 128))
    lane = lax.broadcasted_iota(jnp.int32, (64, 128), 1)

    def lookup(c, ys):
        pairs = [p.pair(dy, zl) for dy in ys for zl in (0, 1)]
        high = len(pairs) * 64
        for i, r in enumerate(pairs):
            mine = idsb[r, pl.ds(pl.multiple_of(c * 64, 64), 64), :] - lane
            for k in range(32):
                onehot[i * 64 : (i + 1) * 64, k * 128 : (k + 1) * 128] = jnp.where(
                    mine == k * 128, 1.0, 0.0
                ).astype(BF16)

        def pick(cols_at):
            got = jnp.dot(onehot[0:high, :], tab[:, cols_at], preferred_element_type=F32)
            for i, r in enumerate(pairs):
                epart[r, c, :, cols_at] = got[i * 64 : (i + 1) * 64].astype(BF16)

        for at in (0, 256, 512, 768):
            pick(slice(at, min(at + 256, 896)))

    def keep_emb(total):
        emb_own[...] = total.astype(BF16)

    far = (2, 1, 3)
    fetch.wait()
    lookup(1 - p.c, far)
    ers = scatter_mp(
        w, p, w.group(enc.at[pl.ds(0, 15)]), epart, esib, eacc, eland, keep_emb, True
    )
    next(ers)
    lookup(p.c, far)
    next(ers)
    lookup(1 - p.c, (0,))
    next(ers)
    lookup(p.c, (0,))
    next(ers)
    next(gh), next(gc)
    next(gq), next(gk), next(go)
    next(gu)
    next(ers)
    next(gq), next(gk)
    next(go)
    next(ers, None)
    ey = gather_y(w, p, emb_own, emb4)
    next(ey)
    next(ey)
    next(ey, None)
    next(gu, None)
    next(gq), next(gk)

    e = emb4[...].reshape(256, 896).astype(F32)
    normed[...] = (
        e * lax.rsqrt(jnp.mean(e * e, axis=-1, keepdims=True) + 1e-06)
    ).astype(BF16)
    for j in range(4):
        acts[j] = jax.nn.gelu(
            lax.dot_general(normed[...], up4[j], NT, preferred_element_type=F32)
        ).astype(BF16)
    next(gd), next(ge)
    next(gq), next(gk)
    next(gd, None), next(ge, None)
    total = jnp.dot(acts[0], down4[0], preferred_element_type=F32)
    for j in range(1, 4):
        total = total + jnp.dot(acts[j], down4[j], preferred_element_type=F32)
    for y in range(4):
        fblk[y] = total[y * 64 : (y + 1) * 64, :].astype(BF16)

    def keep_enc(rows, total):
        v = emb_own[rows, :].astype(F32) + total
        v = v * lax.rsqrt(jnp.mean(v * v, axis=-1, keepdims=True) + 1e-06)
        enc_own[rows, :] = v.astype(BF16)

    fy = scatter_y(
        w, p, w.group(enc.at[pl.ds(0, 3)]), fblk, lambda dy: (p.y + dy) % 4, lambda dy: None, fland, keep_enc
    )
    next(fy)
    next(fy)
    next(gq), next(gk)
    next(go)
    next(fy)
    next(gh), next(gh)
    next(gq), next(gk)
    next(fy, None)
    ga = gather_mp(w, p, enc_own, enc)
    next(ga)
    next(go)
    next(ga)
    next(go)
    next(ga)
    next(ga)
    next(gc), next(gc)
    next(go)
    drain([gq, gk])
    for i in range(16):
        wkv_f[pl.ds(56 * i, 56), :] = wkv_s[i].astype(F32)
    wkv_w[...] = wkv_f[...].astype(BF16)
    next(gh)
    next(ga)
    next(go)
    next(gh, None)

    def project(src, weights, sums, columns, start):
        total = None if start else sums[...]
        for dx in columns:
            for dz in range(4):
                b = p.seq(dx, dz)
                got = jnp.dot(src[b], weights[b], preferred_element_type=F32)
                total = got if total is None else total + got
        sums[...] = total

    project(hid_s, wq_s, sum_o, (0, 1, 2, 3), True)
    q_s[...] = pltpu.roll(sum_o[...], 193, 0).astype(BF16)
    next(gc), next(gc, None)
    swap = w.group(q_land)
    kq = swap.send(q_s.at[pl.ds(192, 64)], q_land.at[0], p.prv)
    project(cot_s, wo_s, sum_o, (0,), True)
    drain([go])
    project(cot_s, wo_s, sum_o, (1, 3, 2), False)
    d_s[...] = pltpu.roll(sum_o[...], 193, 0).astype(BF16)
    kd = swap.send(d_s.at[pl.ds(192, 64)], q_land.at[1], p.prv)
    next(ga, None)

    def keyval(g):
        rows = enc[g * 4 : g * 4 + 4].reshape(256, 896)
        kv_s[g] = jnp.dot(rows, wkv_w[...], preferred_element_type=F32).astype(BF16)

    first = lax.broadcasted_iota(jnp.int32, (64, 256), 0) == 0
    tail = pl.ds(192, 64)
    key = lax.broadcasted_iota(jnp.int32, (64, 256), 1)
    scale = 128 ** (-0.5)

    def swapped(i, src):
        last[i] = jnp.where(
            first, src[tail, :].astype(F32), q_land[i].astype(F32)
        ).astype(BF16)

    def heads(spans):
        return [
            (g, h, slice(g * 64, (g + 1) * 64), slice(h * 128, (h + 1) * 128))
            for g in spans
            for h in range(2)
        ]

    def keys_of(g, h):
        return kv_s[g, :, h * 256 : h * 256 + 128]

    def values_of(g, h):
        return kv_s[g, :, h * 256 + 128 : (h + 1) * 256]

    def attend(spans):
        jobs = heads(spans)
        score = [
            lax.dot_general(
                last[0, :, head] if g == 3 else q_s[rows, head], keys_of(g, h), NT,
                preferred_element_type=F32,
            )
            for g, h, rows, head in jobs
        ]
        expo = []
        for (g, _, _, _), x in zip(jobs, score):
            span = p.s * 4 + g
            live = key < jnp.where(key < 128, lens[0, span], lens[1, span] + 128)
            expo.append(jnp.where(live, jnp.exp(x * scale), 0.0))
        prob = [x / jnp.sum(x, axis=-1, keepdims=True) for x in expo]
        attn = [
            jnp.dot(x.astype(BF16), values_of(g, h), preferred_element_type=F32)
            for (g, h, _, _), x in zip(jobs, prob)
        ]
        for (g, h, rows, head), x, y in zip(jobs, prob, attn):
            prob_s[g * 2 + h] = x
            a_s[0, rows, head] = y.astype(BF16)

    def differentiate(spans):
        jobs = heads(spans)
        d_prob = [
            lax.dot_general(
                last[1, :, head] if g == 3 else d_s[rows, head], values_of(g, h), NT,
                preferred_element_type=F32,
            )
            for g, h, rows, head in jobs
        ]
        prob = [prob_s[g * 2 + h] for g, h, _, _ in jobs]
        delta = [jnp.sum(x * y, axis=-1, keepdims=True) for x, y in zip(prob, d_prob)]
        d_score = [
            (x * (y - z) * scale).astype(BF16) for x, y, z in zip(prob, d_prob, delta)
        ]
        d_query = [
            jnp.dot(x, keys_of(g, h), preferred_element_type=F32)
            for (g, h, _, _), x in zip(jobs, d_score)
        ]
        for (_, _, rows, head), y in zip(jobs, d_query):
            a_s[1, rows, head] = y.astype(BF16)

    def give_back(i):
        back = w.group(a_land.at[i])
        return back, back.send(a_s.at[i, tail], a_land.at[i], p.nxt)

    def take_back(i, back, k):
        w.wait(k, a_land.at[i], p.prv)
        back.flush()
        got = jnp.where(p.s > 0, a_land[i].astype(F32), 0.0)
        a_s[i, tail, :] = jnp.where(first, a_s[i, tail, :].astype(F32), got).astype(BF16)

    keyval(3)
    w.wait(kq, q_land.at[0], p.nxt)
    swapped(0, q_s)
    attend((3,))
    back_o = give_back(0)
    for g in range(3):
        keyval(g)
    attend((0, 1, 2))
    w.wait(kd, q_land.at[1], p.nxt)
    swapped(1, d_s)
    differentiate((3,))
    back_g = give_back(1)
    differentiate((0, 1, 2))

    def fill(i, weights, part, c):
        for b in range(8):
            part[b, c] = lax.dot_general(
                a_s[i], weights[b * 2 + c], NT, preferred_element_type=F32
            ).astype(BF16)

    def keep_out(total):
        res[0] = pltpu.roll(total, 63, 0).astype(BF16)

    def keep_grad(rows, total):
        sum_o[rows, :] = total

    blocks = pl.ds(0, 15)
    ro = scatter_mp(
        w, p, w.group(wo_s.at[blocks]), part_o, sib_o, acc_o, land_o, keep_out, False
    )
    rg = scatter_zy(
        w, p, w.group(wq_s.at[blocks]), part_g, sib_g, acc_g, zland_g, land_g, keep_grad
    )
    take_back(0, *back_o)
    fill(0, wo_s, part_o, 1 - p.c)
    next(ro)
    fill(0, wo_s, part_o, p.c)
    next(ro)
    take_back(1, *back_g)
    fill(1, wq_s, part_g, 1 - p.c)
    next(rg)
    fill(1, wq_s, part_g, p.c)
    next(rg)
    next(rg)
    next(ro)
    next(rg)
    next(ro)
    next(rg)
    next(ro, None)
    next(rg, None)
    res[1] = pltpu.roll(sum_o[...], 63, 0).astype(BF16)
    w.finish()


def per_device(
    hidden, cotangent, neighbour_ids, neighbour_lengths, embed_table,
    enc_up, enc_down, w_query, w_keyval, w_out,
):
    blk = (256, 256)
    row = (64, 896)
    bf = lambda *s: pltpu.VMEM(s, BF16)
    vm = pl.BlockSpec(memory_space=pltpu.VMEM)
    messages, groups = 119, 17
    res = pl.pallas_call(
        body,
        out_shape=jax.ShapeDtypeStruct((2,) + blk, BF16),
        in_specs=[vm] * 5
        + [pl.BlockSpec(memory_space=pl.ANY), vm, pl.BlockSpec(memory_space=pltpu.SMEM), vm, vm],
        out_specs=vm,
        scratch_shapes=[
            bf(4096, 896), pltpu.VMEM((8, 128, 128), jnp.int32), bf(512, 4096),
            bf(8, 2, *row), bf(8, *row), bf(8, *row), bf(7, *row), bf(*row), bf(4, *row),
            bf(256, 896),
            bf(4, 224, 896), bf(4, 224, 896), bf(4, 256, 224), bf(4, *row),
            bf(6, 32, 896), bf(*row), bf(16, *row),
            bf(16, *blk), bf(16, *blk), bf(16, *blk), bf(16, *blk), bf(16, 56, 512),
            bf(896, 512), pltpu.VMEM((896, 512), F32), bf(4, 256, 512),
            bf(*blk), bf(*blk), bf(2, 64, 256), bf(2, 64, 256), bf(2, *blk), bf(2, 64, 256),
            bf(8, 2, *blk), bf(8, 2, *blk), bf(8, *blk), bf(8, *blk), bf(8, *blk), bf(8, *blk),
            bf(7, *blk), bf(4, *blk), bf(6, 128, 256), pltpu.VMEM(blk, F32), pltpu.VMEM((8, 64, 256), F32),
            pltpu.SemaphoreType.DMA,
            pltpu.SemaphoreType.DMA((groups,)), pltpu.SemaphoreType.DMA((messages,)),
        ],
        compiler_params=pltpu.CompilerParams(
            collective_id=1, has_side_effects=True, vmem_limit_bytes=62 * 1024 * 1024
        ),
        name="block",
    )(
        hidden, cotangent, w_query.reshape(blk), w_out.reshape(blk),
        w_keyval.reshape(56, 512), embed_table, neighbour_ids.reshape(8, 128),
        neighbour_lengths.T, enc_up, enc_down,
    )
    return res[0], res[1]


def solution(mesh):
    return jax.shard_map(
        per_device,
        mesh=mesh,
        in_specs=(
            P("seq", "mp"),
            P("seq", "mp"),
            P("seq", None, None),
            P(),
            P("mp", None),
            P("mp", None),
            P("mp", None),
            P("seq", "mp", None),
            P("seq", "mp", None, None),
            P("seq", "mp", None),
        ),
        out_specs=(P("seq", "mp"), P("seq", "mp")),
        check_vma=False,
    )
```

```python
import functools

import jax
import jax.numpy as jnp
from jax import lax
from jax.experimental import pallas as pl
from jax.experimental.pallas import tpu as pltpu
from jax.sharding import PartitionSpec as P

MESH = pl.DeviceIdType.MESH
F32 = jnp.float32
BF16 = jnp.bfloat16


class Place:
    def __init__(self):
        s = lax.axis_index("seq")
        m = lax.axis_index("mp")
        self.s, self.m = s, m
        self.x, self.zh = s // 4, s % 4
        self.y, self.zl, self.c = m // 4, (m // 2) % 2, m % 2
        self.sib = (s, self.mp(0, self.zl, 1 - self.c))
        self.zn = (s, self.mp(0, 1 - self.zl, self.c))
        self.zo = (self.seq(0, 2 * self.zl + 3), self.mp(0, 1 - self.zl, self.c))
        self.yp = (s, self.mp(1, self.zl, self.c))
        self.ym = (s, self.mp(3, self.zl, self.c))
        self.zp = (self.seq(0, 1), m)
        self.zm = (self.seq(0, 3), m)
        self.xp = (self.seq(1, 0), m)
        self.xm = (self.seq(3, 0), m)
        self.nxt = ((s + 1) % 16, m)
        self.prv = ((s + 15) % 16, m)

    def mp(self, dy, zl, c):
        return (((self.y + dy) % 4) * 2 + zl) * 2 + c

    def pair(self, dy, zl):
        return ((self.y + dy) % 4) * 2 + zl

    def seq(self, dx, dz):
        return ((self.x + dx) % 4) * 4 + (self.zh + dz) % 4


class Wire:
    def __init__(self, send_sem, recv_sem):
        self.send_sem, self.recv_sem = send_sem, recv_sem
        self.count = 0
        self.groups = []
        self.open = []

    def slot(self):
        self.count += 1
        return self.count - 1

    def wait(self, k, landing, frm):
        pltpu.make_async_remote_copy(
            src_ref=landing,
            dst_ref=landing,
            send_sem=self.send_sem.at[0],
            recv_sem=self.recv_sem.at[k],
            device_id=frm,
            device_id_type=MESH,
        ).wait_recv()

    def group(self, total):
        return Group(self, total)

    def finish(self):
        for group in list(self.open):
            group.flush()


class Group:
    def __init__(self, wire, total):
        self.wire, self.total = wire, total
        self.sem = wire.send_sem.at[len(wire.groups)]
        wire.groups.append(self)
        wire.open.append(self)

    def send(self, src, dst, to, k=None):
        k = self.wire.slot() if k is None else k
        self.to = to
        pltpu.make_async_remote_copy(
            src_ref=src,
            dst_ref=dst,
            send_sem=self.sem,
            recv_sem=self.wire.recv_sem.at[k],
            device_id=to,
            device_id_type=MESH,
        ).start()
        return k

    def flush(self):
        self.wire.open.remove(self)
        pltpu.make_async_remote_copy(
            src_ref=self.total,
            dst_ref=self.total,
            send_sem=self.sem,
            recv_sem=self.wire.recv_sem.at[0],
            device_id=self.to,
            device_id_type=MESH,
        ).wait_send()


def greet(peers):
    barrier = pltpu.get_barrier_semaphore()
    for peer in peers:
        pl.semaphore_signal(barrier, inc=1, device_id=peer, device_id_type=MESH)
    pl.semaphore_wait(barrier, len(peers))


def gather_mp(w, p, shard, out, flip=False):
    n = w.group(out.at[pl.ds(0, 15)])
    ks = w.slot()
    mine = p.mp(0, p.zl, p.c)
    o = 1 - p.zl
    fore, back, f, b3 = (p.ym, p.yp, 3, 1) if flip else (p.yp, p.ym, 1, 3)
    at = lambda dy, zl, c: out.at[p.mp(dy, zl, c)]
    own = out.at[mine]
    k_y1 = n.send(shard, own, fore)
    k_y2 = n.send(shard, own, back)
    k_z = n.send(shard, own, p.zn)
    n.send(shard, own, p.sib, ks)
    out[mine] = shard[...]
    yield
    w.wait(k_z, at(0, o, p.c), p.zn)
    zb = at(0, o, p.c)
    k_z1 = n.send(zb, zb, fore)
    k_z2 = n.send(zb, zb, back)
    n.send(zb, zb, p.sib, ks)
    yield
    b = at(b3, p.zl, p.c)
    w.wait(k_y1, b, back)
    k_f1 = n.send(b, b, fore)
    n.send(b, b, p.sib, ks)
    b = at(f, p.zl, p.c)
    w.wait(k_y2, b, fore)
    n.send(b, b, p.sib, ks)
    yield
    b = at(f, o, p.c)
    w.wait(k_z2, b, fore)
    k_f2 = n.send(b, b, back)
    n.send(b, b, p.sib, ks)
    b = at(b3, o, p.c)
    w.wait(k_z1, b, back)
    n.send(b, b, p.sib, ks)
    yield
    b = at(2, p.zl, p.c)
    w.wait(k_f1, b, back)
    n.send(b, b, p.sib, ks)
    b = at(2, o, p.c)
    w.wait(k_f2, b, fore)
    n.send(b, b, p.sib, ks)
    yield
    w.wait(ks, out.at[pl.ds(0, 8)], p.sib)


def scatter_mp(w, p, n, part, sibl, acc, land, result, late):
    o = 1 - p.zl
    ks = {}

    def share(dy):
        row = ((p.y + dy) % 4) * 2
        ks[dy] = n.send(
            part.at[pl.ds(row, 2), 1 - p.c], sibl.at[pl.ds(row, 2)], p.sib
        )

    def combine(dy):
        row = ((p.y + dy) % 4) * 2
        w.wait(ks[dy], sibl.at[pl.ds(row, 2)], p.sib)
        for zl in (0, 1):
            acc[row + zl] = (
                part[row + zl, p.c].astype(F32) + sibl[row + zl].astype(F32)
            ).astype(BF16)

    for dy in (2, 1, 3) if late else (2, 1, 3, 0):
        share(dy)
    yield
    combine(2)
    k0 = n.send(acc.at[p.pair(2, p.zl)], land.at[0], p.yp)
    k1 = n.send(acc.at[p.pair(2, o)], land.at[1], p.ym)
    combine(1)
    k2b = n.send(acc.at[p.pair(1, o)], land.at[2], p.yp)
    combine(3)
    k3a = n.send(acc.at[p.pair(3, p.zl)], land.at[3], p.ym)
    yield
    if late:
        share(0)
        yield
    w.wait(k0, land.at[0], p.ym)
    i = p.pair(1, p.zl)
    acc[i] = (acc[i].astype(F32) + land[0].astype(F32)).astype(BF16)
    k2a = n.send(acc.at[i], land.at[4], p.yp)
    w.wait(k1, land.at[1], p.yp)
    i = p.pair(3, o)
    acc[i] = (acc[i].astype(F32) + land[1].astype(F32)).astype(BF16)
    k3b = n.send(acc.at[i], land.at[5], p.ym)
    combine(0)
    yield
    w.wait(k2b, land.at[2], p.ym)
    w.wait(k3b, land.at[5], p.yp)
    i = p.pair(0, o)
    acc[i] = (acc[i].astype(F32) + land[2].astype(F32) + land[5].astype(F32)).astype(BF16)
    kz = n.send(acc.at[i], land.at[6], p.zn)
    yield
    w.wait(k3a, land.at[3], p.yp)
    w.wait(k2a, land.at[4], p.ym)
    w.wait(kz, land.at[6], p.zn)
    result(
        acc[p.pair(0, p.zl)].astype(F32)
        + land[3].astype(F32)
        + land[4].astype(F32)
        + land[6].astype(F32)
    )


def drain(gens):
    gens = list(gens)
    while gens:
        gens = [g for g in gens if next(g, True) is None]


def gather_seq(w, p, shard, out, up, late):
    n = w.group(out.at[pl.ds(0, 15)])
    k_last = w.slot()
    mine = p.seq(0, 0)
    at = lambda dx, dz: out.at[p.seq(dx, dz)]
    own = out.at[mine]
    kx = {0: (n.send(shard, own, p.xp), n.send(shard, own, p.xm))}
    out[mine] = shard[...]

    def spread(dz):
        b = at(0, dz)
        kx[dz] = (n.send(b, b, p.xp), n.send(b, b, p.xm))

    def relay(dz, upward):
        k1, k2 = kx[dz]
        if upward:
            b = at(3, dz)
            w.wait(k1, b, p.xm)
            n.send(b, b, p.xp, k_last)
            w.wait(k2, at(1, dz), p.xp)
        else:
            b = at(1, dz)
            w.wait(k2, b, p.xp)
            n.send(b, b, p.xm, k_last)
            w.wait(k1, at(3, dz), p.xm)

    yield
    if late:
        relay(0, up)
        yield
    k_zp = n.send(shard, own, p.zp)
    k_zm = n.send(shard, own, p.zm)
    yield
    if not late:
        relay(0, up)
        yield
    if up:
        b = at(0, 3)
        w.wait(k_zp, b, p.zm)
        k_zf = n.send(b, b, p.zp)
        spread(3)
        w.wait(k_zm, at(0, 1), p.zp)
        spread(1)
    else:
        b = at(0, 1)
        w.wait(k_zm, b, p.zp)
        k_zf = n.send(b, b, p.zm)
        spread(1)
        w.wait(k_zp, at(0, 3), p.zm)
        spread(3)
    yield
    w.wait(k_zf, at(0, 2), p.zm if up else p.zp)
    spread(2)
    yield
    relay(3 if up else 1, up)
    yield
    relay(1 if up else 3, not up)
    yield
    relay(2, not up)
    yield
    w.wait(k_last, out.at[pl.ds(0, 4)], p.xm)


def gather_pair(w, p, shard, out, other):
    n = w.group(out.at[pl.ds(0, 3)])
    o, oc = 1 - p.zl, 1 - p.c
    mine = p.zl * 2 + p.c
    k_z = n.send(shard, out.at[mine], other)
    k_s = n.send(shard, out.at[mine], p.sib)
    out[mine] = shard[...]
    yield
    b = out.at[o * 2 + p.c]
    w.wait(k_z, b, other)
    k_zs = n.send(b, b, p.sib)
    yield
    w.wait(k_s, out.at[p.zl * 2 + oc], p.sib)
    w.wait(k_zs, out.at[o * 2 + oc], p.sib)


def gather_y(w, p, shard, out):
    n = w.group(out.at[pl.ds(0, 3)])
    rows = shard.shape[0] // 2
    lo, hi = pl.ds(0, rows), pl.ds(rows, rows)
    at = lambda dy: (p.y + dy) % 4
    own = out.at[at(0)]
    k1 = n.send(shard, own, p.yp)
    k2 = n.send(shard, own, p.ym)
    out[at(0)] = shard[...]
    yield
    w.wait(k1, out.at[at(3)], p.ym)
    b = out.at[at(3), lo]
    f1 = n.send(b, b, p.yp)
    w.wait(k2, out.at[at(1)], p.yp)
    b = out.at[at(1), hi]
    f2 = n.send(b, b, p.ym)
    yield
    w.wait(f1, out.at[at(2), lo], p.ym)
    w.wait(f2, out.at[at(2), hi], p.yp)


def scatter_y(w, p, n, blk, index, ready, land, result):
    rows = blk.shape[1] // 2
    lo, hi = pl.ds(0, rows), pl.ds(rows, rows)
    i0, i1, i2, i3 = index(0), index(1), index(2), index(3)
    ready(2)
    k0 = n.send(blk.at[i2, lo], land.at[0], p.yp)
    k1 = n.send(blk.at[i2, hi], land.at[1], p.ym)
    yield
    ready(1)
    k2b = n.send(blk.at[i1, hi], land.at[2], p.yp)
    ready(3)
    k3a = n.send(blk.at[i3, lo], land.at[3], p.ym)
    yield
    w.wait(k0, land.at[0], p.ym)
    blk[i1, lo, :] = (blk[i1, lo, :].astype(F32) + land[0].astype(F32)).astype(BF16)
    k2a = n.send(blk.at[i1, lo], land.at[4], p.yp)
    w.wait(k1, land.at[1], p.yp)
    blk[i3, hi, :] = (blk[i3, hi, :].astype(F32) + land[1].astype(F32)).astype(BF16)
    k3b = n.send(blk.at[i3, hi], land.at[5], p.ym)
    yield
    ready(0)
    w.wait(k2b, land.at[2], p.ym)
    w.wait(k3a, land.at[3], p.yp)
    w.wait(k2a, land.at[4], p.ym)
    w.wait(k3b, land.at[5], p.yp)
    f = lambda v: v.astype(F32)
    result(lo, f(blk[i0, lo, :]) + f(land[4]) + f(land[3]))
    result(hi, f(blk[i0, hi, :]) + f(land[2]) + f(land[5]))


def scatter_zy(w, p, n, part, sibl, acc, zland, land, result):
    o = 1 - p.zl
    ks, kz = {}, {}
    for dy in (2, 1, 3, 0):
        row = ((p.y + dy) % 4) * 2
        ks[dy] = n.send(
            part.at[pl.ds(row, 2), 1 - p.c], sibl.at[pl.ds(row, 2)], p.sib
        )
    yield
    for dy in (2, 1, 3, 0):
        row = ((p.y + dy) % 4) * 2
        w.wait(ks[dy], sibl.at[pl.ds(row, 2)], p.sib)
        for zl in (o, p.zl):
            acc[row + zl] = (
                part[row + zl, p.c].astype(F32) + sibl[row + zl].astype(F32)
            ).astype(BF16)
        kz[dy] = n.send(acc.at[row + o], zland.at[dy], p.zn)
    yield

    def ready(dy):
        w.wait(kz[dy], zland.at[dy], p.zn)
        i = p.pair(dy, p.zl)
        acc[i] = (acc[i].astype(F32) + zland[dy].astype(F32)).astype(BF16)

    yield from scatter_y(w, p, n, acc, lambda dy: p.pair(dy, p.zl), ready, land, result)


NT = (((1,), (1,)), ((), ()))


def body(
    hid, cot, wq, wo, wkv, table, ids, lens, up, down,
    res,
    tab, idsb, onehot, epart, esib, eacc, eland, emb_own, emb4, normed,
    up4, down4, acts, fblk, fland, enc_own, enc,
    hid_s, cot_s, wq_s, wo_s, wkv_s, wkv_w, wkv_f, kv_s,
    q_s, d_s, q_land, last, a_s, a_land,
    part_o, sib_o, acc_o, land_o, part_g, sib_g, acc_g, zland_g, land_g,
    part_t, sib_t, acc_t, land_t, sum_o, prob_s,
    tab_sem, send_sem, recv_sem,
):
    p = Place()
    w = Wire(send_sem, recv_sem)
    fetch = pltpu.make_async_copy(table, tab.at[pl.ds(0, 4000)], tab_sem)
    fetch.start()
    greet((p.sib, p.zn, p.zo, p.yp, p.ym, p.zp, p.zm, p.xp, p.xm, p.nxt, p.prv))

    gh = gather_mp(w, p, hid, hid_s)
    gc = gather_mp(w, p, cot, cot_s, True)
    gu = gather_pair(w, p, up, up4, p.zo)
    lo, hi = pl.ds(0, 112), pl.ds(112, 112)
    gd = gather_pair(w, p, down.at[lo], down4.at[:, lo], p.zo)
    ge = gather_pair(w, p, down.at[hi], down4.at[:, hi], p.zn)
    gq = gather_seq(w, p, wq, wq_s, True, False)
    gk = gather_seq(w, p, wkv, wkv_s, True, False)
    go = gather_seq(w, p, wo, wo_s, False, True)
    next(gh), next(gc), next(gu)
    next(gq), next(gq)
    next(gk), next(gk)
    next(gd), next(ge), next(go)

    tab[pl.ds(4000, 96), :] = jnp.zeros((96, 896), BF16)
    cols = jnp.transpose(ids[...] - p.m * 4000)
    for r in range(8):
        idsb[r] = jnp.broadcast_to(cols[:, r : r + 1], (128, 128))
    lane = lax.broadcasted_iota(jnp.int32, (64, 128), 1)

    def lookup(c, ys):
        pairs = [p.pair(dy, zl) for dy in ys for zl in (0, 1)]
        high = len(pairs) * 64
        for i, r in enumerate(pairs):
            mine = idsb[r, pl.ds(pl.multiple_of(c * 64, 64), 64), :] - lane
            for k in range(32):
                onehot[i * 64 : (i + 1) * 64, k * 128 : (k + 1) * 128] = jnp.where(
                    mine == k * 128, 1.0, 0.0
                ).astype(BF16)

        def pick(cols_at):
            got = jnp.dot(onehot[0:high, :], tab[:, cols_at], preferred_element_type=F32)
            for i, r in enumerate(pairs):
                epart[r, c, :, cols_at] = got[i * 64 : (i + 1) * 64].astype(BF16)

        for at in (0, 256, 512, 768):
            pick(slice(at, min(at + 256, 896)))

    def keep_emb(total):
        emb_own[...] = total.astype(BF16)

    far = (2, 1, 3)
    fetch.wait()
    lookup(1 - p.c, far)
    ers = scatter_mp(
        w, p, w.group(enc.at[pl.ds(0, 15)]), epart, esib, eacc, eland, keep_emb, True
    )
    next(ers)
    lookup(p.c, far)
    next(ers)
    lookup(1 - p.c, (0,))
    next(ers)
    lookup(p.c, (0,))
    next(ers)
    next(gh), next(gc)
    next(gq), next(gk), next(go)
    next(gu)
    next(ers)
    next(gq), next(gk)
    next(go)
    next(ers, None)
    ey = gather_y(w, p, emb_own, emb4)
    next(ey)
    next(ey)
    next(gh), next(gh)
    next(ey, None)
    next(gu, None)
    next(gq), next(gk)

    e = emb4[...].reshape(256, 896).astype(F32)
    normed[...] = (
        e * lax.rsqrt(jnp.mean(e * e, axis=-1, keepdims=True) + 1e-06)
    ).astype(BF16)
    for j in range(4):
        acts[j] = jax.nn.gelu(
            lax.dot_general(normed[...], up4[j], NT, preferred_element_type=F32)
        ).astype(BF16)
    next(gd), next(ge)
    next(gq), next(gk)
    next(gd, None), next(ge, None)
    total = jnp.dot(acts[0], down4[0], preferred_element_type=F32)
    for j in range(1, 4):
        total = total + jnp.dot(acts[j], down4[j], preferred_element_type=F32)
    for y in range(4):
        fblk[y] = total[y * 64 : (y + 1) * 64, :].astype(BF16)

    def keep_enc(rows, total):
        v = emb_own[rows, :].astype(F32) + total
        v = v * lax.rsqrt(jnp.mean(v * v, axis=-1, keepdims=True) + 1e-06)
        enc_own[rows, :] = v.astype(BF16)

    fy = scatter_y(
        w, p, w.group(enc.at[pl.ds(0, 3)]), fblk, lambda dy: (p.y + dy) % 4, lambda dy: None, fland, keep_enc
    )
    next(fy)
    next(fy)
    next(gq), next(gk)
    next(go)
    next(gh)
    next(fy)
    next(gc), next(gc)
    next(gq), next(gk)
    next(fy, None)
    ga = gather_mp(w, p, enc_own, enc)
    next(ga)
    next(go)
    next(gh, None)
    next(ga)
    next(go)
    next(ga)
    next(ga)
    next(gc)
    next(go)
    drain([gq, gk])
    for i in range(16):
        wkv_f[pl.ds(56 * i, 56), :] = wkv_s[i].astype(F32)
    wkv_w[...] = wkv_f[...].astype(BF16)

    def project(src, weights, sums, columns, start):
        total = None if start else sums[...]
        for dx in columns:
            for dz in range(4):
                b = p.seq(dx, dz)
                got = jnp.dot(src[b], weights[b], preferred_element_type=F32)
                total = got if total is None else total + got
        sums[...] = total

    next(go)
    project(hid_s, wq_s, sum_o, (0, 1, 2, 3), True)
    q_s[...] = pltpu.roll(sum_o[...], 193, 0).astype(BF16)
    swap = w.group(q_land)
    kq = swap.send(q_s.at[pl.ds(192, 64)], q_land.at[0], p.prv)
    next(ga)
    next(gc, None)
    project(cot_s, wo_s, sum_o, (0,), True)
    drain([go])
    project(cot_s, wo_s, sum_o, (1, 3, 2), False)
    d_s[...] = pltpu.roll(sum_o[...], 193, 0).astype(BF16)
    kd = swap.send(d_s.at[pl.ds(192, 64)], q_land.at[1], p.prv)
    next(ga, None)

    def keyval(g):
        rows = enc[g * 4 : g * 4 + 4].reshape(256, 896)
        kv_s[g] = jnp.dot(rows, wkv_w[...], preferred_element_type=F32).astype(BF16)

    first = lax.broadcasted_iota(jnp.int32, (64, 256), 0) == 0
    tail = pl.ds(192, 64)
    key = lax.broadcasted_iota(jnp.int32, (64, 256), 1)
    scale = 128 ** (-0.5)

    def swapped(i, src):
        last[i] = jnp.where(
            first, src[tail, :].astype(F32), q_land[i].astype(F32)
        ).astype(BF16)

    def heads(spans):
        return [
            (g, h, slice(g * 64, (g + 1) * 64), slice(h * 128, (h + 1) * 128))
            for g in spans
            for h in range(2)
        ]

    def keys_of(g, h):
        return kv_s[g, :, h * 256 : h * 256 + 128]

    def values_of(g, h):
        return kv_s[g, :, h * 256 + 128 : (h + 1) * 256]

    def attend(spans):
        jobs = heads(spans)
        score = [
            lax.dot_general(
                last[0, :, head] if g == 3 else q_s[rows, head], keys_of(g, h), NT,
                preferred_element_type=F32,
            )
            for g, h, rows, head in jobs
        ]
        expo = []
        for (g, _, _, _), x in zip(jobs, score):
            span = p.s * 4 + g
            live = key < jnp.where(key < 128, lens[0, span], lens[1, span] + 128)
            expo.append(jnp.where(live, jnp.exp(x * scale), 0.0))
        prob = [x / jnp.sum(x, axis=-1, keepdims=True) for x in expo]
        attn = [
            jnp.dot(x.astype(BF16), values_of(g, h), preferred_element_type=F32)
            for (g, h, _, _), x in zip(jobs, prob)
        ]
        for (g, h, rows, head), x, y in zip(jobs, prob, attn):
            prob_s[g * 2 + h] = x
            a_s[0, rows, head] = y.astype(BF16)

    def differentiate(spans):
        jobs = heads(spans)
        d_prob = [
            lax.dot_general(
                last[1, :, head] if g == 3 else d_s[rows, head], values_of(g, h), NT,
                preferred_element_type=F32,
            )
            for g, h, rows, head in jobs
        ]
        prob = [prob_s[g * 2 + h] for g, h, _, _ in jobs]
        delta = [jnp.sum(x * y, axis=-1, keepdims=True) for x, y in zip(prob, d_prob)]
        d_score = [
            (x * (y - z) * scale).astype(BF16) for x, y, z in zip(prob, d_prob, delta)
        ]
        d_query = [
            jnp.dot(x, keys_of(g, h), preferred_element_type=F32)
            for (g, h, _, _), x in zip(jobs, d_score)
        ]
        for (_, _, rows, head), y in zip(jobs, d_query):
            a_s[1, rows, head] = y.astype(BF16)

    def give_back(i):
        back = w.group(a_land.at[i])
        return back, back.send(a_s.at[i, tail], a_land.at[i], p.nxt)

    def take_back(i, back, k):
        w.wait(k, a_land.at[i], p.prv)
        back.flush()
        got = jnp.where(p.s > 0, a_land[i].astype(F32), 0.0)
        a_s[i, tail, :] = jnp.where(first, a_s[i, tail, :].astype(F32), got).astype(BF16)

    keyval(3)
    w.wait(kq, q_land.at[0], p.nxt)
    swapped(0, q_s)
    attend((3,))
    back_o = give_back(0)
    for g in range(3):
        keyval(g)
    def fill(i, weights, part, c, rows):
        for b in range(8):
            part[b, c] = lax.dot_general(
                a_s[i, rows, :], weights[b * 2 + c], NT, preferred_element_type=F32
            ).astype(BF16)

    def keep_out(total):
        res[0] = pltpu.roll(total, 63, 0).astype(BF16)

    def keep_head(rows, total):
        sum_o[rows, :] = total

    def keep_tail(total):
        sum_o[tail, :] = total

    blocks = pl.ds(0, 15)
    body_rows, every = pl.ds(0, 192), slice(None)
    ro = scatter_mp(
        w, p, w.group(wo_s.at[blocks]), part_o, sib_o, acc_o, land_o, keep_out, False
    )
    rg = scatter_zy(
        w, p, w.group(wq_s.at[blocks, body_rows]),
        part_g, sib_g, acc_g, zland_g, land_g, keep_head,
    )
    rt = scatter_mp(
        w, p, w.group(wq_s.at[blocks, pl.ds(0, 64)]),
        part_t, sib_t, acc_t, land_t, keep_tail, False,
    )
    attend((0, 1, 2))
    differentiate((0, 1, 2))
    fill(1, wq_s, part_g, 1 - p.c, body_rows)
    next(rg)
    w.wait(kd, q_land.at[1], p.nxt)
    swapped(1, d_s)
    differentiate((3,))
    back_g = give_back(1)
    fill(1, wq_s, part_g, p.c, body_rows)
    next(rg)
    take_back(0, *back_o)
    fill(0, wo_s, part_o, 1 - p.c, every)
    next(ro)
    fill(0, wo_s, part_o, p.c, every)
    next(ro)
    next(rg)
    take_back(1, *back_g)
    fill(1, wq_s, part_t, 1 - p.c, tail)
    next(rt)
    fill(1, wq_s, part_t, p.c, tail)
    next(rt)
    next(rg)
    next(ro)
    next(rt)
    next(rg)
    next(ro)
    next(rt)
    next(rg, None)
    next(ro, None)
    next(rt, None)
    res[1] = pltpu.roll(sum_o[...], 63, 0).astype(BF16)
    w.finish()


def per_device(
    hidden, cotangent, neighbour_ids, neighbour_lengths, embed_table,
    enc_up, enc_down, w_query, w_keyval, w_out,
):
    blk = (256, 256)
    row = (64, 896)
    bf = lambda *s: pltpu.VMEM(s, BF16)
    vm = pl.BlockSpec(memory_space=pltpu.VMEM)
    messages, groups = 130, 18
    res = pl.pallas_call(
        body,
        out_shape=jax.ShapeDtypeStruct((2,) + blk, BF16),
        in_specs=[vm] * 5
        + [pl.BlockSpec(memory_space=pl.ANY), vm, pl.BlockSpec(memory_space=pltpu.SMEM), vm, vm],
        out_specs=vm,
        scratch_shapes=[
            bf(4096, 896), pltpu.VMEM((8, 128, 128), jnp.int32), bf(512, 4096),
            bf(8, 2, *row), bf(8, *row), bf(8, *row), bf(7, *row), bf(*row), bf(4, *row),
            bf(256, 896),
            bf(4, 224, 896), bf(4, 224, 896), bf(4, 256, 224), bf(4, *row),
            bf(6, 32, 896), bf(*row), bf(16, *row),
            bf(16, *blk), bf(16, *blk), bf(16, *blk), bf(16, *blk), bf(16, 56, 512),
            bf(896, 512), pltpu.VMEM((896, 512), F32), bf(4, 256, 512),
            bf(*blk), bf(*blk), bf(2, 64, 256), bf(2, 64, 256), bf(2, *blk), bf(2, 64, 256),
            bf(8, 2, *blk), bf(8, *blk), bf(8, *blk), bf(7, *blk),
            bf(8, 2, 192, 256), bf(8, 192, 256), bf(8, 192, 256), bf(4, 192, 256), bf(6, 96, 256),
            bf(8, 2, 64, 256), bf(8, 64, 256), bf(8, 64, 256), bf(7, 64, 256),
            pltpu.VMEM(blk, F32), pltpu.VMEM((8, 64, 256), F32),
            pltpu.SemaphoreType.DMA,
            pltpu.SemaphoreType.DMA((groups,)), pltpu.SemaphoreType.DMA((messages,)),
        ],
        compiler_params=pltpu.CompilerParams(
            collective_id=1, has_side_effects=True, vmem_limit_bytes=62 * 1024 * 1024
        ),
        name="block",
    )(
        hidden, cotangent, w_query.reshape(blk), w_out.reshape(blk),
        w_keyval.reshape(56, 512), embed_table, neighbour_ids.reshape(8, 128),
        neighbour_lengths.T, enc_up, enc_down,
    )
    return res[0], res[1]


def solution(mesh):
    return jax.shard_map(
        per_device,
        mesh=mesh,
        in_specs=(
            P("seq", "mp"),
            P("seq", "mp"),
            P("seq", None, None),
            P(),
            P("mp", None),
            P("mp", None),
            P("mp", None),
            P("seq", "mp", None),
            P("seq", "mp", None, None),
            P("seq", "mp", None),
        ),
        out_specs=(P("seq", "mp"), P("seq", "mp")),
        check_vma=False,
    )
```

```python
import functools

import jax
import jax.numpy as jnp
from jax import lax
from jax.experimental import pallas as pl
from jax.experimental.pallas import tpu as pltpu
from jax.sharding import PartitionSpec as P

MESH = pl.DeviceIdType.MESH
F32 = jnp.float32
BF16 = jnp.bfloat16


class Place:
    def __init__(self):
        s = lax.axis_index("seq")
        m = lax.axis_index("mp")
        self.s, self.m = s, m
        self.x, self.zh = s // 4, s % 4
        self.y, self.zl, self.c = m // 4, (m // 2) % 2, m % 2
        self.sib = (s, self.mp(0, self.zl, 1 - self.c))
        self.zn = (s, self.mp(0, 1 - self.zl, self.c))
        self.zo = (self.seq(0, 2 * self.zl + 3), self.mp(0, 1 - self.zl, self.c))
        self.yp = (s, self.mp(1, self.zl, self.c))
        self.ym = (s, self.mp(3, self.zl, self.c))
        self.zp = (self.seq(0, 1), m)
        self.zm = (self.seq(0, 3), m)
        self.xp = (self.seq(1, 0), m)
        self.xm = (self.seq(3, 0), m)
        self.nxt = ((s + 1) % 16, m)
        self.prv = ((s + 15) % 16, m)

    def mp(self, dy, zl, c):
        return (((self.y + dy) % 4) * 2 + zl) * 2 + c

    def pair(self, dy, zl):
        return ((self.y + dy) % 4) * 2 + zl

    def seq(self, dx, dz):
        return ((self.x + dx) % 4) * 4 + (self.zh + dz) % 4


class Wire:
    def __init__(self, send_sem, recv_sem):
        self.send_sem, self.recv_sem = send_sem, recv_sem
        self.count = 0
        self.groups = []
        self.open = []

    def slot(self):
        self.count += 1
        return self.count - 1

    def wait(self, k, landing, frm):
        pltpu.make_async_remote_copy(
            src_ref=landing,
            dst_ref=landing,
            send_sem=self.send_sem.at[0],
            recv_sem=self.recv_sem.at[k],
            device_id=frm,
            device_id_type=MESH,
        ).wait_recv()

    def group(self, total):
        return Group(self, total)

    def finish(self):
        for group in list(self.open):
            group.flush()


class Group:
    def __init__(self, wire, total):
        self.wire, self.total = wire, total
        self.sem = wire.send_sem.at[len(wire.groups)]
        wire.groups.append(self)
        wire.open.append(self)

    def send(self, src, dst, to, k=None):
        k = self.wire.slot() if k is None else k
        self.to = to
        pltpu.make_async_remote_copy(
            src_ref=src,
            dst_ref=dst,
            send_sem=self.sem,
            recv_sem=self.wire.recv_sem.at[k],
            device_id=to,
            device_id_type=MESH,
        ).start()
        return k

    def flush(self):
        self.wire.open.remove(self)
        pltpu.make_async_remote_copy(
            src_ref=self.total,
            dst_ref=self.total,
            send_sem=self.sem,
            recv_sem=self.wire.recv_sem.at[0],
            device_id=self.to,
            device_id_type=MESH,
        ).wait_send()


def greet(peers):
    barrier = pltpu.get_barrier_semaphore()
    for peer in peers:
        pl.semaphore_signal(barrier, inc=1, device_id=peer, device_id_type=MESH)
    pl.semaphore_wait(barrier, len(peers))


def gather_mp(w, p, shard, out, flip=False):
    n = w.group(out.at[pl.ds(0, 15)])
    ks = w.slot()
    mine = p.mp(0, p.zl, p.c)
    o = 1 - p.zl
    fore, back, f, b3 = (p.ym, p.yp, 3, 1) if flip else (p.yp, p.ym, 1, 3)
    at = lambda dy, zl, c: out.at[p.mp(dy, zl, c)]
    own = out.at[mine]
    k_y1 = n.send(shard, own, fore)
    k_y2 = n.send(shard, own, back)
    k_z = n.send(shard, own, p.zn)
    n.send(shard, own, p.sib, ks)
    out[mine] = shard[...]
    yield
    w.wait(k_z, at(0, o, p.c), p.zn)
    zb = at(0, o, p.c)
    k_z1 = n.send(zb, zb, fore)
    k_z2 = n.send(zb, zb, back)
    n.send(zb, zb, p.sib, ks)
    yield
    b = at(b3, p.zl, p.c)
    w.wait(k_y1, b, back)
    k_f1 = n.send(b, b, fore)
    n.send(b, b, p.sib, ks)
    b = at(f, p.zl, p.c)
    w.wait(k_y2, b, fore)
    n.send(b, b, p.sib, ks)
    yield
    b = at(f, o, p.c)
    w.wait(k_z2, b, fore)
    k_f2 = n.send(b, b, back)
    n.send(b, b, p.sib, ks)
    b = at(b3, o, p.c)
    w.wait(k_z1, b, back)
    n.send(b, b, p.sib, ks)
    yield
    b = at(2, p.zl, p.c)
    w.wait(k_f1, b, back)
    n.send(b, b, p.sib, ks)
    b = at(2, o, p.c)
    w.wait(k_f2, b, fore)
    n.send(b, b, p.sib, ks)
    yield
    w.wait(ks, out.at[pl.ds(0, 8)], p.sib)


def scatter_mp(w, p, n, part, sibl, acc, land, result, late):
    o = 1 - p.zl
    ks = {}

    def share(dy):
        row = ((p.y + dy) % 4) * 2
        ks[dy] = n.send(
            part.at[pl.ds(row, 2), 1 - p.c], sibl.at[pl.ds(row, 2)], p.sib
        )

    def combine(dy):
        row = ((p.y + dy) % 4) * 2
        w.wait(ks[dy], sibl.at[pl.ds(row, 2)], p.sib)
        for zl in (0, 1):
            acc[row + zl] = (
                part[row + zl, p.c].astype(F32) + sibl[row + zl].astype(F32)
            ).astype(BF16)

    for dy in (2, 1, 3) if late else (2, 1, 3, 0):
        share(dy)
    yield
    combine(2)
    k0 = n.send(acc.at[p.pair(2, p.zl)], land.at[0], p.yp)
    k1 = n.send(acc.at[p.pair(2, o)], land.at[1], p.ym)
    combine(1)
    k2b = n.send(acc.at[p.pair(1, o)], land.at[2], p.yp)
    combine(3)
    k3a = n.send(acc.at[p.pair(3, p.zl)], land.at[3], p.ym)
    yield
    if late:
        share(0)
        yield
    w.wait(k0, land.at[0], p.ym)
    i = p.pair(1, p.zl)
    acc[i] = (acc[i].astype(F32) + land[0].astype(F32)).astype(BF16)
    k2a = n.send(acc.at[i], land.at[4], p.yp)
    w.wait(k1, land.at[1], p.yp)
    i = p.pair(3, o)
    acc[i] = (acc[i].astype(F32) + land[1].astype(F32)).astype(BF16)
    k3b = n.send(acc.at[i], land.at[5], p.ym)
    combine(0)
    yield
    w.wait(k2b, land.at[2], p.ym)
    w.wait(k3b, land.at[5], p.yp)
    i = p.pair(0, o)
    acc[i] = (acc[i].astype(F32) + land[2].astype(F32) + land[5].astype(F32)).astype(BF16)
    kz = n.send(acc.at[i], land.at[6], p.zn)
    yield
    w.wait(k3a, land.at[3], p.yp)
    w.wait(k2a, land.at[4], p.ym)
    w.wait(kz, land.at[6], p.zn)
    result(
        acc[p.pair(0, p.zl)].astype(F32)
        + land[3].astype(F32)
        + land[4].astype(F32)
        + land[6].astype(F32)
    )


def drain(gens):
    gens = list(gens)
    while gens:
        gens = [g for g in gens if next(g, True) is None]


def gather_seq(w, p, shard, out, up, late):
    n = w.group(out.at[pl.ds(0, 15)])
    k_last = w.slot()
    away = {0: 0, "behind": 3 - 2 * p.zl, "ahead": 1 + 2 * p.zl, 2: 2}
    ahead = (p.seq(0, away["ahead"]), p.m)
    behind = (p.seq(0, away["behind"]), p.m)
    mine = p.seq(0, 0)
    at = lambda dx, dz: out.at[p.seq(dx, away[dz])]
    own = out.at[mine]
    kx = {0: (n.send(shard, own, p.xp), n.send(shard, own, p.xm))}
    out[mine] = shard[...]

    def spread(dz):
        b = at(0, dz)
        kx[dz] = (n.send(b, b, p.xp), n.send(b, b, p.xm))

    def relay(dz, upward):
        k1, k2 = kx[dz]
        if upward:
            b = at(3, dz)
            w.wait(k1, b, p.xm)
            n.send(b, b, p.xp, k_last)
            w.wait(k2, at(1, dz), p.xp)
        else:
            b = at(1, dz)
            w.wait(k2, b, p.xp)
            n.send(b, b, p.xm, k_last)
            w.wait(k1, at(3, dz), p.xm)

    yield
    if late:
        relay(0, up)
        yield
    k_a = n.send(shard, own, ahead)
    k_b = n.send(shard, own, behind)
    yield
    if not late:
        relay(0, up)
        yield
    b = at(0, "behind")
    w.wait(k_a, b, behind)
    k_zf = n.send(b, b, ahead)
    spread("behind")
    w.wait(k_b, at(0, "ahead"), ahead)
    spread("ahead")
    yield
    w.wait(k_zf, at(0, 2), behind)
    spread(2)
    yield
    relay("behind", up)
    yield
    relay("ahead", not up)
    yield
    relay(2, not up)
    yield
    w.wait(k_last, out.at[pl.ds(0, 4)], p.xm)


def gather_pair(w, p, shard, out, other):
    n = w.group(out.at[pl.ds(0, 3)])
    o, oc = 1 - p.zl, 1 - p.c
    mine = p.zl * 2 + p.c
    k_z = n.send(shard, out.at[mine], other)
    k_s = n.send(shard, out.at[mine], p.sib)
    out[mine] = shard[...]
    yield
    b = out.at[o * 2 + p.c]
    w.wait(k_z, b, other)
    k_zs = n.send(b, b, p.sib)
    yield
    w.wait(k_s, out.at[p.zl * 2 + oc], p.sib)
    w.wait(k_zs, out.at[o * 2 + oc], p.sib)


def gather_y(w, p, shard, out):
    n = w.group(out.at[pl.ds(0, 3)])
    rows = shard.shape[0] // 2
    lo, hi = pl.ds(0, rows), pl.ds(rows, rows)
    at = lambda dy: (p.y + dy) % 4
    k1 = n.send(shard.at[lo], out.at[at(0), lo], p.yp)
    k2 = n.send(shard.at[hi], out.at[at(0), hi], p.ym)
    k3 = n.send(shard.at[hi], out.at[at(0), hi], p.yp)
    k4 = n.send(shard.at[lo], out.at[at(0), lo], p.ym)
    out[at(0)] = shard[...]
    yield
    b = out.at[at(3), lo]
    w.wait(k1, b, p.ym)
    f1 = n.send(b, b, p.yp)
    b = out.at[at(1), hi]
    w.wait(k2, b, p.yp)
    f2 = n.send(b, b, p.ym)
    yield
    w.wait(k3, out.at[at(3), hi], p.ym)
    w.wait(k4, out.at[at(1), lo], p.yp)
    w.wait(f1, out.at[at(2), lo], p.ym)
    w.wait(f2, out.at[at(2), hi], p.yp)


def scatter_y(w, p, n, blk, index, ready, land, result):
    rows = blk.shape[1] // 2
    lo, hi = pl.ds(0, rows), pl.ds(rows, rows)
    i0, i1, i2, i3 = index(0), index(1), index(2), index(3)
    ready(2)
    k0 = n.send(blk.at[i2, lo], land.at[0], p.yp)
    k1 = n.send(blk.at[i2, hi], land.at[1], p.ym)
    yield
    ready(1)
    k2b = n.send(blk.at[i1, hi], land.at[2], p.yp)
    ready(3)
    k3a = n.send(blk.at[i3, lo], land.at[3], p.ym)
    yield
    w.wait(k0, land.at[0], p.ym)
    blk[i1, lo, :] = (blk[i1, lo, :].astype(F32) + land[0].astype(F32)).astype(BF16)
    k2a = n.send(blk.at[i1, lo], land.at[4], p.yp)
    w.wait(k1, land.at[1], p.yp)
    blk[i3, hi, :] = (blk[i3, hi, :].astype(F32) + land[1].astype(F32)).astype(BF16)
    k3b = n.send(blk.at[i3, hi], land.at[5], p.ym)
    yield
    ready(0)
    w.wait(k2b, land.at[2], p.ym)
    w.wait(k3a, land.at[3], p.yp)
    w.wait(k2a, land.at[4], p.ym)
    w.wait(k3b, land.at[5], p.yp)
    f = lambda v: v.astype(F32)
    result(lo, f(blk[i0, lo, :]) + f(land[4]) + f(land[3]))
    result(hi, f(blk[i0, hi, :]) + f(land[2]) + f(land[5]))


def scatter_zy(w, p, n, part, sibl, acc, zland, land, result):
    o = 1 - p.zl
    ks, kz = {}, {}
    for dy in (2, 1, 3, 0):
        row = ((p.y + dy) % 4) * 2
        ks[dy] = n.send(
            part.at[pl.ds(row, 2), 1 - p.c], sibl.at[pl.ds(row, 2)], p.sib
        )
    yield
    for dy in (2, 1, 3, 0):
        row = ((p.y + dy) % 4) * 2
        w.wait(ks[dy], sibl.at[pl.ds(row, 2)], p.sib)
        for zl in (o, p.zl):
            acc[row + zl] = (
                part[row + zl, p.c].astype(F32) + sibl[row + zl].astype(F32)
            ).astype(BF16)
        kz[dy] = n.send(acc.at[row + o], zland.at[dy], p.zn)
    yield

    def ready(dy):
        w.wait(kz[dy], zland.at[dy], p.zn)
        i = p.pair(dy, p.zl)
        acc[i] = (acc[i].astype(F32) + zland[dy].astype(F32)).astype(BF16)

    yield from scatter_y(w, p, n, acc, lambda dy: p.pair(dy, p.zl), ready, land, result)


NT = (((1,), (1,)), ((), ()))


def body(
    hid, cot, wq, wo, wkv, table, ids, lens, up, down,
    res,
    tab, idsb, onehot, epart, esib, eacc, eland, emb_own, emb4, normed,
    up4, down4, acts, fblk, fland, enc_own, enc,
    hid_s, cot_s, wq_s, wo_s, wkv_s, wkv_w, wkv_f, kv_s,
    q_s, d_s, q_land, last, a_s, a_land,
    part_o, sib_o, acc_o, land_o, part_g, sib_g, acc_g, zland_g, land_g,
    part_t, sib_t, acc_t, land_t, sum_o, prob_s,
    tab_sem, send_sem, recv_sem,
):
    p = Place()
    w = Wire(send_sem, recv_sem)
    fetch = pltpu.make_async_copy(table, tab.at[pl.ds(0, 4000)], tab_sem)
    fetch.start()
    greet((p.sib, p.zn, p.zo, p.yp, p.ym, p.zp, p.zm, p.xp, p.xm, p.nxt, p.prv))

    gh = gather_mp(w, p, hid, hid_s)
    gc = gather_mp(w, p, cot, cot_s, True)
    gu = gather_pair(w, p, up, up4, p.zo)
    lo, hi = pl.ds(0, 112), pl.ds(112, 112)
    gd = gather_pair(w, p, down.at[lo], down4.at[:, lo], p.zo)
    ge = gather_pair(w, p, down.at[hi], down4.at[:, hi], p.zn)
    gq = gather_seq(w, p, wq, wq_s, True, False)
    gk = gather_seq(w, p, wkv, wkv_s, True, False)
    go = gather_seq(w, p, wo, wo_s, False, True)
    next(gh), next(gc), next(gu)
    next(gq), next(gq)
    next(gk), next(gk)
    next(gd), next(ge), next(go)

    tab[pl.ds(4000, 96), :] = jnp.zeros((96, 896), BF16)
    cols = jnp.transpose(ids[...] - p.m * 4000)
    for r in range(8):
        idsb[r] = jnp.broadcast_to(cols[:, r : r + 1], (128, 128))
    lane = lax.broadcasted_iota(jnp.int32, (64, 128), 1)

    def lookup(c, ys):
        pairs = [p.pair(dy, zl) for dy in ys for zl in (0, 1)]
        high = len(pairs) * 64
        for i, r in enumerate(pairs):
            mine = idsb[r, pl.ds(pl.multiple_of(c * 64, 64), 64), :] - lane
            for k in range(32):
                onehot[i * 64 : (i + 1) * 64, k * 128 : (k + 1) * 128] = jnp.where(
                    mine == k * 128, 1.0, 0.0
                ).astype(BF16)

        def pick(cols_at):
            got = jnp.dot(onehot[0:high, :], tab[:, cols_at], preferred_element_type=F32)
            for i, r in enumerate(pairs):
                epart[r, c, :, cols_at] = got[i * 64 : (i + 1) * 64].astype(BF16)

        for at in (0, 256, 512, 768):
            pick(slice(at, min(at + 256, 896)))

    def keep_emb(total):
        emb_own[...] = total.astype(BF16)

    far = (2, 1, 3)
    fetch.wait()
    lookup(1 - p.c, far)
    ers = scatter_mp(
        w, p, w.group(enc.at[pl.ds(0, 15)]), epart, esib, eacc, eland, keep_emb, True
    )
    next(ers)
    lookup(p.c, far)
    next(ers)
    lookup(1 - p.c, (0,))
    next(ers)
    lookup(p.c, (0,))
    next(ers)
    next(gh), next(gc)
    next(gq), next(gk), next(go)
    next(gu)
    next(ers)
    next(gq), next(gk)
    next(go)
    next(ers, None)
    ey = gather_y(w, p, emb_own, emb4)
    next(ey)
    next(ey)
    next(gh), next(gh)
    next(ey, None)
    next(gu, None)
    next(gq), next(gk)

    e = emb4[...].reshape(256, 896).astype(F32)
    normed[...] = (
        e * lax.rsqrt(jnp.mean(e * e, axis=-1, keepdims=True) + 1e-06)
    ).astype(BF16)
    for j in range(4):
        acts[j] = jax.nn.gelu(
            lax.dot_general(normed[...], up4[j], NT, preferred_element_type=F32)
        ).astype(BF16)
    next(gd), next(ge)
    next(gq), next(gk)
    next(gd, None), next(ge, None)
    total = jnp.dot(acts[0], down4[0], preferred_element_type=F32)
    for j in range(1, 4):
        total = total + jnp.dot(acts[j], down4[j], preferred_element_type=F32)
    for y in range(4):
        fblk[y] = total[y * 64 : (y + 1) * 64, :].astype(BF16)

    def keep_enc(rows, total):
        v = emb_own[rows, :].astype(F32) + total
        v = v * lax.rsqrt(jnp.mean(v * v, axis=-1, keepdims=True) + 1e-06)
        enc_own[rows, :] = v.astype(BF16)

    fy = scatter_y(
        w, p, w.group(enc.at[pl.ds(0, 3)]), fblk, lambda dy: (p.y + dy) % 4, lambda dy: None, fland, keep_enc
    )
    next(fy)
    next(fy)
    next(gq), next(gk)
    next(go)
    next(gh)
    next(fy)
    next(gc), next(gc)
    next(gq), next(gk)
    next(fy, None)
    ga = gather_mp(w, p, enc_own, enc)
    next(ga)
    next(go)
    next(gh, None)
    next(ga)
    next(go)
    next(ga)
    next(ga)
    next(gc)
    next(go)
    drain([gq, gk])
    for i in range(16):
        wkv_f[pl.ds(56 * i, 56), :] = wkv_s[i].astype(F32)
    wkv_w[...] = wkv_f[...].astype(BF16)

    def project(src, weights, sums, columns, start):
        total = None if start else sums[...]
        for dx in columns:
            for dz in range(4):
                b = p.seq(dx, dz)
                got = jnp.dot(src[b], weights[b], preferred_element_type=F32)
                total = got if total is None else total + got
        sums[...] = total

    next(go)
    project(hid_s, wq_s, sum_o, (0, 1, 2, 3), True)
    q_s[...] = pltpu.roll(sum_o[...], 193, 0).astype(BF16)
    swap = w.group(q_land)
    kq = swap.send(q_s.at[pl.ds(192, 64)], q_land.at[0], p.prv)
    next(ga)
    next(gc, None)
    project(cot_s, wo_s, sum_o, (0,), True)
    drain([go])
    project(cot_s, wo_s, sum_o, (1, 3, 2), False)
    d_s[...] = pltpu.roll(sum_o[...], 193, 0).astype(BF16)
    kd = swap.send(d_s.at[pl.ds(192, 64)], q_land.at[1], p.prv)
    next(ga, None)

    def keyval(g):
        rows = enc[g * 4 : g * 4 + 4].reshape(256, 896)
        kv_s[g] = jnp.dot(rows, wkv_w[...], preferred_element_type=F32).astype(BF16)

    first = lax.broadcasted_iota(jnp.int32, (64, 256), 0) == 0
    tail = pl.ds(192, 64)
    key = lax.broadcasted_iota(jnp.int32, (64, 256), 1)
    scale = 128 ** (-0.5)

    def swapped(i, src):
        last[i] = jnp.where(
            first, src[tail, :].astype(F32), q_land[i].astype(F32)
        ).astype(BF16)

    def heads(spans):
        return [
            (g, h, slice(g * 64, (g + 1) * 64), slice(h * 128, (h + 1) * 128))
            for g in spans
            for h in range(2)
        ]

    def keys_of(g, h):
        return kv_s[g, :, h * 256 : h * 256 + 128]

    def values_of(g, h):
        return kv_s[g, :, h * 256 + 128 : (h + 1) * 256]

    def attend(spans):
        jobs = heads(spans)
        score = [
            lax.dot_general(
                last[0, :, head] if g == 3 else q_s[rows, head], keys_of(g, h), NT,
                preferred_element_type=F32,
            )
            for g, h, rows, head in jobs
        ]
        expo = []
        for (g, _, _, _), x in zip(jobs, score):
            span = p.s * 4 + g
            live = key < jnp.where(key < 128, lens[0, span], lens[1, span] + 128)
            expo.append(jnp.where(live, jnp.exp(x * scale), 0.0))
        prob = [x / jnp.sum(x, axis=-1, keepdims=True) for x in expo]
        attn = [
            jnp.dot(x.astype(BF16), values_of(g, h), preferred_element_type=F32)
            for (g, h, _, _), x in zip(jobs, prob)
        ]
        for (g, h, rows, head), x, y in zip(jobs, prob, attn):
            prob_s[g * 2 + h] = x
            a_s[0, rows, head] = y.astype(BF16)

    def differentiate(spans):
        jobs = heads(spans)
        d_prob = [
            lax.dot_general(
                last[1, :, head] if g == 3 else d_s[rows, head], values_of(g, h), NT,
                preferred_element_type=F32,
            )
            for g, h, rows, head in jobs
        ]
        prob = [prob_s[g * 2 + h] for g, h, _, _ in jobs]
        delta = [jnp.sum(x * y, axis=-1, keepdims=True) for x, y in zip(prob, d_prob)]
        d_score = [
            (x * (y - z) * scale).astype(BF16) for x, y, z in zip(prob, d_prob, delta)
        ]
        d_query = [
            jnp.dot(x, keys_of(g, h), preferred_element_type=F32)
            for (g, h, _, _), x in zip(jobs, d_score)
        ]
        for (_, _, rows, head), y in zip(jobs, d_query):
            a_s[1, rows, head] = y.astype(BF16)

    def give_back(i):
        back = w.group(a_land.at[i])
        return back, back.send(a_s.at[i, tail], a_land.at[i], p.nxt)

    def take_back(i, back, k):
        w.wait(k, a_land.at[i], p.prv)
        back.flush()
        got = jnp.where(p.s > 0, a_land[i].astype(F32), 0.0)
        a_s[i, tail, :] = jnp.where(first, a_s[i, tail, :].astype(F32), got).astype(BF16)

    keyval(3)
    w.wait(kq, q_land.at[0], p.nxt)
    swapped(0, q_s)
    attend((3,))
    back_o = give_back(0)
    for g in range(3):
        keyval(g)
    def fill(i, weights, part, c, rows):
        for b in range(8):
            part[b, c] = lax.dot_general(
                a_s[i, rows, :], weights[b * 2 + c], NT, preferred_element_type=F32
            ).astype(BF16)

    def keep_out(total):
        res[0] = pltpu.roll(total, 63, 0).astype(BF16)

    def keep_head(rows, total):
        sum_o[rows, :] = total

    def keep_tail(total):
        sum_o[tail, :] = total

    blocks = pl.ds(0, 15)
    body_rows, every = pl.ds(0, 192), slice(None)
    ro = scatter_mp(
        w, p, w.group(wo_s.at[blocks]), part_o, sib_o, acc_o, land_o, keep_out, False
    )
    rg = scatter_zy(
        w, p, w.group(wq_s.at[blocks, body_rows]),
        part_g, sib_g, acc_g, zland_g, land_g, keep_head,
    )
    rt = scatter_mp(
        w, p, w.group(wq_s.at[blocks, pl.ds(0, 64)]),
        part_t, sib_t, acc_t, land_t, keep_tail, False,
    )
    attend((0, 1, 2))
    differentiate((0, 1, 2))
    fill(1, wq_s, part_g, 1 - p.c, body_rows)
    next(rg)
    w.wait(kd, q_land.at[1], p.nxt)
    swapped(1, d_s)
    differentiate((3,))
    back_g = give_back(1)
    fill(1, wq_s, part_g, p.c, body_rows)
    next(rg)
    take_back(0, *back_o)
    fill(0, wo_s, part_o, 1 - p.c, every)
    next(ro)
    fill(0, wo_s, part_o, p.c, every)
    next(ro)
    next(rg)
    take_back(1, *back_g)
    fill(1, wq_s, part_t, 1 - p.c, tail)
    next(rt)
    fill(1, wq_s, part_t, p.c, tail)
    next(rt)
    next(rg)
    next(ro)
    next(rt)
    next(rg)
    next(ro)
    next(rt)
    next(rg, None)
    next(ro, None)
    next(rt, None)
    res[1] = pltpu.roll(sum_o[...], 63, 0).astype(BF16)
    w.finish()


def per_device(
    hidden, cotangent, neighbour_ids, neighbour_lengths, embed_table,
    enc_up, enc_down, w_query, w_keyval, w_out,
):
    blk = (256, 256)
    row = (64, 896)
    bf = lambda *s: pltpu.VMEM(s, BF16)
    vm = pl.BlockSpec(memory_space=pltpu.VMEM)
    messages, groups = 132, 18
    res = pl.pallas_call(
        body,
        out_shape=jax.ShapeDtypeStruct((2,) + blk, BF16),
        in_specs=[vm] * 5
        + [pl.BlockSpec(memory_space=pl.ANY), vm, pl.BlockSpec(memory_space=pltpu.SMEM), vm, vm],
        out_specs=vm,
        scratch_shapes=[
            bf(4096, 896), pltpu.VMEM((8, 128, 128), jnp.int32), bf(512, 4096),
            bf(8, 2, *row), bf(8, *row), bf(8, *row), bf(7, *row), bf(*row), bf(4, *row),
            bf(256, 896),
            bf(4, 224, 896), bf(4, 224, 896), bf(4, 256, 224), bf(4, *row),
            bf(6, 32, 896), bf(*row), bf(16, *row),
            bf(16, *blk), bf(16, *blk), bf(16, *blk), bf(16, *blk), bf(16, 56, 512),
            bf(896, 512), pltpu.VMEM((896, 512), F32), bf(4, 256, 512),
            bf(*blk), bf(*blk), bf(2, 64, 256), bf(2, 64, 256), bf(2, *blk), bf(2, 64, 256),
            bf(8, 2, *blk), bf(8, *blk), bf(8, *blk), bf(7, *blk),
            bf(8, 2, 192, 256), bf(8, 192, 256), bf(8, 192, 256), bf(4, 192, 256), bf(6, 96, 256),
            bf(8, 2, 64, 256), bf(8, 64, 256), bf(8, 64, 256), bf(7, 64, 256),
            pltpu.VMEM(blk, F32), pltpu.VMEM((8, 64, 256), F32),
            pltpu.SemaphoreType.DMA,
            pltpu.SemaphoreType.DMA((groups,)), pltpu.SemaphoreType.DMA((messages,)),
        ],
        compiler_params=pltpu.CompilerParams(
            collective_id=1, has_side_effects=True, vmem_limit_bytes=62 * 1024 * 1024
        ),
        name="block",
    )(
        hidden, cotangent, w_query.reshape(blk), w_out.reshape(blk),
        w_keyval.reshape(56, 512), embed_table, neighbour_ids.reshape(8, 128),
        neighbour_lengths.T, enc_up, enc_down,
    )
    return res[0], res[1]


def solution(mesh):
    return jax.shard_map(
        per_device,
        mesh=mesh,
        in_specs=(
            P("seq", "mp"),
            P("seq", "mp"),
            P("seq", None, None),
            P(),
            P("mp", None),
            P("mp", None),
            P("mp", None),
            P("seq", "mp", None),
            P("seq", "mp", None, None),
            P("seq", "mp", None),
        ),
        out_specs=(P("seq", "mp"), P("seq", "mp")),
        check_vma=False,
    )
```

```python
import functools

import jax
import jax.numpy as jnp
from jax import lax
from jax.experimental import pallas as pl
from jax.experimental.pallas import tpu as pltpu
from jax.sharding import PartitionSpec as P

MESH = pl.DeviceIdType.MESH
F32 = jnp.float32
BF16 = jnp.bfloat16


class Place:
    def __init__(self):
        s = lax.axis_index("seq")
        m = lax.axis_index("mp")
        self.s, self.m = s, m
        self.x, self.zh = s // 4, s % 4
        self.y, self.zl, self.c = m // 4, (m // 2) % 2, m % 2
        self.sib = (s, self.mp(0, self.zl, 1 - self.c))
        self.zn = (s, self.mp(0, 1 - self.zl, self.c))
        self.zo = (self.seq(0, 2 * self.zl + 3), self.mp(0, 1 - self.zl, self.c))
        self.yp = (s, self.mp(1, self.zl, self.c))
        self.ym = (s, self.mp(3, self.zl, self.c))
        self.zp = (self.seq(0, 1), m)
        self.zm = (self.seq(0, 3), m)
        self.xp = (self.seq(1, 0), m)
        self.xm = (self.seq(3, 0), m)
        self.nxt = ((s + 1) % 16, m)
        self.prv = ((s + 15) % 16, m)

    def mp(self, dy, zl, c):
        return (((self.y + dy) % 4) * 2 + zl) * 2 + c

    def pair(self, dy, zl):
        return ((self.y + dy) % 4) * 2 + zl

    def seq(self, dx, dz):
        return ((self.x + dx) % 4) * 4 + (self.zh + dz) % 4


class Wire:
    def __init__(self, send_sem, recv_sem):
        self.send_sem, self.recv_sem = send_sem, recv_sem
        self.count = 0
        self.groups = []
        self.open = []

    def slot(self):
        self.count += 1
        return self.count - 1

    def wait(self, k, landing, frm):
        pltpu.make_async_remote_copy(
            src_ref=landing,
            dst_ref=landing,
            send_sem=self.send_sem.at[0],
            recv_sem=self.recv_sem.at[k],
            device_id=frm,
            device_id_type=MESH,
        ).wait_recv()

    def group(self, total):
        return Group(self, total)

    def finish(self):
        for group in list(self.open):
            group.flush()


class Group:
    def __init__(self, wire, total):
        self.wire, self.total = wire, total
        self.sem = wire.send_sem.at[len(wire.groups)]
        wire.groups.append(self)
        wire.open.append(self)

    def send(self, src, dst, to, k=None):
        k = self.wire.slot() if k is None else k
        self.to = to
        pltpu.make_async_remote_copy(
            src_ref=src,
            dst_ref=dst,
            send_sem=self.sem,
            recv_sem=self.wire.recv_sem.at[k],
            device_id=to,
            device_id_type=MESH,
        ).start()
        return k

    def flush(self):
        self.wire.open.remove(self)
        pltpu.make_async_remote_copy(
            src_ref=self.total,
            dst_ref=self.total,
            send_sem=self.sem,
            recv_sem=self.wire.recv_sem.at[0],
            device_id=self.to,
            device_id_type=MESH,
        ).wait_send()


def greet(peers, meanwhile):
    barrier = pltpu.get_barrier_semaphore()
    for peer in peers:
        pl.semaphore_signal(barrier, inc=1, device_id=peer, device_id_type=MESH)
    meanwhile()
    pl.semaphore_wait(barrier, len(peers))


def gather_mp(w, p, shard, out, flip=False):
    n = w.group(out.at[pl.ds(0, 15)])
    ks = w.slot()
    mine = p.mp(0, p.zl, p.c)
    o = 1 - p.zl
    fore, back, f, b3 = (p.ym, p.yp, 3, 1) if flip else (p.yp, p.ym, 1, 3)
    at = lambda dy, zl, c: out.at[p.mp(dy, zl, c)]
    own = out.at[mine]
    k_y1 = n.send(shard, own, fore)
    k_y2 = n.send(shard, own, back)
    k_z = n.send(shard, own, p.zn)
    n.send(shard, own, p.sib, ks)
    out[mine] = shard[...]
    yield
    w.wait(k_z, at(0, o, p.c), p.zn)
    zb = at(0, o, p.c)
    k_z1 = n.send(zb, zb, fore)
    k_z2 = n.send(zb, zb, back)
    n.send(zb, zb, p.sib, ks)
    yield
    b = at(b3, p.zl, p.c)
    w.wait(k_y1, b, back)
    k_f1 = n.send(b, b, fore)
    n.send(b, b, p.sib, ks)
    b = at(f, p.zl, p.c)
    w.wait(k_y2, b, fore)
    n.send(b, b, p.sib, ks)
    yield
    b = at(f, o, p.c)
    w.wait(k_z2, b, fore)
    k_f2 = n.send(b, b, back)
    n.send(b, b, p.sib, ks)
    b = at(b3, o, p.c)
    w.wait(k_z1, b, back)
    n.send(b, b, p.sib, ks)
    yield
    b = at(2, p.zl, p.c)
    w.wait(k_f1, b, back)
    n.send(b, b, p.sib, ks)
    b = at(2, o, p.c)
    w.wait(k_f2, b, fore)
    n.send(b, b, p.sib, ks)
    yield
    w.wait(ks, out.at[pl.ds(0, 8)], p.sib)


def scatter_mp(w, p, n, part, sibl, acc, land, result, late):
    o = 1 - p.zl
    ks = {}

    def share(dy):
        row = ((p.y + dy) % 4) * 2
        ks[dy] = n.send(
            part.at[pl.ds(row, 2), 1 - p.c], sibl.at[pl.ds(row, 2)], p.sib
        )

    def combine(dy):
        row = ((p.y + dy) % 4) * 2
        w.wait(ks[dy], sibl.at[pl.ds(row, 2)], p.sib)
        for zl in (0, 1):
            acc[row + zl] = (
                part[row + zl, p.c].astype(F32) + sibl[row + zl].astype(F32)
            ).astype(BF16)

    for dy in (2, 1, 3) if late else (2, 1, 3, 0):
        share(dy)
    yield
    combine(2)
    k0 = n.send(acc.at[p.pair(2, p.zl)], land.at[0], p.yp)
    k1 = n.send(acc.at[p.pair(2, o)], land.at[1], p.ym)
    combine(1)
    k2b = n.send(acc.at[p.pair(1, o)], land.at[2], p.yp)
    combine(3)
    k3a = n.send(acc.at[p.pair(3, p.zl)], land.at[3], p.ym)
    yield
    if late:
        share(0)
        yield
    w.wait(k0, land.at[0], p.ym)
    i = p.pair(1, p.zl)
    acc[i] = (acc[i].astype(F32) + land[0].astype(F32)).astype(BF16)
    k2a = n.send(acc.at[i], land.at[4], p.yp)
    w.wait(k1, land.at[1], p.yp)
    i = p.pair(3, o)
    acc[i] = (acc[i].astype(F32) + land[1].astype(F32)).astype(BF16)
    k3b = n.send(acc.at[i], land.at[5], p.ym)
    combine(0)
    yield
    w.wait(k2b, land.at[2], p.ym)
    w.wait(k3b, land.at[5], p.yp)
    i = p.pair(0, o)
    acc[i] = (acc[i].astype(F32) + land[2].astype(F32) + land[5].astype(F32)).astype(BF16)
    kz = n.send(acc.at[i], land.at[6], p.zn)
    yield
    w.wait(k3a, land.at[3], p.yp)
    w.wait(k2a, land.at[4], p.ym)
    w.wait(kz, land.at[6], p.zn)
    result(
        acc[p.pair(0, p.zl)].astype(F32)
        + land[3].astype(F32)
        + land[4].astype(F32)
        + land[6].astype(F32)
    )


def drain(gens):
    gens = list(gens)
    while gens:
        gens = [g for g in gens if next(g, True) is None]


def gather_seq(w, p, shard, out, up, late):
    n = w.group(out.at[pl.ds(0, 15)])
    k_last = w.slot()
    away = {0: 0, "behind": 3 - 2 * p.zl, "ahead": 1 + 2 * p.zl, 2: 2}
    ahead = (p.seq(0, away["ahead"]), p.m)
    behind = (p.seq(0, away["behind"]), p.m)
    mine = p.seq(0, 0)
    at = lambda dx, dz: out.at[p.seq(dx, away[dz])]
    own = out.at[mine]
    kx = {0: (n.send(shard, own, p.xp), n.send(shard, own, p.xm))}
    out[mine] = shard[...]

    def spread(dz):
        b = at(0, dz)
        kx[dz] = (n.send(b, b, p.xp), n.send(b, b, p.xm))

    def relay(dz, upward):
        k1, k2 = kx[dz]
        if upward:
            b = at(3, dz)
            w.wait(k1, b, p.xm)
            n.send(b, b, p.xp, k_last)
            w.wait(k2, at(1, dz), p.xp)
        else:
            b = at(1, dz)
            w.wait(k2, b, p.xp)
            n.send(b, b, p.xm, k_last)
            w.wait(k1, at(3, dz), p.xm)

    yield
    if late:
        relay(0, up)
        yield
    k_a = n.send(shard, own, ahead)
    k_b = n.send(shard, own, behind)
    yield
    if not late:
        relay(0, up)
        yield
    b = at(0, "behind")
    w.wait(k_a, b, behind)
    k_zf = n.send(b, b, ahead)
    spread("behind")
    w.wait(k_b, at(0, "ahead"), ahead)
    spread("ahead")
    yield
    w.wait(k_zf, at(0, 2), behind)
    spread(2)
    yield
    relay("behind", up)
    yield
    relay("ahead", not up)
    yield
    relay(2, not up)
    yield
    w.wait(k_last, out.at[pl.ds(0, 4)], p.xm)


def gather_pair(w, p, shard, out, other):
    n = w.group(out.at[pl.ds(0, 3)])
    o, oc = 1 - p.zl, 1 - p.c
    mine = p.zl * 2 + p.c
    k_z = n.send(shard, out.at[mine], other)
    k_s = n.send(shard, out.at[mine], p.sib)
    out[mine] = shard[...]
    yield
    b = out.at[o * 2 + p.c]
    w.wait(k_z, b, other)
    k_zs = n.send(b, b, p.sib)
    yield
    w.wait(k_s, out.at[p.zl * 2 + oc], p.sib)
    w.wait(k_zs, out.at[o * 2 + oc], p.sib)


def gather_y(w, p, shard, out):
    n = w.group(out.at[pl.ds(0, 3)])
    rows = shard.shape[0] // 2
    lo, hi = pl.ds(0, rows), pl.ds(rows, rows)
    at = lambda dy: (p.y + dy) % 4
    k1 = n.send(shard.at[lo], out.at[at(0), lo], p.yp)
    k2 = n.send(shard.at[hi], out.at[at(0), hi], p.ym)
    k3 = n.send(shard.at[hi], out.at[at(0), hi], p.yp)
    k4 = n.send(shard.at[lo], out.at[at(0), lo], p.ym)
    out[at(0)] = shard[...]
    yield
    b = out.at[at(3), lo]
    w.wait(k1, b, p.ym)
    f1 = n.send(b, b, p.yp)
    b = out.at[at(1), hi]
    w.wait(k2, b, p.yp)
    f2 = n.send(b, b, p.ym)
    yield
    w.wait(k3, out.at[at(3), hi], p.ym)
    w.wait(k4, out.at[at(1), lo], p.yp)
    w.wait(f1, out.at[at(2), lo], p.ym)
    w.wait(f2, out.at[at(2), hi], p.yp)


def scatter_y(w, p, n, blk, index, ready, land, result):
    rows = blk.shape[1] // 2
    lo, hi = pl.ds(0, rows), pl.ds(rows, rows)
    i0, i1, i2, i3 = index(0), index(1), index(2), index(3)
    ready(2)
    k0 = n.send(blk.at[i2, lo], land.at[0], p.yp)
    k1 = n.send(blk.at[i2, hi], land.at[1], p.ym)
    yield
    ready(1)
    k2b = n.send(blk.at[i1, hi], land.at[2], p.yp)
    ready(3)
    k3a = n.send(blk.at[i3, lo], land.at[3], p.ym)
    yield
    w.wait(k0, land.at[0], p.ym)
    blk[i1, lo, :] = (blk[i1, lo, :].astype(F32) + land[0].astype(F32)).astype(BF16)
    k2a = n.send(blk.at[i1, lo], land.at[4], p.yp)
    w.wait(k1, land.at[1], p.yp)
    blk[i3, hi, :] = (blk[i3, hi, :].astype(F32) + land[1].astype(F32)).astype(BF16)
    k3b = n.send(blk.at[i3, hi], land.at[5], p.ym)
    yield
    ready(0)
    w.wait(k2b, land.at[2], p.ym)
    w.wait(k3a, land.at[3], p.yp)
    w.wait(k2a, land.at[4], p.ym)
    w.wait(k3b, land.at[5], p.yp)
    f = lambda v: v.astype(F32)
    result(lo, f(blk[i0, lo, :]) + f(land[4]) + f(land[3]))
    result(hi, f(blk[i0, hi, :]) + f(land[2]) + f(land[5]))


def scatter_zy(w, p, n, part, sibl, acc, zland, land, result):
    o = 1 - p.zl
    ks, kz = {}, {}
    for dy in (2, 1, 3, 0):
        row = ((p.y + dy) % 4) * 2
        ks[dy] = n.send(
            part.at[pl.ds(row, 2), 1 - p.c], sibl.at[pl.ds(row, 2)], p.sib
        )
    yield
    for dy in (2, 1, 3, 0):
        row = ((p.y + dy) % 4) * 2
        w.wait(ks[dy], sibl.at[pl.ds(row, 2)], p.sib)
        for zl in (o, p.zl):
            acc[row + zl] = (
                part[row + zl, p.c].astype(F32) + sibl[row + zl].astype(F32)
            ).astype(BF16)
        kz[dy] = n.send(acc.at[row + o], zland.at[dy], p.zn)
    yield

    def ready(dy):
        w.wait(kz[dy], zland.at[dy], p.zn)
        i = p.pair(dy, p.zl)
        acc[i] = (acc[i].astype(F32) + zland[dy].astype(F32)).astype(BF16)

    yield from scatter_y(w, p, n, acc, lambda dy: p.pair(dy, p.zl), ready, land, result)


NT = (((1,), (1,)), ((), ()))


def body(
    hid, cot, wq3, wo3, wkv3, table, ids, lens, up, down,
    res,
    tab, idsb, onehot, epart, esib, eacc, eland, emb_own, emb4, normed,
    up4, down4, acts, fblk, fland, enc_own, enc,
    hid_s, cot_s, wq_s, wo_s, wkv_s, wkv_w, wkv_f, kv_s,
    q_s, d_s, q_land, last, a_s, a_land,
    part_o, sib_o, acc_o, land_o, part_g, sib_g, acc_g, zland_g, land_g,
    part_t, sib_t, acc_t, land_t, sum_o, prob_s,
    wq, wo, wkv, tab_sem, send_sem, recv_sem,
):
    p = Place()
    w = Wire(send_sem, recv_sem)
    fetch = pltpu.make_async_copy(table, tab.at[pl.ds(0, 4000)], tab_sem)
    fetch.start()
    def relay_weights():
        for h in range(2):
            head = slice(h * 128, (h + 1) * 128)
            wq[:, head] = wq3[:, h, :]
            wo[:, head] = wo3[:, h, :]
            for kv in range(2):
                wkv[:, h * 256 + kv * 128 : h * 256 + (kv + 1) * 128] = wkv3[:, h, kv, :]

    greet((p.sib, p.zn, p.zo, p.yp, p.ym, p.zp, p.zm, p.xp, p.xm, p.nxt, p.prv), relay_weights)

    gh = gather_mp(w, p, hid, hid_s)
    gc = gather_mp(w, p, cot, cot_s, True)
    gu = gather_pair(w, p, up, up4, p.zo)
    lo, hi = pl.ds(0, 112), pl.ds(112, 112)
    gd = gather_pair(w, p, down.at[lo], down4.at[:, lo], p.zo)
    ge = gather_pair(w, p, down.at[hi], down4.at[:, hi], p.zn)
    gq = gather_seq(w, p, wq, wq_s, True, False)
    gk = gather_seq(w, p, wkv, wkv_s, True, False)
    go = gather_seq(w, p, wo, wo_s, False, True)
    next(gh), next(gc), next(gu)
    next(gq), next(gq)
    next(gk), next(gk)
    next(gd), next(ge), next(go)

    tab[pl.ds(4000, 96), :] = jnp.zeros((96, 896), BF16)
    cols = jnp.transpose(ids[...] - p.m * 4000)
    for r in range(8):
        idsb[r] = jnp.broadcast_to(cols[:, r : r + 1], (128, 128))
    lane = lax.broadcasted_iota(jnp.int32, (64, 128), 1)

    def lookup(c, ys):
        pairs = [p.pair(dy, zl) for dy in ys for zl in (0, 1)]
        high = len(pairs) * 64
        for i, r in enumerate(pairs):
            mine = idsb[r, pl.ds(pl.multiple_of(c * 64, 64), 64), :] - lane
            for k in range(32):
                onehot[i * 64 : (i + 1) * 64, k * 128 : (k + 1) * 128] = jnp.where(
                    mine == k * 128, 1.0, 0.0
                ).astype(BF16)

        def pick(cols_at):
            got = jnp.dot(onehot[0:high, :], tab[:, cols_at], preferred_element_type=F32)
            for i, r in enumerate(pairs):
                epart[r, c, :, cols_at] = got[i * 64 : (i + 1) * 64].astype(BF16)

        for at in (0, 256, 512, 768):
            pick(slice(at, min(at + 256, 896)))

    def keep_emb(total):
        emb_own[...] = total.astype(BF16)

    far = (2, 1, 3)
    fetch.wait()
    lookup(1 - p.c, far)
    ers = scatter_mp(
        w, p, w.group(enc.at[pl.ds(0, 15)]), epart, esib, eacc, eland, keep_emb, True
    )
    next(ers)
    lookup(p.c, far)
    next(ers)
    lookup(1 - p.c, (0,))
    next(ers)
    lookup(p.c, (0,))
    next(ers)
    next(gh), next(gc)
    next(gq), next(gk), next(go)
    next(gu)
    next(ers)
    next(gq), next(gk)
    next(go)
    next(ers, None)
    ey = gather_y(w, p, emb_own, emb4)
    next(ey)
    next(ey)
    next(gh), next(gh)
    next(ey, None)
    next(gu, None)
    next(gq), next(gk)

    e = emb4[...].reshape(256, 896).astype(F32)
    normed[...] = (
        e * lax.rsqrt(jnp.mean(e * e, axis=-1, keepdims=True) + 1e-06)
    ).astype(BF16)
    for j in range(4):
        acts[j] = jax.nn.gelu(
            lax.dot_general(normed[...], up4[j], NT, preferred_element_type=F32)
        ).astype(BF16)
    next(gd), next(ge)
    next(gq), next(gk)
    next(gd, None), next(ge, None)
    total = jnp.dot(acts[0], down4[0], preferred_element_type=F32)
    for j in range(1, 4):
        total = total + jnp.dot(acts[j], down4[j], preferred_element_type=F32)
    for y in range(4):
        fblk[y] = total[y * 64 : (y + 1) * 64, :].astype(BF16)

    def keep_enc(rows, total):
        v = emb_own[rows, :].astype(F32) + total
        v = v * lax.rsqrt(jnp.mean(v * v, axis=-1, keepdims=True) + 1e-06)
        enc_own[rows, :] = v.astype(BF16)

    fy = scatter_y(
        w, p, w.group(enc.at[pl.ds(0, 3)]), fblk, lambda dy: (p.y + dy) % 4, lambda dy: None, fland, keep_enc
    )
    next(fy)
    next(fy)
    next(gq), next(gk)
    next(go)
    next(gh)
    next(fy)
    next(gc), next(gc)
    next(gq), next(gk)
    next(fy, None)
    ga = gather_mp(w, p, enc_own, enc)
    next(ga)
    next(go)
    next(gh, None)
    next(ga)
    next(go)
    next(ga)
    next(ga)
    next(gc)
    next(go)
    drain([gq, gk])
    for i in range(16):
        wkv_f[pl.ds(56 * i, 56), :] = wkv_s[i].astype(F32)
    wkv_w[...] = wkv_f[...].astype(BF16)

    def project(src, weights, sums, columns, start):
        total = None if start else sums[...]
        for dx in columns:
            for dz in range(4):
                b = p.seq(dx, dz)
                got = jnp.dot(src[b], weights[b], preferred_element_type=F32)
                total = got if total is None else total + got
        sums[...] = total

    next(go)
    project(hid_s, wq_s, sum_o, (0, 1, 2, 3), True)
    q_s[...] = pltpu.roll(sum_o[...], 193, 0).astype(BF16)
    swap = w.group(q_land)
    kq = swap.send(q_s.at[pl.ds(192, 64)], q_land.at[0], p.prv)
    next(ga)
    next(gc, None)
    project(cot_s, wo_s, sum_o, (0,), True)
    drain([go])
    project(cot_s, wo_s, sum_o, (1, 3, 2), False)
    d_s[...] = pltpu.roll(sum_o[...], 193, 0).astype(BF16)
    kd = swap.send(d_s.at[pl.ds(192, 64)], q_land.at[1], p.prv)
    next(ga, None)

    def keyval(g):
        rows = enc[g * 4 : g * 4 + 4].reshape(256, 896)
        kv_s[g] = jnp.dot(rows, wkv_w[...], preferred_element_type=F32).astype(BF16)

    first = lax.broadcasted_iota(jnp.int32, (64, 256), 0) == 0
    tail = pl.ds(192, 64)
    key = lax.broadcasted_iota(jnp.int32, (64, 256), 1)
    scale = 128 ** (-0.5)

    def swapped(i, src):
        last[i] = jnp.where(
            first, src[tail, :].astype(F32), q_land[i].astype(F32)
        ).astype(BF16)

    def heads(spans):
        return [
            (g, h, slice(g * 64, (g + 1) * 64), slice(h * 128, (h + 1) * 128))
            for g in spans
            for h in range(2)
        ]

    def keys_of(g, h):
        return kv_s[g, :, h * 256 : h * 256 + 128]

    def values_of(g, h):
        return kv_s[g, :, h * 256 + 128 : (h + 1) * 256]

    def attend(spans):
        jobs = heads(spans)
        score = [
            lax.dot_general(
                last[0, :, head] if g == 3 else q_s[rows, head], keys_of(g, h), NT,
                preferred_element_type=F32,
            )
            for g, h, rows, head in jobs
        ]
        expo = []
        for (g, _, _, _), x in zip(jobs, score):
            span = p.s * 4 + g
            live = key < jnp.where(key < 128, lens[0, span], lens[1, span] + 128)
            expo.append(jnp.where(live, jnp.exp(x * scale), 0.0))
        prob = [x / jnp.sum(x, axis=-1, keepdims=True) for x in expo]
        attn = [
            jnp.dot(x.astype(BF16), values_of(g, h), preferred_element_type=F32)
            for (g, h, _, _), x in zip(jobs, prob)
        ]
        for (g, h, rows, head), x, y in zip(jobs, prob, attn):
            prob_s[g * 2 + h] = x
            a_s[0, rows, head] = y.astype(BF16)

    def differentiate(spans):
        jobs = heads(spans)
        d_prob = [
            lax.dot_general(
                last[1, :, head] if g == 3 else d_s[rows, head], values_of(g, h), NT,
                preferred_element_type=F32,
            )
            for g, h, rows, head in jobs
        ]
        prob = [prob_s[g * 2 + h] for g, h, _, _ in jobs]
        delta = [jnp.sum(x * y, axis=-1, keepdims=True) for x, y in zip(prob, d_prob)]
        d_score = [
            (x * (y - z) * scale).astype(BF16) for x, y, z in zip(prob, d_prob, delta)
        ]
        d_query = [
            jnp.dot(x, keys_of(g, h), preferred_element_type=F32)
            for (g, h, _, _), x in zip(jobs, d_score)
        ]
        for (_, _, rows, head), y in zip(jobs, d_query):
            a_s[1, rows, head] = y.astype(BF16)

    def give_back(i):
        back = w.group(a_land.at[i])
        return back, back.send(a_s.at[i, tail], a_land.at[i], p.nxt)

    def take_back(i, back, k):
        w.wait(k, a_land.at[i], p.prv)
        back.flush()
        got = jnp.where(p.s > 0, a_land[i].astype(F32), 0.0)
        a_s[i, tail, :] = jnp.where(first, a_s[i, tail, :].astype(F32), got).astype(BF16)

    keyval(3)
    w.wait(kq, q_land.at[0], p.nxt)
    swapped(0, q_s)
    attend((3,))
    back_o = give_back(0)
    for g in range(3):
        keyval(g)
    def fill(i, weights, part, c, rows):
        for b in range(8):
            part[b, c] = lax.dot_general(
                a_s[i, rows, :], weights[b * 2 + c], NT, preferred_element_type=F32
            ).astype(BF16)

    def keep_out(total):
        res[0] = pltpu.roll(total, 63, 0).astype(BF16)

    def keep_head(rows, total):
        sum_o[rows, :] = total

    def keep_tail(total):
        sum_o[tail, :] = total

    blocks = pl.ds(0, 15)
    body_rows, every = pl.ds(0, 192), slice(None)
    ro = scatter_mp(
        w, p, w.group(wo_s.at[blocks]), part_o, sib_o, acc_o, land_o, keep_out, False
    )
    rg = scatter_zy(
        w, p, w.group(wq_s.at[blocks, body_rows]),
        part_g, sib_g, acc_g, zland_g, land_g, keep_head,
    )
    rt = scatter_mp(
        w, p, w.group(wq_s.at[blocks, pl.ds(0, 64)]),
        part_t, sib_t, acc_t, land_t, keep_tail, False,
    )
    attend((0, 1, 2))
    differentiate((0, 1, 2))
    fill(1, wq_s, part_g, 1 - p.c, body_rows)
    next(rg)
    w.wait(kd, q_land.at[1], p.nxt)
    swapped(1, d_s)
    differentiate((3,))
    back_g = give_back(1)
    fill(1, wq_s, part_g, p.c, body_rows)
    next(rg)
    take_back(0, *back_o)
    fill(0, wo_s, part_o, 1 - p.c, every)
    next(ro)
    fill(0, wo_s, part_o, p.c, every)
    next(ro)
    next(rg)
    take_back(1, *back_g)
    fill(1, wq_s, part_t, 1 - p.c, tail)
    next(rt)
    fill(1, wq_s, part_t, p.c, tail)
    next(rt)
    next(rg)
    next(ro)
    next(rt)
    next(rg)
    next(ro)
    next(rt)
    next(rg, None)
    next(ro, None)
    next(rt, None)
    res[1] = pltpu.roll(sum_o[...], 63, 0).astype(BF16)
    w.finish()


def per_device(
    hidden, cotangent, neighbour_ids, neighbour_lengths, embed_table,
    enc_up, enc_down, w_query, w_keyval, w_out,
):
    blk = (256, 256)
    row = (64, 896)
    bf = lambda *s: pltpu.VMEM(s, BF16)
    vm = pl.BlockSpec(memory_space=pltpu.VMEM)
    messages, groups = 132, 18
    res = pl.pallas_call(
        body,
        out_shape=jax.ShapeDtypeStruct((2,) + blk, BF16),
        in_specs=[vm] * 5
        + [pl.BlockSpec(memory_space=pl.ANY), vm, pl.BlockSpec(memory_space=pltpu.SMEM), vm, vm],
        out_specs=vm,
        scratch_shapes=[
            bf(4096, 896), pltpu.VMEM((8, 128, 128), jnp.int32), bf(512, 4096),
            bf(8, 2, *row), bf(8, *row), bf(8, *row), bf(7, *row), bf(*row), bf(4, *row),
            bf(256, 896),
            bf(4, 224, 896), bf(4, 224, 896), bf(4, 256, 224), bf(4, *row),
            bf(6, 32, 896), bf(*row), bf(16, *row),
            bf(16, *blk), bf(16, *blk), bf(16, *blk), bf(16, *blk), bf(16, 56, 512),
            bf(896, 512), pltpu.VMEM((896, 512), F32), bf(4, 256, 512),
            bf(*blk), bf(*blk), bf(2, 64, 256), bf(2, 64, 256), bf(2, *blk), bf(2, 64, 256),
            bf(8, 2, *blk), bf(8, *blk), bf(8, *blk), bf(7, *blk),
            bf(8, 2, 192, 256), bf(8, 192, 256), bf(8, 192, 256), bf(4, 192, 256), bf(6, 96, 256),
            bf(8, 2, 64, 256), bf(8, 64, 256), bf(8, 64, 256), bf(7, 64, 256),
            pltpu.VMEM(blk, F32), pltpu.VMEM((8, 64, 256), F32),
            bf(*blk), bf(*blk), bf(56, 512),
            pltpu.SemaphoreType.DMA,
            pltpu.SemaphoreType.DMA((groups,)), pltpu.SemaphoreType.DMA((messages,)),
        ],
        compiler_params=pltpu.CompilerParams(
            collective_id=1, has_side_effects=True, vmem_limit_bytes=62 * 1024 * 1024
        ),
        name="block",
    )(
        hidden, cotangent, w_query, w_out, w_keyval, embed_table, neighbour_ids.reshape(8, 128),
        neighbour_lengths.T, enc_up, enc_down,
    )
    return res[0], res[1]


def solution(mesh):
    return jax.shard_map(
        per_device,
        mesh=mesh,
        in_specs=(
            P("seq", "mp"),
            P("seq", "mp"),
            P("seq", None, None),
            P(),
            P("mp", None),
            P("mp", None),
            P("mp", None),
            P("seq", "mp", None),
            P("seq", "mp", None, None),
            P("seq", "mp", None),
        ),
        out_specs=(P("seq", "mp"), P("seq", "mp")),
        check_vma=False,
    )
```

```python
import functools

import jax
import jax.numpy as jnp
from jax import lax
from jax.experimental import pallas as pl
from jax.experimental.pallas import tpu as pltpu
from jax.sharding import PartitionSpec as P

MESH = pl.DeviceIdType.MESH
F32 = jnp.float32
BF16 = jnp.bfloat16


class Place:
    def __init__(self):
        s = lax.axis_index("seq")
        m = lax.axis_index("mp")
        self.s, self.m = s, m
        self.x, self.zh = s // 4, s % 4
        self.y, self.zl, self.c = m // 4, (m // 2) % 2, m % 2
        self.sib = (s, self.mp(0, self.zl, 1 - self.c))
        self.zn = (s, self.mp(0, 1 - self.zl, self.c))
        self.zo = (self.seq(0, 2 * self.zl + 3), self.mp(0, 1 - self.zl, self.c))
        self.yp = (s, self.mp(1, self.zl, self.c))
        self.ym = (s, self.mp(3, self.zl, self.c))
        self.zp = (self.seq(0, 1), m)
        self.zm = (self.seq(0, 3), m)
        self.xp = (self.seq(1, 0), m)
        self.xm = (self.seq(3, 0), m)
        self.nxt = ((s + 1) % 16, m)
        self.prv = ((s + 15) % 16, m)

    def mp(self, dy, zl, c):
        return (((self.y + dy) % 4) * 2 + zl) * 2 + c

    def pair(self, dy, zl):
        return ((self.y + dy) % 4) * 2 + zl

    def seq(self, dx, dz):
        return ((self.x + dx) % 4) * 4 + (self.zh + dz) % 4


class Wire:
    def __init__(self, send_sem, recv_sem):
        self.send_sem, self.recv_sem = send_sem, recv_sem
        self.count = 0
        self.groups = []
        self.open = []

    def slot(self):
        self.count += 1
        return self.count - 1

    def wait(self, k, landing, frm):
        pltpu.make_async_remote_copy(
            src_ref=landing,
            dst_ref=landing,
            send_sem=self.send_sem.at[0],
            recv_sem=self.recv_sem.at[k],
            device_id=frm,
            device_id_type=MESH,
        ).wait_recv()

    def group(self, total):
        return Group(self, total)

    def finish(self):
        for group in list(self.open):
            group.flush()


class Group:
    def __init__(self, wire, total):
        self.wire, self.total = wire, total
        self.sem = wire.send_sem.at[len(wire.groups)]
        wire.groups.append(self)
        wire.open.append(self)

    def send(self, src, dst, to, k=None):
        k = self.wire.slot() if k is None else k
        self.to = to
        pltpu.make_async_remote_copy(
            src_ref=src,
            dst_ref=dst,
            send_sem=self.sem,
            recv_sem=self.wire.recv_sem.at[k],
            device_id=to,
            device_id_type=MESH,
        ).start()
        return k

    def flush(self):
        self.wire.open.remove(self)
        pltpu.make_async_remote_copy(
            src_ref=self.total,
            dst_ref=self.total,
            send_sem=self.sem,
            recv_sem=self.wire.recv_sem.at[0],
            device_id=self.to,
            device_id_type=MESH,
        ).wait_send()


def greet(peers, meanwhile):
    barrier = pltpu.get_barrier_semaphore()
    for peer in peers:
        pl.semaphore_signal(barrier, inc=1, device_id=peer, device_id_type=MESH)
    meanwhile()
    pl.semaphore_wait(barrier, len(peers))


def gather_mp(w, p, shard, out, flip=False):
    n = w.group(out.at[pl.ds(0, 15)])
    ks = w.slot()
    mine = p.mp(0, p.zl, p.c)
    o = 1 - p.zl
    fore, back, f, b3 = (p.ym, p.yp, 3, 1) if flip else (p.yp, p.ym, 1, 3)
    at = lambda dy, zl, c: out.at[p.mp(dy, zl, c)]
    own = out.at[mine]
    k_y1 = n.send(shard, own, fore)
    k_y2 = n.send(shard, own, back)
    k_z = n.send(shard, own, p.zn)
    n.send(shard, own, p.sib, ks)
    out[mine] = shard[...]
    yield
    w.wait(k_z, at(0, o, p.c), p.zn)
    zb = at(0, o, p.c)
    k_z1 = n.send(zb, zb, fore)
    k_z2 = n.send(zb, zb, back)
    n.send(zb, zb, p.sib, ks)
    yield
    b = at(b3, p.zl, p.c)
    w.wait(k_y1, b, back)
    k_f1 = n.send(b, b, fore)
    n.send(b, b, p.sib, ks)
    b = at(f, p.zl, p.c)
    w.wait(k_y2, b, fore)
    n.send(b, b, p.sib, ks)
    yield
    b = at(f, o, p.c)
    w.wait(k_z2, b, fore)
    k_f2 = n.send(b, b, back)
    n.send(b, b, p.sib, ks)
    b = at(b3, o, p.c)
    w.wait(k_z1, b, back)
    n.send(b, b, p.sib, ks)
    yield
    b = at(2, p.zl, p.c)
    w.wait(k_f1, b, back)
    n.send(b, b, p.sib, ks)
    b = at(2, o, p.c)
    w.wait(k_f2, b, fore)
    n.send(b, b, p.sib, ks)
    yield
    w.wait(ks, out.at[pl.ds(0, 8)], p.sib)


def scatter_mp(w, p, n, part, sibl, acc, land, result, late):
    o = 1 - p.zl
    ks = {}

    def share(dy):
        row = ((p.y + dy) % 4) * 2
        ks[dy] = n.send(
            part.at[pl.ds(row, 2), 1 - p.c], sibl.at[pl.ds(row, 2)], p.sib
        )

    def combine(dy):
        row = ((p.y + dy) % 4) * 2
        w.wait(ks[dy], sibl.at[pl.ds(row, 2)], p.sib)
        for zl in (0, 1):
            acc[row + zl] = (
                part[row + zl, p.c].astype(F32) + sibl[row + zl].astype(F32)
            ).astype(BF16)

    for dy in (2, 1, 3) if late else (2, 1, 3, 0):
        share(dy)
    yield
    combine(2)
    k0 = n.send(acc.at[p.pair(2, p.zl)], land.at[0], p.yp)
    k1 = n.send(acc.at[p.pair(2, o)], land.at[1], p.ym)
    combine(1)
    k2b = n.send(acc.at[p.pair(1, o)], land.at[2], p.yp)
    combine(3)
    k3a = n.send(acc.at[p.pair(3, p.zl)], land.at[3], p.ym)
    yield
    if late:
        share(0)
        yield
    w.wait(k0, land.at[0], p.ym)
    i = p.pair(1, p.zl)
    acc[i] = (acc[i].astype(F32) + land[0].astype(F32)).astype(BF16)
    k2a = n.send(acc.at[i], land.at[4], p.yp)
    w.wait(k1, land.at[1], p.yp)
    i = p.pair(3, o)
    acc[i] = (acc[i].astype(F32) + land[1].astype(F32)).astype(BF16)
    k3b = n.send(acc.at[i], land.at[5], p.ym)
    combine(0)
    yield
    w.wait(k2b, land.at[2], p.ym)
    w.wait(k3b, land.at[5], p.yp)
    i = p.pair(0, o)
    acc[i] = (acc[i].astype(F32) + land[2].astype(F32) + land[5].astype(F32)).astype(BF16)
    kz = n.send(acc.at[i], land.at[6], p.zn)
    yield
    w.wait(k3a, land.at[3], p.yp)
    w.wait(k2a, land.at[4], p.ym)
    w.wait(kz, land.at[6], p.zn)
    result(
        acc[p.pair(0, p.zl)].astype(F32)
        + land[3].astype(F32)
        + land[4].astype(F32)
        + land[6].astype(F32)
    )


def drain(gens):
    gens = list(gens)
    while gens:
        gens = [g for g in gens if next(g, True) is None]


def gather_seq(w, p, shard, out, up, late):
    n = w.group(out.at[pl.ds(0, 15)])
    k_last = w.slot()
    away = {0: 0, "behind": 3 - 2 * p.zl, "ahead": 1 + 2 * p.zl, 2: 2}
    ahead = (p.seq(0, away["ahead"]), p.m)
    behind = (p.seq(0, away["behind"]), p.m)
    mine = p.seq(0, 0)
    at = lambda dx, dz: out.at[p.seq(dx, away[dz])]
    own = out.at[mine]
    kx = {0: (n.send(shard, own, p.xp), n.send(shard, own, p.xm))}
    out[mine] = shard[...]

    def spread(dz):
        b = at(0, dz)
        kx[dz] = (n.send(b, b, p.xp), n.send(b, b, p.xm))

    def relay(dz, upward):
        k1, k2 = kx[dz]
        if upward:
            b = at(3, dz)
            w.wait(k1, b, p.xm)
            n.send(b, b, p.xp, k_last)
            w.wait(k2, at(1, dz), p.xp)
        else:
            b = at(1, dz)
            w.wait(k2, b, p.xp)
            n.send(b, b, p.xm, k_last)
            w.wait(k1, at(3, dz), p.xm)

    yield
    if late:
        relay(0, up)
        yield
    k_a = n.send(shard, own, ahead)
    k_b = n.send(shard, own, behind)
    yield
    if not late:
        relay(0, up)
        yield
    b = at(0, "behind")
    w.wait(k_a, b, behind)
    k_zf = n.send(b, b, ahead)
    spread("behind")
    w.wait(k_b, at(0, "ahead"), ahead)
    spread("ahead")
    yield
    w.wait(k_zf, at(0, 2), behind)
    spread(2)
    yield
    relay("behind", up)
    yield
    relay("ahead", not up)
    yield
    relay(2, not up)
    yield
    w.wait(k_last, out.at[pl.ds(0, 4)], p.xm)


def gather_pair(w, p, shard, out, other):
    n = w.group(out.at[pl.ds(0, 3)])
    o, oc = 1 - p.zl, 1 - p.c
    mine = p.zl * 2 + p.c
    k_z = n.send(shard, out.at[mine], other)
    k_s = n.send(shard, out.at[mine], p.sib)
    out[mine] = shard[...]
    yield
    b = out.at[o * 2 + p.c]
    w.wait(k_z, b, other)
    k_zs = n.send(b, b, p.sib)
    yield
    w.wait(k_s, out.at[p.zl * 2 + oc], p.sib)
    w.wait(k_zs, out.at[o * 2 + oc], p.sib)


def gather_y(w, p, shard, out):
    n = w.group(out.at[pl.ds(0, 3)])
    rows = shard.shape[0] // 2
    lo, hi = pl.ds(0, rows), pl.ds(rows, rows)
    at = lambda dy: (p.y + dy) % 4
    k1 = n.send(shard.at[lo], out.at[at(0), lo], p.yp)
    k2 = n.send(shard.at[hi], out.at[at(0), hi], p.ym)
    k3 = n.send(shard.at[hi], out.at[at(0), hi], p.yp)
    k4 = n.send(shard.at[lo], out.at[at(0), lo], p.ym)
    out[at(0)] = shard[...]
    yield
    b = out.at[at(3), lo]
    w.wait(k1, b, p.ym)
    f1 = n.send(b, b, p.yp)
    b = out.at[at(1), hi]
    w.wait(k2, b, p.yp)
    f2 = n.send(b, b, p.ym)
    yield
    w.wait(k3, out.at[at(3), hi], p.ym)
    w.wait(k4, out.at[at(1), lo], p.yp)
    w.wait(f1, out.at[at(2), lo], p.ym)
    w.wait(f2, out.at[at(2), hi], p.yp)


def scatter_y(w, p, n, blk, index, ready, land, result):
    rows = blk.shape[1] // 2
    lo, hi = pl.ds(0, rows), pl.ds(rows, rows)
    i0, i1, i2, i3 = index(0), index(1), index(2), index(3)
    ready(2)
    k0 = n.send(blk.at[i2, lo], land.at[0], p.yp)
    k1 = n.send(blk.at[i2, hi], land.at[1], p.ym)
    yield
    ready(1)
    k2b = n.send(blk.at[i1, hi], land.at[2], p.yp)
    ready(3)
    k3a = n.send(blk.at[i3, lo], land.at[3], p.ym)
    yield
    w.wait(k0, land.at[0], p.ym)
    blk[i1, lo, :] = (blk[i1, lo, :].astype(F32) + land[0].astype(F32)).astype(BF16)
    k2a = n.send(blk.at[i1, lo], land.at[4], p.yp)
    w.wait(k1, land.at[1], p.yp)
    blk[i3, hi, :] = (blk[i3, hi, :].astype(F32) + land[1].astype(F32)).astype(BF16)
    k3b = n.send(blk.at[i3, hi], land.at[5], p.ym)
    yield
    ready(0)
    w.wait(k2b, land.at[2], p.ym)
    w.wait(k3a, land.at[3], p.yp)
    w.wait(k2a, land.at[4], p.ym)
    w.wait(k3b, land.at[5], p.yp)
    f = lambda v: v.astype(F32)
    result(lo, f(blk[i0, lo, :]) + f(land[4]) + f(land[3]))
    result(hi, f(blk[i0, hi, :]) + f(land[2]) + f(land[5]))


def scatter_zy(w, p, n, part, sibl, acc, zland, land, result):
    o = 1 - p.zl
    ks, kz = {}, {}
    for dy in (2, 1, 3, 0):
        row = ((p.y + dy) % 4) * 2
        ks[dy] = n.send(
            part.at[pl.ds(row, 2), 1 - p.c], sibl.at[pl.ds(row, 2)], p.sib
        )
    yield
    for dy in (2, 1, 3, 0):
        row = ((p.y + dy) % 4) * 2
        w.wait(ks[dy], sibl.at[pl.ds(row, 2)], p.sib)
        for zl in (o, p.zl):
            acc[row + zl] = (
                part[row + zl, p.c].astype(F32) + sibl[row + zl].astype(F32)
            ).astype(BF16)
        kz[dy] = n.send(acc.at[row + o], zland.at[dy], p.zn)
    yield

    def ready(dy):
        w.wait(kz[dy], zland.at[dy], p.zn)
        i = p.pair(dy, p.zl)
        acc[i] = (acc[i].astype(F32) + zland[dy].astype(F32)).astype(BF16)

    yield from scatter_y(w, p, n, acc, lambda dy: p.pair(dy, p.zl), ready, land, result)


NT = (((1,), (1,)), ((), ()))


def body(
    hid, cot, wq3, wo3, wkv3, table, ids, lens, up, down,
    res,
    tab, idsb, onehot, epart, esib, eacc, eland, emb_own, emb4, normed,
    up4, down4, acts, fblk, fland, enc_own, enc,
    hid_s, cot_s, wq_s, wo_s, wkv_s, wkv_w, wkv_f, kv_s,
    q_s, d_s, q_land, last, a_s, a_land,
    part_o, sib_o, acc_o, land_o, part_g, sib_g, acc_g, zland_g, land_g,
    part_t, sib_t, acc_t, zland_t, land_t, sum_o, prob_s,
    wq, wo, wkv, tab_sem, send_sem, recv_sem,
):
    p = Place()
    w = Wire(send_sem, recv_sem)
    fetch = pltpu.make_async_copy(table, tab.at[pl.ds(0, 4000)], tab_sem)
    fetch.start()
    def relay_weights():
        for h in range(2):
            head = slice(h * 128, (h + 1) * 128)
            wq[:, head] = wq3[:, h, :]
            wo[:, head] = wo3[:, h, :]
            for kv in range(2):
                wkv[:, h * 256 + kv * 128 : h * 256 + (kv + 1) * 128] = wkv3[:, h, kv, :]

    greet((p.sib, p.zn, p.zo, p.yp, p.ym, p.zp, p.zm, p.xp, p.xm, p.nxt, p.prv), relay_weights)

    gh = gather_mp(w, p, hid, hid_s)
    gc = gather_mp(w, p, cot, cot_s, True)
    gu = gather_pair(w, p, up, up4, p.zo)
    lo, hi = pl.ds(0, 112), pl.ds(112, 112)
    gd = gather_pair(w, p, down.at[lo], down4.at[:, lo], p.zo)
    ge = gather_pair(w, p, down.at[hi], down4.at[:, hi], p.zn)
    gq = gather_seq(w, p, wq, wq_s, True, False)
    gk = gather_seq(w, p, wkv, wkv_s, True, False)
    go = gather_seq(w, p, wo, wo_s, False, True)
    next(gh), next(gc), next(gu)
    next(gq), next(gq)
    next(gk), next(gk)
    next(gd), next(ge), next(go)

    tab[pl.ds(4000, 96), :] = jnp.zeros((96, 896), BF16)
    cols = jnp.transpose(ids[...] - p.m * 4000)
    for r in range(8):
        idsb[r] = jnp.broadcast_to(cols[:, r : r + 1], (128, 128))
    lane = lax.broadcasted_iota(jnp.int32, (64, 128), 1)

    def lookup(c, ys):
        pairs = [p.pair(dy, zl) for dy in ys for zl in (0, 1)]
        high = len(pairs) * 64
        for i, r in enumerate(pairs):
            mine = idsb[r, pl.ds(pl.multiple_of(c * 64, 64), 64), :] - lane
            for k in range(32):
                onehot[i * 64 : (i + 1) * 64, k * 128 : (k + 1) * 128] = jnp.where(
                    mine == k * 128, 1.0, 0.0
                ).astype(BF16)

        def pick(cols_at):
            got = jnp.dot(onehot[0:high, :], tab[:, cols_at], preferred_element_type=F32)
            for i, r in enumerate(pairs):
                epart[r, c, :, cols_at] = got[i * 64 : (i + 1) * 64].astype(BF16)

        for at in (0, 256, 512, 768):
            pick(slice(at, min(at + 256, 896)))

    def keep_emb(total):
        emb_own[...] = total.astype(BF16)

    far = (2, 1, 3)
    fetch.wait()
    lookup(1 - p.c, far)
    ers = scatter_mp(
        w, p, w.group(enc.at[pl.ds(0, 15)]), epart, esib, eacc, eland, keep_emb, True
    )
    next(ers)
    lookup(p.c, far)
    next(ers)
    lookup(1 - p.c, (0,))
    next(ers)
    lookup(p.c, (0,))
    next(ers)
    next(gh), next(gc)
    next(gq), next(gk), next(go)
    next(gu)
    next(ers)
    next(gq), next(gk)
    next(go)
    next(ers, None)
    ey = gather_y(w, p, emb_own, emb4)
    next(ey)
    next(ey)
    next(gh), next(gh)
    next(ey, None)
    next(gu, None)
    next(gq), next(gk)

    e = emb4[...].reshape(256, 896).astype(F32)
    normed[...] = (
        e * lax.rsqrt(jnp.mean(e * e, axis=-1, keepdims=True) + 1e-06)
    ).astype(BF16)
    for j in range(4):
        acts[j] = jax.nn.gelu(
            lax.dot_general(normed[...], up4[j], NT, preferred_element_type=F32)
        ).astype(BF16)
    next(gd), next(ge)
    next(gq), next(gk)
    next(gd, None), next(ge, None)
    total = jnp.dot(acts[0], down4[0], preferred_element_type=F32)
    for j in range(1, 4):
        total = total + jnp.dot(acts[j], down4[j], preferred_element_type=F32)
    for y in range(4):
        fblk[y] = total[y * 64 : (y + 1) * 64, :].astype(BF16)

    def keep_enc(rows, total):
        v = emb_own[rows, :].astype(F32) + total
        v = v * lax.rsqrt(jnp.mean(v * v, axis=-1, keepdims=True) + 1e-06)
        enc_own[rows, :] = v.astype(BF16)

    fy = scatter_y(
        w, p, w.group(enc.at[pl.ds(0, 3)]), fblk, lambda dy: (p.y + dy) % 4, lambda dy: None, fland, keep_enc
    )
    next(fy)
    next(fy)
    next(gq), next(gk)
    next(go)
    next(gh)
    next(fy)
    next(gc), next(gc)
    next(gq), next(gk)
    next(fy, None)
    ga = gather_mp(w, p, enc_own, enc)
    next(ga)
    next(go)
    next(gh, None)
    next(ga)
    next(go)
    next(ga)
    next(ga)
    next(gc)
    next(go)
    drain([gq, gk])
    for i in range(16):
        wkv_f[pl.ds(56 * i, 56), :] = wkv_s[i].astype(F32)
    wkv_w[...] = wkv_f[...].astype(BF16)

    def project(src, weights, sums, columns, start):
        total = None if start else sums[...]
        for dx in columns:
            for dz in range(4):
                b = p.seq(dx, dz)
                got = jnp.dot(src[b], weights[b], preferred_element_type=F32)
                total = got if total is None else total + got
        sums[...] = total

    next(go)
    project(hid_s, wq_s, sum_o, (0, 1, 2, 3), True)
    q_s[...] = pltpu.roll(sum_o[...], 193, 0).astype(BF16)
    swap = w.group(q_land)
    kq = swap.send(q_s.at[pl.ds(192, 64)], q_land.at[0], p.prv)
    next(ga)
    next(gc, None)
    project(cot_s, wo_s, sum_o, (0,), True)
    drain([go])
    project(cot_s, wo_s, sum_o, (1, 3, 2), False)
    d_s[...] = pltpu.roll(sum_o[...], 193, 0).astype(BF16)
    kd = swap.send(d_s.at[pl.ds(192, 64)], q_land.at[1], p.prv)
    next(ga, None)

    def keyval(g):
        rows = enc[g * 4 : g * 4 + 4].reshape(256, 896)
        kv_s[g] = jnp.dot(rows, wkv_w[...], preferred_element_type=F32).astype(BF16)

    first = lax.broadcasted_iota(jnp.int32, (64, 256), 0) == 0
    tail = pl.ds(192, 64)
    key = lax.broadcasted_iota(jnp.int32, (64, 256), 1)
    scale = 128 ** (-0.5)

    def swapped(i, src):
        last[i] = jnp.where(
            first, src[tail, :].astype(F32), q_land[i].astype(F32)
        ).astype(BF16)

    def heads(spans):
        return [
            (g, h, slice(g * 64, (g + 1) * 64), slice(h * 128, (h + 1) * 128))
            for g in spans
            for h in range(2)
        ]

    def keys_of(g, h):
        return kv_s[g, :, h * 256 : h * 256 + 128]

    def values_of(g, h):
        return kv_s[g, :, h * 256 + 128 : (h + 1) * 256]

    def attend(spans):
        jobs = heads(spans)
        score = [
            lax.dot_general(
                last[0, :, head] if g == 3 else q_s[rows, head], keys_of(g, h), NT,
                preferred_element_type=F32,
            )
            for g, h, rows, head in jobs
        ]
        expo = []
        for (g, _, _, _), x in zip(jobs, score):
            span = p.s * 4 + g
            live = key < jnp.where(key < 128, lens[0, span], lens[1, span] + 128)
            expo.append(jnp.where(live, jnp.exp(x * scale), 0.0))
        prob = [x / jnp.sum(x, axis=-1, keepdims=True) for x in expo]
        attn = [
            jnp.dot(x.astype(BF16), values_of(g, h), preferred_element_type=F32)
            for (g, h, _, _), x in zip(jobs, prob)
        ]
        for (g, h, rows, head), x, y in zip(jobs, prob, attn):
            prob_s[g * 2 + h] = x
            a_s[0, rows, head] = y.astype(BF16)

    def differentiate(spans):
        jobs = heads(spans)
        d_prob = [
            lax.dot_general(
                last[1, :, head] if g == 3 else d_s[rows, head], values_of(g, h), NT,
                preferred_element_type=F32,
            )
            for g, h, rows, head in jobs
        ]
        prob = [prob_s[g * 2 + h] for g, h, _, _ in jobs]
        delta = [jnp.sum(x * y, axis=-1, keepdims=True) for x, y in zip(prob, d_prob)]
        d_score = [
            (x * (y - z) * scale).astype(BF16) for x, y, z in zip(prob, d_prob, delta)
        ]
        d_query = [
            jnp.dot(x, keys_of(g, h), preferred_element_type=F32)
            for (g, h, _, _), x in zip(jobs, d_score)
        ]
        for (_, _, rows, head), y in zip(jobs, d_query):
            a_s[1, rows, head] = y.astype(BF16)

    def give_back(i):
        back = w.group(a_land.at[i])
        return back, back.send(a_s.at[i, tail], a_land.at[i], p.nxt)

    def take_back(i, back, k):
        w.wait(k, a_land.at[i], p.prv)
        back.flush()
        got = jnp.where(p.s > 0, a_land[i].astype(F32), 0.0)
        a_s[i, tail, :] = jnp.where(first, a_s[i, tail, :].astype(F32), got).astype(BF16)

    keyval(3)
    w.wait(kq, q_land.at[0], p.nxt)
    swapped(0, q_s)
    attend((3,))
    back_o = give_back(0)
    for g in range(3):
        keyval(g)
    def fill(i, weights, part, c, rows):
        for b in range(8):
            part[b, c] = lax.dot_general(
                a_s[i, rows, :], weights[b * 2 + c], NT, preferred_element_type=F32
            ).astype(BF16)

    def keep_out(total):
        res[0] = pltpu.roll(total, 63, 0).astype(BF16)

    def keep_head(rows, total):
        sum_o[rows, :] = total

    def keep_tail(rows, total):
        sum_o[pl.ds(192 + rows.start, rows.size), :] = total

    blocks = pl.ds(0, 15)
    body_rows, every = pl.ds(0, 192), slice(None)
    ro = scatter_mp(
        w, p, w.group(wo_s.at[blocks]), part_o, sib_o, acc_o, land_o, keep_out, False
    )
    rg = scatter_zy(
        w, p, w.group(wq_s.at[blocks, body_rows]),
        part_g, sib_g, acc_g, zland_g, land_g, keep_head,
    )
    rt = scatter_zy(
        w, p, w.group(wq_s.at[blocks, pl.ds(0, 64)]),
        part_t, sib_t, acc_t, zland_t, land_t, keep_tail,
    )
    attend((0, 1, 2))
    differentiate((0, 1, 2))
    fill(1, wq_s, part_g, 1 - p.c, body_rows)
    next(rg)
    w.wait(kd, q_land.at[1], p.nxt)
    swapped(1, d_s)
    differentiate((3,))
    back_g = give_back(1)
    fill(1, wq_s, part_g, p.c, body_rows)
    next(rg)
    take_back(0, *back_o)
    fill(0, wo_s, part_o, 1 - p.c, every)
    next(ro)
    fill(0, wo_s, part_o, p.c, every)
    next(ro)
    take_back(1, *back_g)
    fill(1, wq_s, part_t, 1 - p.c, tail)
    next(rt)
    fill(1, wq_s, part_t, p.c, tail)
    next(rt)
    next(rg)
    next(ro)
    next(rg)
    next(rt)
    next(rt)
    next(ro)
    next(rg)
    next(rt)
    next(rg, None)
    next(rt, None)
    next(ro, None)
    res[1] = pltpu.roll(sum_o[...], 63, 0).astype(BF16)
    w.finish()


def per_device(
    hidden, cotangent, neighbour_ids, neighbour_lengths, embed_table,
    enc_up, enc_down, w_query, w_keyval, w_out,
):
    blk = (256, 256)
    row = (64, 896)
    bf = lambda *s: pltpu.VMEM(s, BF16)
    vm = pl.BlockSpec(memory_space=pltpu.VMEM)
    messages, groups = 135, 18
    res = pl.pallas_call(
        body,
        out_shape=jax.ShapeDtypeStruct((2,) + blk, BF16),
        in_specs=[vm] * 5
        + [pl.BlockSpec(memory_space=pl.ANY), vm, pl.BlockSpec(memory_space=pltpu.SMEM), vm, vm],
        out_specs=vm,
        scratch_shapes=[
            bf(4096, 896), pltpu.VMEM((8, 128, 128), jnp.int32), bf(512, 4096),
            bf(8, 2, *row), bf(8, *row), bf(8, *row), bf(7, *row), bf(*row), bf(4, *row),
            bf(256, 896),
            bf(4, 224, 896), bf(4, 224, 896), bf(4, 256, 224), bf(4, *row),
            bf(6, 32, 896), bf(*row), bf(16, *row),
            bf(16, *blk), bf(16, *blk), bf(16, *blk), bf(16, *blk), bf(16, 56, 512),
            bf(896, 512), pltpu.VMEM((896, 512), F32), bf(4, 256, 512),
            bf(*blk), bf(*blk), bf(2, 64, 256), bf(2, 64, 256), bf(2, *blk), bf(2, 64, 256),
            bf(8, 2, *blk), bf(8, *blk), bf(8, *blk), bf(7, *blk),
            bf(8, 2, 192, 256), bf(8, 192, 256), bf(8, 192, 256), bf(4, 192, 256), bf(6, 96, 256),
            bf(8, 2, 64, 256), bf(8, 64, 256), bf(8, 64, 256), bf(4, 64, 256), bf(6, 32, 256),
            pltpu.VMEM(blk, F32), pltpu.VMEM((8, 64, 256), F32),
            bf(*blk), bf(*blk), bf(56, 512),
            pltpu.SemaphoreType.DMA,
            pltpu.SemaphoreType.DMA((groups,)), pltpu.SemaphoreType.DMA((messages,)),
        ],
        compiler_params=pltpu.CompilerParams(
            collective_id=1, has_side_effects=True, vmem_limit_bytes=62 * 1024 * 1024
        ),
        name="block",
    )(
        hidden, cotangent, w_query, w_out, w_keyval, embed_table, neighbour_ids.reshape(8, 128),
        neighbour_lengths.T, enc_up, enc_down,
    )
    return res[0], res[1]


def solution(mesh):
    return jax.shard_map(
        per_device,
        mesh=mesh,
        in_specs=(
            P("seq", "mp"),
            P("seq", "mp"),
            P("seq", None, None),
            P(),
            P("mp", None),
            P("mp", None),
            P("mp", None),
            P("seq", "mp", None),
            P("seq", "mp", None, None),
            P("seq", "mp", None),
        ),
        out_specs=(P("seq", "mp"), P("seq", "mp")),
        check_vma=False,
    )
```
